32 devices in a mesh: pool: 2 (over core), ep: 4 (over z), half: 4 (over y, x).
Axes of the slice: x: 2, y: 2, z: 4, core: 2. Of those that a mesh axis runs over, the one named last changes fastest.
Arguments:
- tokens: bfloat16 [2, 256, 4096], P('pool', 'ep'), may hold values from -6 to 6
- routes: int32 [2, 256, 8], P('pool', 'ep'), may hold values from 0 to 31, all different within a row; in each aligned block of 64 rows (0 to 63, 64 to 127, ..., all dimensions but the last counted through in order) at most 32 rows name the same one
- router: bfloat16 [4096, 32], replicated, may hold values from -0.03125 to 0.03125
- w_gate: bfloat16 [32, 4096, 1536], P('ep', None, 'half'), may hold values from -0.09375 to 0.09375
- w_up: bfloat16 [32, 4096, 1536], P('ep', None, 'half'), may hold values from -0.09375 to 0.09375
- w_down: bfloat16 [32, 1536, 4096], P('ep', 'half'), may hold values from -0.625 to 0.625
- norm_gain: float32 [4096], replicated, may hold values from 0.1 to 1.9
- w_kv: bfloat16 [4096, 2048], P('ep', 'half'), may hold values from -0.09375 to 0.09375
- lengths: int32 [2, 4, 2], P(None, 'ep'), may hold values from 1 to 48, 64 in all within a row
- queries: bfloat16 [2, 1024, 2048], P('pool', 'ep', 'half'), may hold values from -150 to 150
- new_keys: bfloat16 [2, 1024, 1024], P('pool', 'ep', 'half'), may hold values from -5 to 5
- new_values: bfloat16 [2, 1024, 1024], P('pool', 'ep', 'half'), may hold values from -6 to 6
- w_out: bfloat16 [2048, 2048], P('half'), may hold values from -0.125 to 0.125
Outputs:
- decoded: bfloat16 [2, 1024, 2048], P('pool', ('ep', 'half'))
The draws below stay inside these ranges and needn't reach their ends.
Inputs may be any that keep to these rules, and one draw needn't show every extreme that they name: `routes`: each token names 8 different experts; within each aligned block of 64 tokens no expert is named by more than 32 tokens. The 2 lengths of a group sum to 64.
All inputs are finite; a program needn't handle non-finite values.
Results may differ from the reference program's by a relative error of at most 0.022.
Values may be sent and summed in bfloat16 or wider, within the bound.
No kernel may reach another device: no remote copies, remote signals or barrier semaphores. Data moves between devices by JAX's collectives and lax.ppermute only.
A program may use at most 192 MiB of HBM per device.

```python
import math
import jax
import jax.numpy as jnp
import numpy as np
from jax import lax

D = 4096
FF = 1536
EXPERTS = 32
TOP = 8
HEAD = 128
KV_HEADS = 8
Q_HEADS = 16
D_OUT = 2048
TOK_DEV = 64
PROMPT_GRP = 2
SAMPLES = 128
TOKENS = 256
CAP = 32
LEN_MOST = 48
ROWS = 1024
N_EP = 4
N_HALF = 4


def decode_inputs(key):
    fresh = jnp.clip(jax.random.normal(jax.random.fold_in(key, 101), (2, ROWS, KV_HEADS, HEAD), jnp.float32), -5.0, 5.0)
    query = jnp.clip(jax.random.normal(jax.random.fold_in(key, 102), (2, ROWS, KV_HEADS, Q_HEADS // KV_HEADS, HEAD), jnp.float32), -5.0, 5.0)
    return (query.reshape(2, ROWS, Q_HEADS * HEAD), fresh.reshape(2, ROWS, KV_HEADS * HEAD))


def draw_queries(key, part):
    return decode_inputs(key)[0].astype(jnp.bfloat16)


def draw_new_keys(key, part):
    return decode_inputs(key)[1].astype(jnp.bfloat16)


def steps_of(stream_key, dims, shards, smallest, high):
    def one(dim, blocks):
        draws = jax.random.uniform(jax.random.fold_in(jax.random.fold_in(stream_key, 6), dim), (blocks,), jnp.float32, smallest / len(shards), high / len(shards))
        return jnp.repeat(jnp.exp(draws), dims[dim] // blocks).reshape((-1,) + (1,) * (len(dims) - dim - 1))

    loudness = one(*shards[0])
    for cut in shards[1:]:
        loudness = loudness * one(*cut)
    return loudness


def split_up(count, total, most, skew):
    portions = [(1 << 20) // math.isqrt(standing ** skew) + 1 for standing in range(2, count + 1)]
    spare, holding = total - most - (count - 1), [1] * (count - 1)
    while spare > 0:
        candidates = [i for i in range(count - 1) if holding[i] < most]
        whole, budget = sum([portions[i] for i in candidates]), spare
        for i in candidates:
            more = min(most - holding[i], max(1, budget * portions[i] // whole), spare)
            holding[i] = holding[i] + more
            spare = spare - more
    return np.array([most] + holding)


def ragged_sizes(stream_key, amount, total, bound, skew):
    if amount == 2:
        one = jax.random.randint(stream_key, (), max(1, total - bound), min(bound, total - 1) + 1)
        return jnp.stack([one, total - one])
    sizes = jnp.asarray(split_up(amount, total, bound, skew), jnp.int32)
    pairs = (amount - 1) // 2
    source_of, taker = sizes[1:1 + 2 * pairs:2], sizes[2:2 + 2 * pairs:2]
    room = jnp.minimum(source_of - 1, bound - taker)
    passed = jax.random.randint(jax.random.fold_in(stream_key, 1), (pairs,), 0, 1 << 20) % (room + 1)
    sizes = sizes.at[1:1 + 2 * pairs:2].set(source_of - passed).at[2:2 + 2 * pairs:2].set(taker + passed)
    return sizes[jax.random.permutation(jax.random.fold_in(stream_key, 2), amount)]


def assign_block(rng, own, number, rows, count, top, bound, slope):
    sequence = jax.random.permutation(rng, count)
    packed, common = portions_of(count, rows * top, bound, slope, True), portions_of(count, rows * top, bound, slope, False)
    places = jnp.arange(count)

    def named(sizes, offset_by):
        used = int((sizes > 0).sum())
        fixed = max(1, used // 4)
        shifted = fixed + (places - fixed + offset_by * (used - fixed)) % max(1, count - fixed)
        return jnp.zeros((count,), jnp.int32).at[sequence[jnp.where(places < fixed, places, shifted)]].set(jnp.asarray(sizes, jnp.int32))

    sizes = jnp.where(number % 4 == 0, named(packed, number // 4), named(common, number - number // 4 - 1))
    mixed = jax.random.permutation(jax.random.fold_in(own, 3), count)
    donor, taker = mixed[0:count // 2 * 2:2], mixed[1:count // 2 * 2:2]
    room = jnp.minimum(sizes[donor] - 1, bound - sizes[taker]) // 2
    room = jnp.where((donor == sequence[0]) | (taker == sequence[0]) | (sizes[taker] == 0), 0, jnp.maximum(room, 0))
    shifted = jax.random.randint(jax.random.fold_in(own, 4), (count // 2,), 0, 1 << 20) % (room + 1)
    sizes = sizes.at[donor].add(-shifted).at[taker].add(shifted)
    labels = jnp.searchsorted(jnp.cumsum(sizes), jnp.arange(rows * top), side="right").astype(jnp.int32)
    table = labels.reshape(top, rows).T
    table = table[jax.random.permutation(jax.random.fold_in(own, 1), rows)]
    offset_by = jax.random.randint(jax.random.fold_in(own, 2), (rows, 1), 0, top)
    return jnp.take_along_axis(table, (jnp.arange(top)[None, :] + offset_by) % top, axis=1)


def portions_of(number_of, total, reach, skew, full):
    portions = [(1 << 20) // math.isqrt(grade ** skew) + 1 for grade in range(1, number_of + 1)]
    largest = reach if full else min(reach, max(-(-total // number_of), total * portions[0] // sum(portions)))
    least = 1 if total - largest >= number_of - 1 else 0
    counts, rest = [largest] + [least] * (number_of - 1), total - largest - least * (number_of - 1)
    while rest > 0:
        candidates = [i for i in range(1, number_of) if counts[i] < largest] or [i for i in range(1, number_of) if counts[i] < reach]
        mass, left = sum([portions[i] for i in candidates]), rest
        for i in candidates:
            extra = min(reach - counts[i], max(1, left * portions[i] // mass), rest)
            counts[i] = counts[i] + extra
            rest = rest - extra
    return np.array(counts)


def normal_values(stream_key, extent, scale, limit, split=(), kind=jnp.bfloat16):
    drawn = scale * jax.random.normal(stream_key, extent, jnp.float32)
    if split:
        drawn = drawn * steps_of(stream_key, extent, split, -0.22, 0.18)
    return jnp.clip(drawn, -limit, limit).astype(kind)


def setup_inputs(seed: int = 0) -> dict:
    splits = jax.random.split(jax.random.key(seed), 14)
    tokens = normal_values(splits[0], (2, TOKENS, D), 1.0, 6.0, ((0, 2), (1, 4)))
    routes_keys = jax.random.split(jax.random.fold_in(splits[1], 1), 2 * TOKENS // TOK_DEV)
    routes_turns = jax.random.permutation(jax.random.fold_in(splits[1], 3), 2 * TOKENS // TOK_DEV)
    routes = jax.vmap(lambda own, number: assign_block(jax.random.fold_in(splits[1], 2), own, number, TOK_DEV, EXPERTS, TOP, CAP, 4))(routes_keys, routes_turns).reshape((2, TOKENS, TOP))
    router = normal_values(splits[2], (D, EXPERTS), (8 * D) ** -0.5, 0.03125)
    w_gate = normal_values(splits[3], (EXPERTS, D, FF), D ** -0.5, 0.09375, ((0, 4), (2, 4)))
    w_up = normal_values(splits[4], (EXPERTS, D, FF), D ** -0.5, 0.09375, ((0, 4), (2, 4)))
    w_down = normal_values(splits[5], (EXPERTS, FF, D), (FF // 16) ** -0.5, 0.625, ((0, 4), (1, 4)))
    norm_gain = jnp.clip(1.0 + 0.18 * jax.random.normal(splits[6], (D,), jnp.float32), 0.1, 1.9)
    w_kv = normal_values(splits[7], (D, 2 * KV_HEADS * HEAD), D ** -0.5, 0.09375, ((0, 4), (1, 4)))
    lengths = jax.vmap(lambda own: ragged_sizes(own, PROMPT_GRP, TOK_DEV, LEN_MOST, 2))(jax.random.split(splits[8], 2 * N_EP)).reshape((2, N_EP, PROMPT_GRP)).astype(jnp.int32)
    queries = draw_queries(jax.random.fold_in(splits[13], 71), 0)
    new_keys = draw_new_keys(jax.random.fold_in(splits[13], 71), 0)
    new_values = normal_values(splits[11], (2, ROWS, KV_HEADS * HEAD), 1.0, 6.0, ((0, 2), (1, 4), (2, 4)))
    w_out = normal_values(splits[12], (Q_HEADS * HEAD, D_OUT), (Q_HEADS * HEAD) ** -0.5, 0.125, ((0, 4),))
    return {"tokens": tokens, "routes": routes, "router": router, "w_gate": w_gate, "w_up": w_up, "w_down": w_down, "norm_gain": norm_gain, "w_kv": w_kv, "lengths": lengths, "queries": queries, "new_keys": new_keys, "new_values": new_values, "w_out": w_out}


def prefill(tokens_set, chosen, router, w_gate, w_up, w_down, norm_gain, w_kv):
    logits = jnp.dot(tokens_set, router, preferred_element_type=jnp.float32)
    picked = jnp.take_along_axis(logits, chosen, axis=1)
    weights = jax.nn.softmax(picked, axis=1).reshape(-1)
    blocks = TOKENS // TOK_DEV
    width = TOK_DEV * TOP
    expert_of = chosen.reshape(blocks, width).astype(jnp.int32)
    onehot = (expert_of[:, :, None] == jnp.arange(EXPERTS, dtype=jnp.int32)[None, None, :]).astype(jnp.int32)
    before = jnp.cumsum(onehot, axis=1) - onehot
    rank = lax.optimization_barrier(jnp.sum(before * onehot, axis=2)).astype(jnp.int32)
    block_index = jnp.broadcast_to(jnp.arange(blocks, dtype=jnp.int32)[:, None], (blocks, width))
    flat_index = block_index * width + jnp.arange(width, dtype=jnp.int32)[None, :]
    table = jnp.full((EXPERTS, blocks, CAP), -1, jnp.int32).at[expert_of, block_index, rank].set(flat_index)
    quarter = FF // N_HALF

    def expert_step(carry, expert):
        entry = table[expert].reshape(-1)
        valid = entry >= 0
        safe = jnp.where(valid, entry, 0).astype(jnp.int32)
        token = (safe // TOP).astype(jnp.int32)
        rows = jnp.where(valid[:, None], tokens_set[token], jnp.zeros((), tokens_set.dtype))
        gate = jnp.dot(rows, w_gate[expert], preferred_element_type=jnp.float32)
        up = jnp.dot(rows, w_up[expert], preferred_element_type=jnp.float32)
        hidden = (jax.nn.silu(gate) * up).astype(jnp.bfloat16)
        down = w_down[expert]
        total = jnp.zeros((rows.shape[0], D), jnp.float32)
        for piece_index in range(N_HALF):
            lower = piece_index * quarter
            piece = jnp.dot(hidden[:, lower:lower + quarter], down[lower:lower + quarter], preferred_element_type=jnp.float32)
            total = total + lax.optimization_barrier(piece.astype(jnp.bfloat16)).astype(jnp.float32)
        result = lax.optimization_barrier(total.astype(jnp.bfloat16)).astype(jnp.float32)
        scale = jnp.where(valid, weights[safe], 0.0)
        return (carry.at[token].add(scale[:, None] * result), None)
    mixed, unused = lax.scan(expert_step, tokens_set.astype(jnp.float32), jnp.arange(EXPERTS, dtype=jnp.int32))
    meansq = lax.optimization_barrier(jnp.mean(mixed * mixed, axis=1, keepdims=True))
    normed = (mixed * lax.rsqrt(meansq + 1e-06) * norm_gain).astype(jnp.bfloat16)
    return jnp.dot(normed, w_kv, preferred_element_type=jnp.float32).astype(jnp.bfloat16)

def attend(block, prompt_lengths, query, fresh_key, fresh_value):
    group_tok = block.shape[0]
    group_rows = query.shape[0]
    ends = jnp.cumsum(prompt_lengths)
    position = jnp.arange(group_tok, dtype=jnp.int32)
    segment = lax.optimization_barrier(jnp.sum((position[:, None] >= ends[None, :]).astype(jnp.int32), axis=1))
    prompt = jnp.arange(group_rows, dtype=jnp.int32) // SAMPLES
    allowed = segment[None, :] == prompt[:, None]
    keys = block[:, :, 0, :].astype(jnp.float32)
    values = block[:, :, 1, :].astype(jnp.float32)
    scale = 1.0 / math.sqrt(HEAD)
    scores = jnp.einsum('rhgd,thd->rhgt', query.astype(jnp.float32), keys) * scale
    scores = jnp.where(allowed[:, None, None, :], scores, -1e+30)
    own = jnp.einsum('rhgd,rhd->rhg', query.astype(jnp.float32), fresh_key.astype(jnp.float32)) * scale
    top = jnp.maximum(lax.optimization_barrier(jnp.max(scores, axis=3)), own)
    spread = jnp.where(allowed[:, None, None, :], jnp.exp(scores - top[..., None]), 0.0)
    self_weight = jnp.exp(own - top)
    total = lax.optimization_barrier(jnp.sum(spread, axis=3)) + self_weight
    probs = (spread / total[..., None]).astype(jnp.bfloat16)
    self_prob = (self_weight / total).astype(jnp.bfloat16)
    mixed = jnp.einsum('rhgt,thd->rhgd', probs.astype(jnp.float32), values)
    mixed = mixed + self_prob.astype(jnp.float32)[..., None] * fresh_value.astype(jnp.float32)[:, :, None, :]
    return mixed.astype(jnp.bfloat16).reshape(group_rows, -1)

def decode(keyvals, prompt_lengths, query_set, key_set, value_set, w_out):
    group_tok = TOKENS // N_EP
    group_rows = PROMPT_GRP * SAMPLES
    heads_group = Q_HEADS // KV_HEADS
    blocks = keyvals.reshape(N_EP, group_tok, KV_HEADS, 2, HEAD)
    query_all = query_set.reshape(N_EP, group_rows, KV_HEADS, heads_group, HEAD)
    key_all = key_set.reshape(N_EP, group_rows, KV_HEADS, HEAD)
    value_all = value_set.reshape(N_EP, group_rows, KV_HEADS, HEAD)

    def group_step(items):
        return attend(items[0], items[1], items[2], items[3], items[4])
    attention = lax.map(group_step, (blocks, prompt_lengths, query_all, key_all, value_all))
    flat = attention.reshape(N_EP * group_rows, Q_HEADS * HEAD)
    return jnp.dot(flat, w_out, preferred_element_type=jnp.float32).astype(jnp.bfloat16)

def reference(tokens, routes, router, w_gate, w_up, w_down, norm_gain, w_kv, lengths, queries, new_keys, new_values, w_out):
    keyvals = [prefill(tokens[which], routes[which], router, w_gate, w_up, w_down, norm_gain, w_kv) for which in range(2)]
    outputs = [decode(keyvals[1 - which], lengths[1 - which], queries[which], new_keys[which], new_values[which], w_out) for which in range(2)]
    return jnp.stack(outputs)
```

```python
import functools
import math

import jax
import jax.numpy as jnp
from jax import lax
from jax.experimental import pallas as pl
from jax.experimental.pallas import tpu as pltpu
from jax.sharding import PartitionSpec as P

HEAD = 128
SAMPLES = 128
LANES = 128
F32 = jnp.float32
BF16 = jnp.bfloat16
WHOLE = pl.BlockSpec(memory_space=pltpu.VMEM)


def swap(shard, axis, bits):
    return lax.ppermute(shard, axis, [(i, i ^ bits) for i in range(lax.axis_size(axis))])


def shift(shard, axis, distance):
    count = lax.axis_size(axis)
    return lax.ppermute(shard, axis, [(i, (i + distance) % count) for i in range(count)])


def params(steps):
    return pltpu.CompilerParams(
        dimension_semantics=("arbitrary",) * steps, vmem_limit_bytes=60 * 1024 * 1024
    )


def columns_of(piece, width):
    return pl.ds(pl.multiple_of(piece * width, width), width)


def expand_kernel(parts, top, place, own, *refs):
    others, refs = refs[:parts], refs[parts:]
    tags, router, refs = refs[0], refs[1], refs[2:]
    gates, ups, refs = refs[:parts], refs[parts : 2 * parts], refs[2 * parts :]
    hidden, rows, weights = refs
    half, first = place[0], place[1]
    local, width = own.shape[0], rows.shape[2]
    step = pl.program_id(0)

    @pl.when(step == 0)
    def _():
        logits = jnp.zeros(weights.shape, F32)
        for k in range(parts):
            columns = columns_of(half ^ k, width)
            rows[k, :local, :] = own[:, columns]
            rows[k, local:, :] = others[k][...]
            logits += lax.dot_general(
                rows[k], router[:, columns], (((1,), (1,)), ((), ())), preferred_element_type=F32
            )
        expert = lax.broadcasted_iota(jnp.int32, weights.shape, 1)
        named = tags[...].astype(F32).astype(jnp.int32)
        picked = named[:, 0:1] == expert
        for j in range(1, top):
            picked = jnp.logical_or(picked, named[:, j : j + 1] == expert)
        most = jnp.max(jnp.where(picked, logits, -1e30), axis=1, keepdims=True)
        spread = jnp.where(picked, jnp.exp(logits - most), 0.0)
        weights[...] = spread / jnp.sum(spread, axis=1, keepdims=True)

    gate = jnp.zeros(hidden.shape, F32)
    up = jnp.zeros(hidden.shape, F32)
    for k in range(parts):
        gate += jnp.dot(rows[k], gates[k][0], preferred_element_type=F32)
        up += jnp.dot(rows[k], ups[k][0], preferred_element_type=F32)
    expert = lax.broadcasted_iota(jnp.int32, weights.shape, 1)
    scale = jnp.sum(
        jnp.where(expert == first + step, weights[...], 0.0), axis=1, keepdims=True
    )
    hidden[...] = (gate / (1.0 + jnp.exp(-gate)) * up * scale).astype(BF16)


def expand(place, own, others, tags, router, w_gate, w_up, top):
    parts = len(others)
    local, model = own.shape
    tokens = tags.shape[0]
    experts, units = w_gate.shape[0], w_gate.shape[2]
    width = model // parts
    weight = [
        pl.BlockSpec((1, width, units), lambda e, place, k=k: (e, place[0] ^ k, 0))
        for k in range(parts)
    ]
    return pl.pallas_call(
        functools.partial(expand_kernel, parts, top),
        out_shape=jax.ShapeDtypeStruct((tokens, experts * units), BF16),
        grid_spec=pltpu.PrefetchScalarGridSpec(
            num_scalar_prefetch=1,
            grid=(experts,),
            in_specs=[WHOLE] * (parts + 3) + weight + weight,
            out_specs=pl.BlockSpec((tokens, units), lambda e, place: (0, e)),
            scratch_shapes=[
                pltpu.VMEM((parts, tokens, width), BF16),
                pltpu.VMEM((tokens, router.shape[0]), F32),
            ],
        ),
        compiler_params=params(1),
        name="expand",
    )(place, own, *others, tags, router, *[w_gate] * parts, *[w_up] * parts)


def reduce_kernel(place, hidden, w_down, out):
    weight = w_down[...].reshape(-1, w_down.shape[2])
    out[...] = jnp.dot(hidden[...], weight, preferred_element_type=F32).astype(BF16)


def reduce(piece, hidden, w_down, width, block):
    experts, units, model = w_down.shape
    steps = width // block
    return pl.pallas_call(
        reduce_kernel,
        out_shape=jax.ShapeDtypeStruct((hidden.shape[0], width), BF16),
        grid_spec=pltpu.PrefetchScalarGridSpec(
            num_scalar_prefetch=1,
            grid=(steps,),
            in_specs=[
                WHOLE,
                pl.BlockSpec(
                    (experts, units, block), lambda i, piece: (0, 0, piece[0] * steps + i)
                ),
            ],
            out_specs=pl.BlockSpec((hidden.shape[0], block), lambda i, piece: (0, i)),
        ),
        compiler_params=params(1),
        name="reduce",
    )(piece, hidden, w_down)


def project_kernel(parts, eps, place, own, *refs):
    moe, refs = refs[:parts], refs[parts:]
    gain, home, refs = refs[0], refs[1], refs[2:]
    mine, theirs, out, mixed, normed = refs
    half, ep, pool = place[0], place[1], place[2]
    width = moe[0].shape[1]
    square = jnp.zeros((own.shape[0], 1), F32)
    for k in range(parts):
        columns = columns_of(half ^ k, width)
        value = own[:, columns].astype(F32) + moe[k][...].astype(F32)
        mixed[:, columns] = value
        square += jnp.sum(value * value, axis=1, keepdims=True)
    factor = lax.rsqrt(square / mixed.shape[1] + 1e-06)
    normed[...] = (mixed[...] * factor * gain[...]).astype(BF16)
    depth, narrow = home.shape[0], mine.shape[1]
    for side, pieces in ((pool, mine), (1 - pool, theirs)):
        kept = columns_of(side, narrow)
        total = jnp.dot(
            normed[:, columns_of(ep, depth)], home[:, kept], preferred_element_type=F32
        )
        for d in range(1, eps):
            origin = lax.rem(ep + eps - d, eps)
            total += jnp.dot(
                normed[:, columns_of(origin, depth)],
                pieces[(d - 1) * depth : d * depth, :],
                preferred_element_type=F32,
            )
        out[:, kept] = total.astype(BF16)


def project(place, own, moe, gain, home, mine, theirs, eps):
    return pl.pallas_call(
        functools.partial(project_kernel, len(moe), eps),
        out_shape=jax.ShapeDtypeStruct((own.shape[0], home.shape[1]), BF16),
        grid_spec=pltpu.PrefetchScalarGridSpec(
            num_scalar_prefetch=1,
            grid=(),
            in_specs=[WHOLE] * (len(moe) + 5),
            out_specs=WHOLE,
            scratch_shapes=[pltpu.VMEM(own.shape, F32), pltpu.VMEM(own.shape, BF16)],
        ),
        compiler_params=params(0),
        name="project",
    )(place, own, *moe, gain, home, mine, theirs)


def attend_kernel(prompts, place, block, query, fresh_key, fresh_value, w_out, out):
    rows = query.shape[0]
    group_tok = block.shape[0]
    kv_heads = fresh_key.shape[1] // HEAD
    per_head = query.shape[1] // HEAD // kv_heads
    position = lax.broadcasted_iota(jnp.int32, (rows, group_tok), 1)
    row = place[0] * rows + lax.broadcasted_iota(jnp.int32, (rows, group_tok), 0)
    segment = jnp.zeros((rows, group_tok), jnp.int32)
    end = jnp.int32(0)
    for p in range(prompts):
        end = end + place[1 + p]
        segment += (position >= end).astype(jnp.int32)
    allowed = segment == row // SAMPLES
    scale = 1.0 / math.sqrt(HEAD)
    heads = []
    for kv in range(kv_heads):
        key = block[:, 2 * kv * HEAD : (2 * kv + 1) * HEAD]
        value = block[:, (2 * kv + 1) * HEAD : (2 * kv + 2) * HEAD]
        new_key = fresh_key[:, kv * HEAD : (kv + 1) * HEAD].astype(F32)
        new_value = fresh_value[:, kv * HEAD : (kv + 1) * HEAD].astype(F32)
        for j in range(per_head):
            head = (kv * per_head + j) * HEAD
            asked = query[:, head : head + HEAD]
            scores = (
                lax.dot_general(asked, key, (((1,), (1,)), ((), ())), preferred_element_type=F32)
                * scale
            )
            scores = jnp.where(allowed, scores, -1e30)
            own = jnp.sum(asked.astype(F32) * new_key, axis=1, keepdims=True) * scale
            top = jnp.maximum(jnp.max(scores, axis=1, keepdims=True), own)
            spread = jnp.where(allowed, jnp.exp(scores - top), 0.0)
            self_weight = jnp.exp(own - top)
            total = jnp.sum(spread, axis=1, keepdims=True) + self_weight
            probs = (spread / total).astype(BF16)
            self_prob = (self_weight / total).astype(BF16).astype(F32)
            mixed = jnp.dot(probs, value, preferred_element_type=F32) + self_prob * new_value
            heads.append(mixed.astype(BF16))
    attention = jnp.concatenate(heads, axis=1)
    out[...] = jnp.dot(attention, w_out[...], preferred_element_type=F32).astype(BF16)


def attend(piece, prompt_lengths, block, query, fresh_key, fresh_value, w_out, rows):
    prompts = prompt_lengths.shape[0]

    def cut(array):
        return pl.BlockSpec((rows, array.shape[1]), lambda i, place: (place[0], 0))

    return pl.pallas_call(
        functools.partial(attend_kernel, prompts),
        out_shape=jax.ShapeDtypeStruct((rows, w_out.shape[1]), BF16),
        grid_spec=pltpu.PrefetchScalarGridSpec(
            num_scalar_prefetch=1,
            grid=(1,),
            in_specs=[WHOLE, cut(query), cut(fresh_key), cut(fresh_value), WHOLE],
            out_specs=pl.BlockSpec((rows, w_out.shape[1]), lambda i, place: (0, 0)),
        ),
        compiler_params=params(1),
        name="attend",
    )(
        jnp.concatenate([piece, prompt_lengths]),
        block,
        query,
        fresh_key,
        fresh_value,
        w_out,
    )


def total_of(first, rest):
    value = first.astype(F32)
    for other in rest:
        value = value + other.astype(F32)
    return value


def on_device(
    tokens,
    routes,
    router,
    w_gate,
    w_up,
    w_down,
    norm_gain,
    w_kv,
    lengths,
    queries,
    new_keys,
    new_values,
    w_out,
):
    own = tokens[0]
    chosen = routes[0]
    local, model = own.shape
    top = chosen.shape[1]
    eps = lax.axis_size("ep")
    parts = lax.axis_size("half")
    half, ep, pool = lax.axis_index("half"), lax.axis_index("ep"), lax.axis_index("pool")
    width = model // parts

    tags = jnp.pad(chosen.astype(BF16), ((0, 0), (0, LANES - top)))
    quarter = lax.dynamic_slice_in_dim(own, half * width, width, axis=1)
    parcel = jnp.concatenate([quarter, tags], axis=1)
    arrived = [shift(parcel, "ep", d) for d in range(1, eps)]
    near = jnp.concatenate([a[:, :width] for a in arrived], axis=0)
    all_tags = jnp.concatenate([tags] + [a[:, width:] for a in arrived], axis=0)
    order = sorted(range(1, parts), key=lambda k: -bin(k).count("1"))
    others = [near] + [None] * (parts - 1)
    for k in order:
        others[k] = swap(near, "half", k)

    narrow = w_kv.shape[1] // 2
    piece, near = lax.optimization_barrier(
        (lax.dynamic_slice_in_dim(w_kv, pool * narrow, narrow, axis=1), near)
    )
    others[0] = near
    mine = jnp.concatenate([shift(piece, "ep", d) for d in range(1, eps)], axis=0)
    theirs = swap(mine, "pool", 1)

    place = jnp.stack([half, ep * w_gate.shape[0]])
    hidden = expand(place, own, others, all_tags, router.T, w_gate, w_up, top)
    partial = [None] * parts
    for k in order + [0]:
        partial[k] = reduce((half ^ k)[None], hidden, w_down, width, 256)
    gathered = [swap(partial[k], "half", k) for k in order]
    summed = total_of(partial[0], gathered)
    returned = [
        shift(summed[d * local : (d + 1) * local].astype(BF16), "ep", -d) for d in range(1, eps)
    ]
    moe_quarter = total_of(summed[:local], returned).astype(BF16)
    moe = [moe_quarter] + [None] * (parts - 1)
    for k in order:
        moe[k] = swap(moe_quarter, "half", k)
    keyvals = project(
        jnp.stack([half, ep, pool]), own, moe, norm_gain[None], w_kv, mine, theirs, eps
    )
    block = swap(keyvals, "pool", 1)

    prompt_lengths = lax.dynamic_index_in_dim(lengths, 1 - pool, 0, keepdims=False)[0]
    rows = queries.shape[1] // parts
    decoded = [None] * parts
    for k in order + [0]:
        decoded[k] = attend(
            (half ^ k)[None],
            prompt_lengths,
            block,
            queries[0],
            new_keys[0],
            new_values[0],
            w_out,
            rows,
        )
    sent = [swap(decoded[k], "half", k) for k in order]
    return total_of(decoded[0], sent).astype(BF16)[None]


def solution(mesh):
    in_specs = (
        P("pool", "ep", None),
        P("pool", "ep", None),
        P(),
        P("ep", None, "half"),
        P("ep", None, "half"),
        P("ep", "half", None),
        P(),
        P("ep", "half"),
        P(None, "ep", None),
        P("pool", "ep", "half"),
        P("pool", "ep", "half"),
        P("pool", "ep", "half"),
        P("half", None),
    )
    out_specs = P("pool", ("ep", "half"), None)
    return jax.shard_map(
        on_device, mesh=mesh, in_specs=in_specs, out_specs=out_specs, check_vma=False
    )
```

```python
import functools
import math

import jax
import jax.numpy as jnp
from jax import lax
from jax.experimental import pallas as pl
from jax.experimental.pallas import tpu as pltpu
from jax.sharding import PartitionSpec as P

HEAD = 128
SAMPLES = 128
LANES = 128
F32 = jnp.float32
BF16 = jnp.bfloat16
WHOLE = pl.BlockSpec(memory_space=pltpu.VMEM)


def swap(shard, axis, bits):
    return lax.ppermute(shard, axis, [(i, i ^ bits) for i in range(lax.axis_size(axis))])


def shift(shard, axis, distance):
    count = lax.axis_size(axis)
    return lax.ppermute(shard, axis, [(i, (i + distance) % count) for i in range(count)])


def params(steps, mebibytes):
    return pltpu.CompilerParams(
        dimension_semantics=("arbitrary",) * steps, vmem_limit_bytes=mebibytes * 1024 * 1024
    )


def in_vmem(array):
    return pltpu.with_memory_space_constraint(array, pltpu.VMEM)


def in_hbm(array):
    return pltpu.with_memory_space_constraint(array, pltpu.HBM)


def columns_of(piece, width):
    return pl.ds(pl.multiple_of(piece * width, width), width)


def gather_kernel(k, place, own, near, router, w_gate, w_up, *refs):
    totals, refs = (refs[:3], refs[3:]) if k else ((None,) * 3, refs)
    gate_out, up_out, logits_out, rows = refs
    local, width = own.shape[0], rows.shape[1]
    step = pl.program_id(0)

    @pl.when(step == 0)
    def _():
        columns = columns_of(place[0] ^ k, width)
        rows[:local, :] = own[:, columns]
        rows[local:, :] = near[...]
        logits = lax.dot_general(
            rows[...], router[:, columns], (((1,), (1,)), ((), ())), preferred_element_type=F32
        )
        logits_out[...] = logits + totals[2][...] if k else logits

    for total, weight, out in ((totals[0], w_gate, gate_out), (totals[1], w_up, up_out)):
        value = jnp.dot(rows[...], weight[0], preferred_element_type=F32)
        out[step] = value + total[step] if k else value


def finish_kernel(k, top, place, own, near, router, w_gate, w_up, *refs):
    gate_total, up_total, logits_total, tags, hidden, rows, weights = refs
    local, width = own.shape[0], rows.shape[1]
    step = pl.program_id(0)
    expert = lax.broadcasted_iota(jnp.int32, weights.shape, 1)

    @pl.when(step == 0)
    def _():
        columns = columns_of(place[0] ^ k, width)
        rows[:local, :] = own[:, columns]
        rows[local:, :] = near[...]
        logits = logits_total[...] + lax.dot_general(
            rows[...], router[:, columns], (((1,), (1,)), ((), ())), preferred_element_type=F32
        )
        named = tags[...].astype(F32).astype(jnp.int32)
        picked = named[:, 0:1] == expert
        for j in range(1, top):
            picked = jnp.logical_or(picked, named[:, j : j + 1] == expert)
        most = jnp.max(jnp.where(picked, logits, -1e30), axis=1, keepdims=True)
        spread = jnp.where(picked, jnp.exp(logits - most), 0.0)
        weights[...] = spread / jnp.sum(spread, axis=1, keepdims=True)

    gate = gate_total[step] + jnp.dot(rows[...], w_gate[0], preferred_element_type=F32)
    up = up_total[step] + jnp.dot(rows[...], w_up[0], preferred_element_type=F32)
    mine = expert == place[1] * pl.num_programs(0) + step
    scale = jnp.sum(jnp.where(mine, weights[...], 0.0), axis=1, keepdims=True)
    hidden[...] = (gate / (1.0 + jnp.exp(-gate)) * up * scale).astype(BF16)


def expand(k, place, own, near, router, w_gate, w_up, totals, tags, top):
    local, model = own.shape
    tokens = local + near.shape[0]
    experts, units = w_gate.shape[0], w_gate.shape[2]
    width = near.shape[1]
    last = tags is not None
    weight = pl.BlockSpec((1, width, units), lambda e, place: (e, place[0] ^ k, 0))
    operands = [own, in_vmem(near), router, in_hbm(w_gate), in_hbm(w_up)] + [in_vmem(t) for t in totals]
    scratch = [pltpu.VMEM((tokens, width), BF16)]
    if last:
        operands.append(tags)
        kernel = functools.partial(finish_kernel, k, top)
        scratch.append(pltpu.VMEM((tokens, router.shape[0]), F32))
        out_shape = pltpu.VMEM((tokens, experts * units), BF16)
        out_specs = pl.BlockSpec((tokens, units), lambda e, place: (0, e))
        aliases = {}
    else:
        kernel = functools.partial(gather_kernel, k)
        both = pltpu.VMEM((experts, tokens, units), F32)
        out_shape = [both, both, pltpu.VMEM((tokens, router.shape[0]), F32)]
        out_specs = [WHOLE] * 3
        aliases = {6 + i: i for i in range(len(totals))}
    return pl.pallas_call(
        kernel,
        out_shape=out_shape,
        grid_spec=pltpu.PrefetchScalarGridSpec(
            num_scalar_prefetch=1,
            grid=(experts,),
            in_specs=[WHOLE] * 3 + [weight] * 2 + [WHOLE] * (len(operands) - 5),
            out_specs=out_specs,
            scratch_shapes=scratch,
        ),
        input_output_aliases=aliases,
        compiler_params=params(1, 16 if tokens <= 1024 else 32),
        cost_estimate=pl.CostEstimate(
            flops=4 * tokens * width * experts * units,
            transcendentals=0,
            bytes_accessed=4 * experts * width * units,
        ),
        name="expand",
    )(place, *operands)


def reduce_kernel(place, hidden, w_down, out):
    weight = w_down[...].reshape(-1, w_down.shape[2])
    out[...] = jnp.dot(hidden[...], weight, preferred_element_type=F32).astype(BF16)


def reduce(k, place, hidden, w_down, width, block):
    experts, units, model = w_down.shape
    steps = width // block
    tokens = hidden.shape[0]
    return pl.pallas_call(
        reduce_kernel,
        out_shape=jax.ShapeDtypeStruct((tokens, width), BF16),
        grid_spec=pltpu.PrefetchScalarGridSpec(
            num_scalar_prefetch=1,
            grid=(steps,),
            in_specs=[
                WHOLE,
                pl.BlockSpec(
                    (experts, units, block),
                    lambda i, place: (0, 0, (place[0] ^ k) * steps + i),
                ),
            ],
            out_specs=pl.BlockSpec((tokens, block), lambda i, place: (0, i)),
        ),
        compiler_params=params(1, 16),
        cost_estimate=pl.CostEstimate(
            flops=2 * tokens * width * experts * units,
            transcendentals=0,
            bytes_accessed=2 * experts * width * units,
        ),
        name="reduce",
    )(place, in_vmem(hidden), in_hbm(w_down))


def project_kernel(parts, eps, place, own, *refs):
    moe, refs = refs[:parts], refs[parts:]
    gain, home, refs = refs[0], refs[1], refs[2:]
    mine, theirs, out, mixed, normed = refs
    half, ep, pool = place[0], place[1], place[2]
    width = moe[0].shape[1]
    square = jnp.zeros((own.shape[0], 1), F32)
    for k in range(parts):
        columns = columns_of(half ^ k, width)
        value = own[:, columns].astype(F32) + moe[k][...].astype(F32)
        mixed[:, columns] = value
        square += jnp.sum(value * value, axis=1, keepdims=True)
    factor = lax.rsqrt(square / mixed.shape[1] + 1e-06)
    normed[...] = (mixed[...] * factor * gain[...]).astype(BF16)
    depth, narrow = home.shape[0], mine.shape[1]
    for side, pieces in ((pool, mine), (1 - pool, theirs)):
        kept = columns_of(side, narrow)
        total = jnp.dot(
            normed[:, columns_of(ep, depth)], home[:, kept], preferred_element_type=F32
        )
        for d in range(1, eps):
            origin = lax.rem(ep + eps - d, eps)
            total += jnp.dot(
                normed[:, columns_of(origin, depth)],
                pieces[(d - 1) * depth : d * depth, :],
                preferred_element_type=F32,
            )
        out[:, kept] = total.astype(BF16)


def project(place, own, moe, gain, home, mine, theirs, eps):
    return pl.pallas_call(
        functools.partial(project_kernel, len(moe), eps),
        out_shape=jax.ShapeDtypeStruct((own.shape[0], home.shape[1]), BF16),
        grid_spec=pltpu.PrefetchScalarGridSpec(
            num_scalar_prefetch=1,
            grid=(),
            in_specs=[WHOLE] * (len(moe) + 5),
            out_specs=WHOLE,
            scratch_shapes=[pltpu.VMEM(own.shape, F32), pltpu.VMEM(own.shape, BF16)],
        ),
        compiler_params=params(0, 12),
        name="project",
    )(place, own, *moe, gain, home, mine, theirs)


def attend_kernel(k, prompts, place, block, query, fresh_key, fresh_value, w_out, out):
    rows = query.shape[0]
    group_tok = block.shape[0]
    kv_heads = fresh_key.shape[1] // HEAD
    per_head = query.shape[1] // HEAD // kv_heads
    heads = kv_heads * per_head
    position = lax.broadcasted_iota(jnp.int32, (rows, group_tok), 1)
    row = (place[0] ^ k) * rows + lax.broadcasted_iota(jnp.int32, (rows, group_tok), 0)
    segment = jnp.zeros((rows, group_tok), jnp.int32)
    end = jnp.int32(0)
    for p in range(prompts):
        end = end + place[3 + p]
        segment += (position >= end).astype(jnp.int32)
    allowed = jnp.where(segment == row // SAMPLES, 1.0, 0.0)
    allowed = jnp.concatenate([allowed] * heads, axis=0) > 0.5
    scale = 1.0 / math.sqrt(HEAD)
    scores, owns = [], []
    for kv in range(kv_heads):
        key = block[:, 2 * kv * HEAD : (2 * kv + 1) * HEAD]
        new_key = fresh_key[:, kv * HEAD : (kv + 1) * HEAD].astype(F32)
        first = kv * per_head * HEAD
        asked = [query[:, first + j * HEAD : first + (j + 1) * HEAD] for j in range(per_head)]
        scores.append(
            lax.dot_general(
                jnp.concatenate(asked, axis=0),
                key,
                (((1,), (1,)), ((), ())),
                preferred_element_type=F32,
            )
        )
        owns += [jnp.sum(q.astype(F32) * new_key, axis=1, keepdims=True) for q in asked]
    scores = jnp.where(allowed, jnp.concatenate(scores, axis=0) * scale, -1e30)
    own = jnp.concatenate(owns, axis=0) * scale
    top = jnp.maximum(jnp.max(scores, axis=1, keepdims=True), own)
    spread = jnp.where(allowed, jnp.exp(scores - top), 0.0)
    self_weight = jnp.exp(own - top)
    total = jnp.sum(spread, axis=1, keepdims=True) + self_weight
    probs = (spread / total).astype(BF16)
    self_prob = (self_weight / total).astype(BF16).astype(F32)
    mixed = []
    for kv in range(kv_heads):
        value = block[:, (2 * kv + 1) * HEAD : (2 * kv + 2) * HEAD]
        new_value = fresh_value[:, kv * HEAD : (kv + 1) * HEAD].astype(F32)
        lower = kv * per_head * rows
        summed = jnp.dot(
            probs[lower : lower + per_head * rows], value, preferred_element_type=F32
        )
        for j in range(per_head):
            at = slice(j * rows, (j + 1) * rows)
            own_part = self_prob[lower + j * rows : lower + (j + 1) * rows] * new_value
            mixed.append((summed[at] + own_part).astype(BF16))
    attention = jnp.concatenate(mixed, axis=1)
    out[...] = jnp.dot(attention, w_out[...], preferred_element_type=F32).astype(BF16)


def attend(k, prompts, place, block, query, fresh_key, fresh_value, w_out, rows):
    def cut(array):
        return pl.BlockSpec((rows, array.shape[1]), lambda i, place: (place[0] ^ k, 0))

    return pl.pallas_call(
        functools.partial(attend_kernel, k, prompts),
        out_shape=jax.ShapeDtypeStruct((rows, w_out.shape[1]), BF16),
        grid_spec=pltpu.PrefetchScalarGridSpec(
            num_scalar_prefetch=1,
            grid=(1,),
            in_specs=[WHOLE, cut(query), cut(fresh_key), cut(fresh_value), WHOLE],
            out_specs=pl.BlockSpec((rows, w_out.shape[1]), lambda i, place: (0, 0)),
        ),
        compiler_params=params(1, 8),
        cost_estimate=pl.CostEstimate(
            flops=4 * rows * w_out.shape[0] * w_out.shape[1],
            transcendentals=0,
            bytes_accessed=2 * w_out.size,
        ),
        name="attend",
    )(place, block, query, fresh_key, fresh_value, w_out)


def total_of(first, rest):
    value = first.astype(F32)
    for other in rest:
        value = value + other.astype(F32)
    return value


def on_device(
    tokens,
    routes,
    router,
    w_gate,
    w_up,
    w_down,
    norm_gain,
    w_kv,
    lengths,
    queries,
    new_keys,
    new_values,
    w_out,
):
    own = tokens[0]
    chosen = routes[0]
    local, model = own.shape
    top = chosen.shape[1]
    eps = lax.axis_size("ep")
    parts = lax.axis_size("half")
    half, ep, pool = lax.axis_index("half"), lax.axis_index("ep"), lax.axis_index("pool")
    width = model // parts

    prompt_lengths = lax.dynamic_index_in_dim(lengths, 1 - pool, 0, keepdims=False)[0]
    place = jnp.concatenate([jnp.stack([half, ep, pool]), prompt_lengths])

    tags = jnp.pad(chosen.astype(BF16), ((0, 0), (0, LANES - top)))
    quarter = lax.dynamic_slice_in_dim(own, half * width, width, axis=1)
    parcel = jnp.concatenate([quarter, tags], axis=1)
    arrived = [shift(parcel, "ep", d) for d in range(1, eps)]
    near = jnp.concatenate([a[:, :width] for a in arrived], axis=0)
    all_tags = jnp.concatenate([tags] + [a[:, width:] for a in arrived], axis=0)
    order = sorted(range(1, parts), key=lambda k: bin(k).count("1"))
    others = {k: swap(near, "half", k) for k in order}

    narrow = w_kv.shape[1] // 2
    piece, near = lax.optimization_barrier(
        (lax.dynamic_slice_in_dim(w_kv, pool * narrow, narrow, axis=1), near)
    )
    others[0] = near
    mine = jnp.concatenate([shift(piece, "ep", d) for d in range(1, eps)], axis=0)
    theirs = swap(mine, "pool", 1)

    totals = ()
    for k in [0] + order:
        totals = expand(
            k,
            place,
            own,
            others[k],
            router.T,
            w_gate,
            w_up,
            totals,
            all_tags if k == order[-1] else None,
            top,
        )
    hidden = totals
    partial = {k: reduce(k, place, hidden, w_down, width, width // 2) for k in order + [0]}
    gathered = [swap(partial[k], "half", k) for k in order]
    summed = total_of(partial[0], gathered)
    returned = [
        shift(summed[d * local : (d + 1) * local].astype(BF16), "ep", -d) for d in range(1, eps)
    ]
    moe_quarter = total_of(summed[:local], returned).astype(BF16)
    moe = [moe_quarter] + [None] * (parts - 1)
    for k in order:
        moe[k] = swap(moe_quarter, "half", k)
    keyvals = project(place, own, moe, norm_gain[None], w_kv, mine, theirs, eps)
    block = swap(keyvals, "pool", 1)

    rows = queries.shape[1] // parts
    decoded = {
        k: attend(
            k,
            lengths.shape[2],
            place,
            block,
            queries[0],
            new_keys[0],
            new_values[0],
            w_out,
            rows,
        )
        for k in order + [0]
    }
    sent = [swap(decoded[k], "half", k) for k in order]
    return total_of(decoded[0], sent).astype(BF16)[None]


def solution(mesh):
    in_specs = (
        P("pool", "ep", None),
        P("pool", "ep", None),
        P(),
        P("ep", None, "half"),
        P("ep", None, "half"),
        P("ep", "half", None),
        P(),
        P("ep", "half"),
        P(None, "ep", None),
        P("pool", "ep", "half"),
        P("pool", "ep", "half"),
        P("pool", "ep", "half"),
        P("half", None),
    )
    out_specs = P("pool", ("ep", "half"), None)
    return jax.shard_map(
        on_device, mesh=mesh, in_specs=in_specs, out_specs=out_specs, check_vma=False
    )
```

```python
import functools
import math

import jax
import jax.numpy as jnp
from jax import lax
from jax.experimental import pallas as pl
from jax.experimental.pallas import tpu as pltpu
from jax.sharding import PartitionSpec as P

HEAD = 128
SAMPLES = 128
LANES = 128
F32 = jnp.float32
BF16 = jnp.bfloat16
WHOLE = pl.BlockSpec(memory_space=pltpu.VMEM)


def swap(shard, axis, bits):
    return lax.ppermute(shard, axis, [(i, i ^ bits) for i in range(lax.axis_size(axis))])


def shift(shard, axis, distance):
    count = lax.axis_size(axis)
    return lax.ppermute(shard, axis, [(i, (i + distance) % count) for i in range(count)])


def params(steps, mebibytes):
    return pltpu.CompilerParams(
        dimension_semantics=("arbitrary",) * steps, vmem_limit_bytes=mebibytes * 1024 * 1024
    )


def in_vmem(array):
    return pltpu.with_memory_space_constraint(array, pltpu.VMEM)


def in_hbm(array):
    return pltpu.with_memory_space_constraint(array, pltpu.HBM)


def columns_of(piece, width):
    return pl.ds(pl.multiple_of(piece * width, width), width)


def take_rows(k, place, own, near, rows):
    local, width = own.shape[0], rows.shape[1]
    columns = columns_of(place[0] ^ k, width)
    rows[:local, :] = own[:, columns]
    rows[local:, :] = near[...]
    return columns


def both(rows, w_gate, w_up, i):
    weight = jnp.concatenate([w_gate[i], w_up[i]], axis=1)
    return jnp.dot(rows[...], weight, preferred_element_type=F32)


def router_logits(rows, router, columns):
    return lax.dot_general(
        rows[...], router[:, columns], (((1,), (1,)), ((), ())), preferred_element_type=F32
    )


def gather_kernel(k, place, own, near, router, w_gate, w_up, *refs):
    totals, refs = (refs[:2], refs[2:]) if k else ((None,) * 2, refs)
    out, logits_out, rows = refs
    step = pl.program_id(0)

    @pl.when(step == 0)
    def _():
        columns = take_rows(k, place, own, near, rows)
        logits = router_logits(rows, router, columns)
        logits_out[...] = logits + totals[1][...] if k else logits

    for i in range(w_gate.shape[0]):
        expert = step * w_gate.shape[0] + i
        value = both(rows, w_gate, w_up, i)
        out[expert] = value + totals[0][expert] if k else value


def finish_kernel(k, top, place, own, near, router, w_gate, w_up, *refs):
    total, logits_total, tags, hidden, rows, weights = refs
    step, each, units = pl.program_id(0), w_gate.shape[0], w_gate.shape[2]
    expert = lax.broadcasted_iota(jnp.int32, weights.shape, 1)

    @pl.when(step == 0)
    def _():
        columns = take_rows(k, place, own, near, rows)
        logits = logits_total[...] + router_logits(rows, router, columns)
        named = tags[...].astype(F32).astype(jnp.int32)
        picked = named[:, 0:1] == expert
        for j in range(1, top):
            picked = jnp.logical_or(picked, named[:, j : j + 1] == expert)
        most = jnp.max(jnp.where(picked, logits, -1e30), axis=1, keepdims=True)
        spread = jnp.where(picked, jnp.exp(logits - most), 0.0)
        weights[...] = spread / jnp.sum(spread, axis=1, keepdims=True)

    for i in range(each):
        value = total[step * each + i] + both(rows, w_gate, w_up, i)
        gate, up = value[:, :units], value[:, units:]
        mine = expert == (place[1] * pl.num_programs(0) + step) * each + i
        scale = jnp.sum(jnp.where(mine, weights[...], 0.0), axis=1, keepdims=True)
        hidden[:, i * units : (i + 1) * units] = (
            gate / (1.0 + jnp.exp(-gate)) * up * scale
        ).astype(BF16)


def expand(k, place, own, near, router, w_gate, w_up, totals, tags, top):
    local, model = own.shape
    tokens = local + near.shape[0]
    experts, units = w_gate.shape[0], w_gate.shape[2]
    each = math.gcd(experts, 4)
    width = near.shape[1]
    last = tags is not None
    weight = pl.BlockSpec((each, width, units), lambda e, place: (e, place[0] ^ k, 0))
    operands = [own, in_vmem(near), router, in_hbm(w_gate), in_hbm(w_up)]
    operands += [in_vmem(t) for t in totals]
    scratch = [pltpu.VMEM((tokens, width), BF16)]
    if last:
        operands.append(tags)
        kernel = functools.partial(finish_kernel, k, top)
        scratch.append(pltpu.VMEM((tokens, router.shape[0]), F32))
        out_shape = pltpu.VMEM((tokens, experts * units), BF16)
        out_specs = pl.BlockSpec((tokens, each * units), lambda e, place: (0, e))
        aliases = {}
    else:
        kernel = functools.partial(gather_kernel, k)
        out_shape = [
            pltpu.VMEM((experts, tokens, 2 * units), F32),
            pltpu.VMEM((tokens, router.shape[0]), F32),
        ]
        out_specs = [WHOLE] * 2
        aliases = {6 + i: i for i in range(len(totals))}
    return pl.pallas_call(
        kernel,
        out_shape=out_shape,
        grid_spec=pltpu.PrefetchScalarGridSpec(
            num_scalar_prefetch=1,
            grid=(experts // each,),
            in_specs=[WHOLE] * 3 + [weight] * 2 + [WHOLE] * (len(operands) - 5),
            out_specs=out_specs,
            scratch_shapes=scratch,
        ),
        input_output_aliases=aliases,
        compiler_params=params(1, 24 if tokens <= 1024 else 32),
        cost_estimate=pl.CostEstimate(
            flops=4 * tokens * width * experts * units,
            transcendentals=0,
            bytes_accessed=4 * experts * width * units,
        ),
        name="expand",
    )(place, *operands)


def reduce_kernel(place, hidden, w_down, out):
    weight = w_down[...].reshape(-1, w_down.shape[2])
    out[...] = jnp.dot(hidden[...], weight, preferred_element_type=F32).astype(BF16)


def reduce(k, place, hidden, w_down, width, block):
    experts, units, model = w_down.shape
    steps = width // block
    tokens = hidden.shape[0]
    return pl.pallas_call(
        reduce_kernel,
        out_shape=jax.ShapeDtypeStruct((tokens, width), BF16),
        grid_spec=pltpu.PrefetchScalarGridSpec(
            num_scalar_prefetch=1,
            grid=(steps,),
            in_specs=[
                WHOLE,
                pl.BlockSpec(
                    (experts, units, block),
                    lambda i, place: (0, 0, (place[0] ^ k) * steps + i),
                ),
            ],
            out_specs=pl.BlockSpec((tokens, block), lambda i, place: (0, i)),
        ),
        compiler_params=params(1, 16),
        cost_estimate=pl.CostEstimate(
            flops=2 * tokens * width * experts * units,
            transcendentals=0,
            bytes_accessed=2 * experts * width * units,
        ),
        name="reduce",
    )(place, in_vmem(hidden), in_hbm(w_down))


def project_kernel(parts, eps, place, own, *refs):
    moe, refs = refs[:parts], refs[parts:]
    gain, home, refs = refs[0], refs[1], refs[2:]
    mine, theirs, out, mixed, normed = refs
    half, ep, pool = place[0], place[1], place[2]
    width = moe[0].shape[1]
    square = jnp.zeros((own.shape[0], 1), F32)
    for k in range(parts):
        columns = columns_of(half ^ k, width)
        value = own[:, columns].astype(F32) + moe[k][...].astype(F32)
        mixed[:, columns] = value
        square += jnp.sum(value * value, axis=1, keepdims=True)
    factor = lax.rsqrt(square / mixed.shape[1] + 1e-06)
    normed[...] = (mixed[...] * factor * gain[...]).astype(BF16)
    depth, narrow = home.shape[0], mine.shape[1]
    for side, pieces in ((pool, mine), (1 - pool, theirs)):
        kept = columns_of(side, narrow)
        total = jnp.dot(
            normed[:, columns_of(ep, depth)], home[:, kept], preferred_element_type=F32
        )
        for d in range(1, eps):
            origin = lax.rem(ep + eps - d, eps)
            total += jnp.dot(
                normed[:, columns_of(origin, depth)],
                pieces[(d - 1) * depth : d * depth, :],
                preferred_element_type=F32,
            )
        out[:, kept] = total.astype(BF16)


def project(place, own, moe, gain, home, mine, theirs, eps):
    return pl.pallas_call(
        functools.partial(project_kernel, len(moe), eps),
        out_shape=jax.ShapeDtypeStruct((own.shape[0], home.shape[1]), BF16),
        grid_spec=pltpu.PrefetchScalarGridSpec(
            num_scalar_prefetch=1,
            grid=(),
            in_specs=[WHOLE] * (len(moe) + 5),
            out_specs=WHOLE,
            scratch_shapes=[pltpu.VMEM(own.shape, F32), pltpu.VMEM(own.shape, BF16)],
        ),
        compiler_params=params(0, 12),
        name="project",
    )(place, own, *moe, gain, home, mine, theirs)


def attend_kernel(k, prompts, place, block, query, fresh_key, fresh_value, w_out, out):
    rows = query.shape[0]
    group_tok = block.shape[0]
    kv_heads = fresh_key.shape[1] // HEAD
    per_head = query.shape[1] // HEAD // kv_heads
    heads = kv_heads * per_head
    position = lax.broadcasted_iota(jnp.int32, (rows, group_tok), 1)
    row = (place[0] ^ k) * rows + lax.broadcasted_iota(jnp.int32, (rows, group_tok), 0)
    segment = jnp.zeros((rows, group_tok), jnp.int32)
    end = jnp.int32(0)
    for p in range(prompts):
        end = end + place[3 + p]
        segment += (position >= end).astype(jnp.int32)
    allowed = jnp.where(segment == row // SAMPLES, 1.0, 0.0)
    allowed = jnp.concatenate([allowed] * heads, axis=0) > 0.5
    scale = 1.0 / math.sqrt(HEAD)
    scores, owns = [], []
    for kv in range(kv_heads):
        key = block[:, 2 * kv * HEAD : (2 * kv + 1) * HEAD]
        new_key = fresh_key[:, kv * HEAD : (kv + 1) * HEAD].astype(F32)
        first = kv * per_head * HEAD
        asked = [query[:, first + j * HEAD : first + (j + 1) * HEAD] for j in range(per_head)]
        scores.append(
            lax.dot_general(
                jnp.concatenate(asked, axis=0),
                key,
                (((1,), (1,)), ((), ())),
                preferred_element_type=F32,
            )
        )
        owns += [jnp.sum(q.astype(F32) * new_key, axis=1, keepdims=True) for q in asked]
    scores = jnp.where(allowed, jnp.concatenate(scores, axis=0) * scale, -1e30)
    own = jnp.concatenate(owns, axis=0) * scale
    top = jnp.maximum(jnp.max(scores, axis=1, keepdims=True), own)
    spread = jnp.where(allowed, jnp.exp(scores - top), 0.0)
    self_weight = jnp.exp(own - top)
    total = jnp.sum(spread, axis=1, keepdims=True) + self_weight
    probs = (spread / total).astype(BF16)
    self_prob = (self_weight / total).astype(BF16).astype(F32)
    mixed = []
    for kv in range(kv_heads):
        value = block[:, (2 * kv + 1) * HEAD : (2 * kv + 2) * HEAD]
        new_value = fresh_value[:, kv * HEAD : (kv + 1) * HEAD].astype(F32)
        lower = kv * per_head * rows
        summed = jnp.dot(
            probs[lower : lower + per_head * rows], value, preferred_element_type=F32
        )
        for j in range(per_head):
            at = slice(j * rows, (j + 1) * rows)
            own_part = self_prob[lower + j * rows : lower + (j + 1) * rows] * new_value
            mixed.append((summed[at] + own_part).astype(BF16))
    attention = jnp.concatenate(mixed, axis=1)
    out[...] = jnp.dot(attention, w_out[...], preferred_element_type=F32).astype(BF16)


def attend(k, prompts, place, block, query, fresh_key, fresh_value, w_out, rows):
    def cut(array):
        return pl.BlockSpec((rows, array.shape[1]), lambda i, place: (place[0] ^ k, 0))

    return pl.pallas_call(
        functools.partial(attend_kernel, k, prompts),
        out_shape=jax.ShapeDtypeStruct((rows, w_out.shape[1]), BF16),
        grid_spec=pltpu.PrefetchScalarGridSpec(
            num_scalar_prefetch=1,
            grid=(1,),
            in_specs=[WHOLE, cut(query), cut(fresh_key), cut(fresh_value), WHOLE],
            out_specs=pl.BlockSpec((rows, w_out.shape[1]), lambda i, place: (0, 0)),
        ),
        compiler_params=params(1, 8),
        cost_estimate=pl.CostEstimate(
            flops=4 * rows * w_out.shape[0] * w_out.shape[1],
            transcendentals=0,
            bytes_accessed=2 * w_out.size,
        ),
        name="attend",
    )(place, block, query, fresh_key, fresh_value, w_out)


def total_of(first, rest):
    value = first.astype(F32)
    for other in rest:
        value = value + other.astype(F32)
    return value


def on_device(
    tokens,
    routes,
    router,
    w_gate,
    w_up,
    w_down,
    norm_gain,
    w_kv,
    lengths,
    queries,
    new_keys,
    new_values,
    w_out,
):
    own = tokens[0]
    chosen = routes[0]
    local, model = own.shape
    top = chosen.shape[1]
    eps = lax.axis_size("ep")
    parts = lax.axis_size("half")
    half, ep, pool = lax.axis_index("half"), lax.axis_index("ep"), lax.axis_index("pool")
    width = model // parts

    prompt_lengths = lax.dynamic_index_in_dim(lengths, 1 - pool, 0, keepdims=False)[0]
    place = jnp.concatenate([jnp.stack([half, ep, pool]), prompt_lengths])

    narrow = w_kv.shape[1] // 2
    tags = jnp.pad(chosen.astype(BF16), ((0, 0), (0, LANES - top)))
    quarter = lax.dynamic_slice_in_dim(own, half * width, width, axis=1)
    parcel = jnp.concatenate([quarter, tags], axis=1)
    piece, parcel = lax.optimization_barrier(
        (lax.dynamic_slice_in_dim(w_kv, pool * narrow, narrow, axis=1), parcel)
    )
    arrived = [shift(parcel, "ep", d) for d in range(1, eps)]
    near = jnp.concatenate([a[:, :width] for a in arrived], axis=0)
    all_tags = jnp.concatenate([tags] + [a[:, width:] for a in arrived], axis=0)
    order = sorted(range(1, parts), key=lambda k: bin(k).count("1"))
    others = {k: swap(near, "half", k) for k in order}

    others[0] = near
    pieces = [shift(piece, "ep", d) for d in range(1, eps)]

    totals = ()
    for k in [0] + order:
        totals = expand(
            k,
            place,
            own,
            others[k],
            router.T,
            w_gate,
            w_up,
            totals,
            all_tags if k == order[-1] else None,
            top,
        )
    hidden = totals
    far = order[::-1]
    partial = {k: reduce(k, place, hidden, w_down, width, width // 2) for k in far + [0]}
    gathered = [swap(partial[k], "half", k) for k in far]
    pieces, partial[0] = lax.optimization_barrier((pieces, partial[0]))
    mine = jnp.concatenate(pieces, axis=0)
    theirs = swap(mine, "pool", 1)
    summed = total_of(partial[0], gathered)
    returned = [
        shift(summed[d * local : (d + 1) * local].astype(BF16), "ep", -d) for d in range(1, eps)
    ]
    moe_quarter = total_of(summed[:local], returned).astype(BF16)
    moe = [moe_quarter] + [None] * (parts - 1)
    for k in order:
        moe[k] = swap(moe_quarter, "half", k)
    keyvals = project(place, own, moe, norm_gain[None], w_kv, mine, theirs, eps)
    block = swap(keyvals, "pool", 1)

    rows = queries.shape[1] // parts
    decoded = {
        k: attend(
            k,
            lengths.shape[2],
            place,
            block,
            queries[0],
            new_keys[0],
            new_values[0],
            w_out,
            rows,
        )
        for k in far + [0]
    }
    sent = [swap(decoded[k], "half", k) for k in far]
    return total_of(decoded[0], sent).astype(BF16)[None]


def solution(mesh):
    in_specs = (
        P("pool", "ep", None),
        P("pool", "ep", None),
        P(),
        P("ep", None, "half"),
        P("ep", None, "half"),
        P("ep", "half", None),
        P(),
        P("ep", "half"),
        P(None, "ep", None),
        P("pool", "ep", "half"),
        P("pool", "ep", "half"),
        P("pool", "ep", "half"),
        P("half", None),
    )
    out_specs = P("pool", ("ep", "half"), None)
    return jax.shard_map(
        on_device, mesh=mesh, in_specs=in_specs, out_specs=out_specs, check_vma=False
    )
```

```python
import functools
import math

import jax
import jax.numpy as jnp
from jax import lax
from jax.experimental import pallas as pl
from jax.experimental.pallas import tpu as pltpu
from jax.sharding import PartitionSpec as P


HEAD = 128
SAMPLES = 128
LANES = 128
F32 = jnp.float32
BF16 = jnp.bfloat16
WHOLE = pl.BlockSpec(memory_space=pltpu.VMEM)


def swap(shard, axis, bits):
    return lax.ppermute(shard, axis, [(i, i ^ bits) for i in range(lax.axis_size(axis))])


def shift(shard, axis, distance):
    count = lax.axis_size(axis)
    return lax.ppermute(shard, axis, [(i, (i + distance) % count) for i in range(count)])


def params(steps, mebibytes):
    return pltpu.CompilerParams(
        dimension_semantics=("arbitrary",) * steps, vmem_limit_bytes=mebibytes * 1024 * 1024
    )


def in_vmem(array):
    return pltpu.with_memory_space_constraint(array, pltpu.VMEM)


def in_hbm(array):
    return pltpu.with_memory_space_constraint(array, pltpu.HBM)


def columns_of(piece, width):
    return pl.ds(pl.multiple_of(piece * width, width), width)


def router_logits(rows, router, columns):
    return lax.dot_general(
        rows, router[:, columns], (((1,), (1,)), ((), ())), preferred_element_type=F32
    )


def take_rows(quarters, place, own, nears, router, rows):
    local = own.shape[0]
    width = nears[0].shape[1]
    logits = 0.0
    for i, (k, near) in enumerate(zip(quarters, nears)):
        columns = columns_of(place[0] ^ k, width)
        rows[:local, i * width : (i + 1) * width] = own[:, columns]
        rows[local:, i * width : (i + 1) * width] = near[...]
        logits += router_logits(rows[:, i * width : (i + 1) * width], router, columns)
    return logits


def both(rows, w_gates, w_ups, i):
    width = w_gates[0].shape[1]
    value = 0.0
    for j, (w_gate, w_up) in enumerate(zip(w_gates, w_ups)):
        weight = jnp.concatenate([w_gate[i], w_up[i]], axis=1)
        value += jnp.dot(
            rows[:, j * width : (j + 1) * width], weight, preferred_element_type=F32
        )
    return value


def gather_kernel(quarters, first, place, own, router, *refs):
    count = len(quarters)
    nears, w_gates, w_ups, refs = (
        refs[:count],
        refs[count : 2 * count],
        refs[2 * count : 3 * count],
        refs[3 * count :],
    )
    totals, refs = ((None,) * 2, refs) if first else (refs[:2], refs[2:])
    out, logits_out, rows = refs
    step, each = pl.program_id(0), w_gates[0].shape[0]

    @pl.when(step == 0)
    def _():
        logits = take_rows(quarters, place, own, nears, router, rows)
        logits_out[...] = logits if first else logits + totals[1][...]

    for i in range(each):
        value = both(rows, w_gates, w_ups, i)
        out[step * each + i] = value if first else value + totals[0][step * each + i]


def finish_kernel(quarters, top, place, own, router, *refs):
    count = len(quarters)
    nears, w_gates, w_ups, refs = (
        refs[:count],
        refs[count : 2 * count],
        refs[2 * count : 3 * count],
        refs[3 * count :],
    )
    total, logits_total, tags, hidden, rows, weights = refs
    step, each, units = pl.program_id(0), w_gates[0].shape[0], w_gates[0].shape[2]
    expert = lax.broadcasted_iota(jnp.int32, weights.shape, 1)

    @pl.when(step == 0)
    def _():
        logits = logits_total[...] + take_rows(quarters, place, own, nears, router, rows)
        named = tags[...].astype(F32).astype(jnp.int32)
        picked = named[:, 0:1] == expert
        for j in range(1, top):
            picked = jnp.logical_or(picked, named[:, j : j + 1] == expert)
        most = jnp.max(jnp.where(picked, logits, -1e30), axis=1, keepdims=True)
        spread = jnp.where(picked, jnp.exp(logits - most), 0.0)
        weights[...] = spread / jnp.sum(spread, axis=1, keepdims=True)

    for i in range(each):
        value = total[step * each + i] + both(rows, w_gates, w_ups, i)
        gate, up = value[:, :units], value[:, units:]
        mine = expert == (place[1] * pl.num_programs(0) + step) * each + i
        scale = jnp.sum(jnp.where(mine, weights[...], 0.0), axis=1, keepdims=True)
        hidden[:, i * units : (i + 1) * units] = (
            gate / (1.0 + jnp.exp(-gate)) * up * scale
        ).astype(BF16)


def expand(quarters, place, own, nears, router, w_gate, w_up, totals, tags, top):
    count = len(quarters)
    local, _ = own.shape
    tokens = local + nears[0].shape[0]
    experts, units = w_gate.shape[0], w_gate.shape[2]
    each = math.gcd(experts, 4 // count)
    width = nears[0].shape[1]
    last = tags is not None
    weight = [
        pl.BlockSpec((each, width, units), lambda e, place, k=k: (e, place[0] ^ k, 0))
        for k in quarters
    ]
    operands = [own, router] + [in_vmem(near) for near in nears]
    operands += [in_hbm(w_gate)] * count + [in_hbm(w_up)] * count
    operands += [in_vmem(t) for t in totals]
    scratch = [pltpu.VMEM((tokens, count * width), BF16)]
    if last:
        operands.append(tags)
        kernel = functools.partial(finish_kernel, quarters, top)
        scratch.append(pltpu.VMEM((tokens, router.shape[0]), F32))
        out_shape = pltpu.VMEM((tokens, experts * units), BF16)
        out_specs = pl.BlockSpec((tokens, each * units), lambda e, place: (0, e))
        aliases = {}
    else:
        kernel = functools.partial(gather_kernel, quarters, not totals)
        out_shape = [
            pltpu.VMEM((experts, tokens, 2 * units), F32),
            pltpu.VMEM((tokens, router.shape[0]), F32),
        ]
        out_specs = [WHOLE] * 2
        aliases = {3 + 3 * count + i: i for i in range(len(totals))}
    return pl.pallas_call(
        kernel,
        out_shape=out_shape,
        grid_spec=pltpu.PrefetchScalarGridSpec(
            num_scalar_prefetch=1,
            grid=(experts // each,),
            in_specs=[WHOLE] * (2 + count)
            + weight * 2
            + [WHOLE] * (len(operands) - 2 - 3 * count),
            out_specs=out_specs,
            scratch_shapes=scratch,
        ),
        input_output_aliases=aliases,
        compiler_params=params(1, 24 if tokens <= 1024 else 40),
        cost_estimate=pl.CostEstimate(
            flops=4 * tokens * width * experts * units * count,
            transcendentals=0,
            bytes_accessed=4 * experts * width * units * count,
        ),
        name="expand",
    )(place, *operands)


def reduce_kernel(place, hidden, w_down, out):
    weight = w_down[...].reshape(-1, w_down.shape[2])
    out[...] = jnp.dot(hidden[...], weight, preferred_element_type=F32).astype(BF16)


def reduce(k, place, hidden, w_down, width, block):
    experts, units, _ = w_down.shape
    steps = width // block
    tokens = hidden.shape[0]
    return pl.pallas_call(
        reduce_kernel,
        out_shape=jax.ShapeDtypeStruct((tokens, width), BF16),
        grid_spec=pltpu.PrefetchScalarGridSpec(
            num_scalar_prefetch=1,
            grid=(steps,),
            in_specs=[
                WHOLE,
                pl.BlockSpec(
                    (experts, units, block),
                    lambda i, place: (0, 0, (place[0] ^ k) * steps + i),
                ),
            ],
            out_specs=pl.BlockSpec((tokens, block), lambda i, place: (0, i)),
        ),
        compiler_params=params(1, 16),
        cost_estimate=pl.CostEstimate(
            flops=2 * tokens * width * experts * units,
            transcendentals=0,
            bytes_accessed=2 * experts * width * units,
        ),
        name="reduce",
    )(place, in_vmem(hidden), in_hbm(w_down))


def project_kernel(parts, eps, place, own, *refs):
    moe, refs = refs[:parts], refs[parts:]
    gain, home, refs = refs[0], refs[1], refs[2:]
    mine, theirs, out, mixed, normed = refs
    half, ep, pool = place[0], place[1], place[2]
    width = moe[0].shape[1]
    square = jnp.zeros((own.shape[0], 1), F32)
    for k in range(parts):
        columns = columns_of(half ^ k, width)
        value = own[:, columns].astype(F32) + moe[k][...].astype(F32)
        mixed[:, columns] = value
        square += jnp.sum(value * value, axis=1, keepdims=True)
    factor = lax.rsqrt(square / mixed.shape[1] + 1e-06)
    normed[...] = (mixed[...] * factor * gain[...]).astype(BF16)
    depth, narrow = home.shape[0], mine.shape[1]
    for side, pieces in ((pool, mine), (1 - pool, theirs)):
        kept = columns_of(side, narrow)
        total = jnp.dot(
            normed[:, columns_of(ep, depth)], home[:, kept], preferred_element_type=F32
        )
        for d in range(1, eps):
            origin = lax.rem(ep + eps - d, eps)
            total += jnp.dot(
                normed[:, columns_of(origin, depth)],
                pieces[(d - 1) * depth : d * depth, :],
                preferred_element_type=F32,
            )
        out[:, kept] = total.astype(BF16)


def project(place, own, moe, gain, home, mine, theirs, eps):
    return pl.pallas_call(
        functools.partial(project_kernel, len(moe), eps),
        out_shape=jax.ShapeDtypeStruct((own.shape[0], home.shape[1]), BF16),
        grid_spec=pltpu.PrefetchScalarGridSpec(
            num_scalar_prefetch=1,
            grid=(),
            in_specs=[WHOLE] * (len(moe) + 5),
            out_specs=WHOLE,
            scratch_shapes=[pltpu.VMEM(own.shape, F32), pltpu.VMEM(own.shape, BF16)],
        ),
        compiler_params=params(0, 12),
        name="project",
    )(place, own, *moe, gain, home, mine, theirs)


def attend_kernel(k, prompts, place, block, query, fresh_key, fresh_value, w_out, out):
    rows = query.shape[0]
    group_tok = block.shape[0]
    kv_heads = fresh_key.shape[1] // HEAD
    per_head = query.shape[1] // HEAD // kv_heads
    heads = kv_heads * per_head
    position = lax.broadcasted_iota(jnp.int32, (rows, group_tok), 1)
    row = (place[0] ^ k) * rows + lax.broadcasted_iota(jnp.int32, (rows, group_tok), 0)
    segment = jnp.zeros((rows, group_tok), jnp.int32)
    end = jnp.int32(0)
    for p in range(prompts):
        end = end + place[3 + p]
        segment += (position >= end).astype(jnp.int32)
    allowed = jnp.where(segment == row // SAMPLES, 1.0, 0.0)
    allowed = jnp.concatenate([allowed] * heads, axis=0) > 0.5
    scale = 1.0 / math.sqrt(HEAD)
    scores, owns = [], []
    for kv in range(kv_heads):
        key = block[:, 2 * kv * HEAD : (2 * kv + 1) * HEAD]
        new_key = fresh_key[:, kv * HEAD : (kv + 1) * HEAD].astype(F32)
        first = kv * per_head * HEAD
        asked = [query[:, first + j * HEAD : first + (j + 1) * HEAD] for j in range(per_head)]
        scores.append(
            lax.dot_general(
                jnp.concatenate(asked, axis=0),
                key,
                (((1,), (1,)), ((), ())),
                preferred_element_type=F32,
            )
        )
        owns += [jnp.sum(q.astype(F32) * new_key, axis=1, keepdims=True) for q in asked]
    scores = jnp.where(allowed, jnp.concatenate(scores, axis=0) * scale, -1e30)
    own = jnp.concatenate(owns, axis=0) * scale
    top = jnp.maximum(jnp.max(scores, axis=1, keepdims=True), own)
    spread = jnp.where(allowed, jnp.exp(scores - top), 0.0)
    self_weight = jnp.exp(own - top)
    total = jnp.sum(spread, axis=1, keepdims=True) + self_weight
    probs = (spread / total).astype(BF16)
    self_prob = (self_weight / total).astype(BF16).astype(F32)
    mixed = []
    for kv in range(kv_heads):
        value = block[:, (2 * kv + 1) * HEAD : (2 * kv + 2) * HEAD]
        new_value = fresh_value[:, kv * HEAD : (kv + 1) * HEAD].astype(F32)
        lower = kv * per_head * rows
        summed = jnp.dot(
            probs[lower : lower + per_head * rows], value, preferred_element_type=F32
        )
        for j in range(per_head):
            at = slice(j * rows, (j + 1) * rows)
            own_part = self_prob[lower + j * rows : lower + (j + 1) * rows] * new_value
            mixed.append((summed[at] + own_part).astype(BF16))
    attention = jnp.concatenate(mixed, axis=1)
    out[...] = jnp.dot(attention, w_out[...], preferred_element_type=F32).astype(BF16)


def attend(k, prompts, place, block, query, fresh_key, fresh_value, w_out, rows):
    def cut(array):
        return pl.BlockSpec((rows, array.shape[1]), lambda i, place: (place[0] ^ k, 0))

    return pl.pallas_call(
        functools.partial(attend_kernel, k, prompts),
        out_shape=jax.ShapeDtypeStruct((rows, w_out.shape[1]), BF16),
        grid_spec=pltpu.PrefetchScalarGridSpec(
            num_scalar_prefetch=1,
            grid=(1,),
            in_specs=[WHOLE, cut(query), cut(fresh_key), cut(fresh_value), WHOLE],
            out_specs=pl.BlockSpec((rows, w_out.shape[1]), lambda i, place: (0, 0)),
        ),
        compiler_params=params(1, 8),
        cost_estimate=pl.CostEstimate(
            flops=4 * rows * w_out.shape[0] * w_out.shape[1],
            transcendentals=0,
            bytes_accessed=2 * w_out.size,
        ),
        name="attend",
    )(place, block, query, fresh_key, fresh_value, w_out)


def total_of(first, rest):
    value = first.astype(F32)
    for other in rest:
        value = value + other.astype(F32)
    return value


def on_device(
    tokens,
    routes,
    router,
    w_gate,
    w_up,
    w_down,
    norm_gain,
    w_kv,
    lengths,
    queries,
    new_keys,
    new_values,
    w_out,
):
    own = tokens[0]
    chosen = routes[0]
    local, model = own.shape
    top = chosen.shape[1]
    eps = lax.axis_size("ep")
    parts = lax.axis_size("half")
    half, ep, pool = lax.axis_index("half"), lax.axis_index("ep"), lax.axis_index("pool")
    width = model // parts

    prompt_lengths = lax.dynamic_index_in_dim(lengths, 1 - pool, 0, keepdims=False)[0]
    place = jnp.concatenate([jnp.stack([half, ep, pool]), prompt_lengths])

    narrow = w_kv.shape[1] // 2
    tags = jnp.pad(chosen.astype(BF16), ((0, 0), (0, LANES - top)))
    quarter = lax.dynamic_slice_in_dim(own, half * width, width, axis=1)
    parcel = jnp.concatenate([quarter, tags], axis=1)
    piece, parcel = lax.optimization_barrier(
        (lax.dynamic_slice_in_dim(w_kv, pool * narrow, narrow, axis=1), parcel)
    )
    arrived = [shift(parcel, "ep", d) for d in range(1, eps)]
    near = jnp.concatenate([a[:, :width] for a in arrived], axis=0)
    all_tags = jnp.concatenate([tags] + [a[:, width:] for a in arrived], axis=0)
    order = sorted(range(1, parts), key=lambda k: bin(k).count("1"))
    far = order[::-1]
    others = {k: swap(near, "half", k) for k in order}
    others[0] = near
    pieces = [shift(piece, "ep", d) for d in range(1, eps)]

    totals = ()
    batches = [[0], order[:-1], order[-1:]]
    for quarters in batches:
        totals = expand(
            quarters,
            place,
            own,
            [others[k] for k in quarters],
            router.T,
            w_gate,
            w_up,
            totals,
            all_tags if quarters is batches[-1] else None,
            top,
        )
    hidden = totals
    partial = {}
    for k in far + [0]:
        partial[k] = reduce(k, place, hidden, w_down, width, width // 2)
    gathered = []
    for k in far:
        gathered.append(swap(partial[k], "half", k))
    pieces, partial[0] = lax.optimization_barrier((pieces, partial[0]))
    mine = jnp.concatenate(pieces, axis=0)
    theirs = swap(mine, "pool", 1)
    summed = total_of(partial[0], gathered)
    returned = [
        shift(summed[d * local : (d + 1) * local].astype(BF16), "ep", -d) for d in range(1, eps)
    ]
    moe_quarter = total_of(summed[:local], returned).astype(BF16)
    moe = [moe_quarter] + [None] * (parts - 1)
    for k in order:
        moe[k] = swap(moe_quarter, "half", k)
    keyvals = project(place, own, moe, norm_gain[None], w_kv, mine, theirs, eps)
    block = swap(keyvals, "pool", 1)

    rows = queries.shape[1] // parts
    decoded = {}
    for k in far + [0]:
        decoded[k] = attend(
            k,
            lengths.shape[2],
            place,
            block,
            queries[0],
            new_keys[0],
            new_values[0],
            w_out,
            rows,
        )
    sent = []
    for k in far:
        sent.append(swap(decoded[k], "half", k))
    return total_of(decoded[0], sent).astype(BF16)[None]


def solution(mesh):
    in_specs = (
        P("pool", "ep", None),
        P("pool", "ep", None),
        P(),
        P("ep", None, "half"),
        P("ep", None, "half"),
        P("ep", "half", None),
        P(),
        P("ep", "half"),
        P(None, "ep", None),
        P("pool", "ep", "half"),
        P("pool", "ep", "half"),
        P("pool", "ep", "half"),
        P("half", None),
    )
    out_specs = P("pool", ("ep", "half"), None)
    return jax.shard_map(
        on_device, mesh=mesh, in_specs=in_specs, out_specs=out_specs, check_vma=False
    )
```

```python
import functools
import math

import jax
import jax.numpy as jnp
from jax import lax
from jax.experimental import pallas as pl
from jax.experimental.pallas import tpu as pltpu
from jax.sharding import PartitionSpec as P


HEAD = 128
SAMPLES = 128
LANES = 128
F32 = jnp.float32
BF16 = jnp.bfloat16
WHOLE = pl.BlockSpec(memory_space=pltpu.VMEM)


def swap(shard, axis, bits):
    return lax.ppermute(shard, axis, [(i, i ^ bits) for i in range(lax.axis_size(axis))])


def shift(shard, axis, distance):
    count = lax.axis_size(axis)
    return lax.ppermute(shard, axis, [(i, (i + distance) % count) for i in range(count)])


def params(steps, mebibytes):
    return pltpu.CompilerParams(
        dimension_semantics=("arbitrary",) * steps, vmem_limit_bytes=mebibytes * 1024 * 1024
    )


def in_vmem(array):
    return pltpu.with_memory_space_constraint(array, pltpu.VMEM)


def in_hbm(array):
    return pltpu.with_memory_space_constraint(array, pltpu.HBM)


def columns_of(piece, width):
    return pl.ds(pl.multiple_of(piece * width, width), width)


def router_logits(rows, router, columns):
    return lax.dot_general(
        rows, router[:, columns], (((1,), (1,)), ((), ())), preferred_element_type=F32
    )


def take_rows(quarters, place, own, nears, router, rows):
    local = own.shape[0]
    width = nears[0].shape[1]
    logits = 0.0
    for i, (k, near) in enumerate(zip(quarters, nears)):
        columns = columns_of(place[0] ^ k, width)
        rows[:local, i * width : (i + 1) * width] = own[:, columns]
        rows[local:, i * width : (i + 1) * width] = near[...]
        logits += router_logits(rows[:, i * width : (i + 1) * width], router, columns)
    return logits


def both(rows, w_gates, w_ups, i):
    width = w_gates[0].shape[1]
    value = 0.0
    for j, (w_gate, w_up) in enumerate(zip(w_gates, w_ups)):
        weight = jnp.concatenate([w_gate[i], w_up[i]], axis=1)
        value += jnp.dot(
            rows[:, j * width : (j + 1) * width], weight, preferred_element_type=F32
        )
    return value


def gather_kernel(quarters, first, place, own, router, *refs):
    count = len(quarters)
    nears, w_gates, w_ups, refs = (
        refs[:count],
        refs[count : 2 * count],
        refs[2 * count : 3 * count],
        refs[3 * count :],
    )
    totals, refs = ((None,) * 2, refs) if first else (refs[:2], refs[2:])
    out, logits_out, rows = refs
    step, each = pl.program_id(0), w_gates[0].shape[0]

    @pl.when(step == 0)
    def _():
        logits = take_rows(quarters, place, own, nears, router, rows)
        logits_out[...] = logits if first else logits + totals[1][...]

    for i in range(each):
        value = both(rows, w_gates, w_ups, i)
        out[step * each + i] = value if first else value + totals[0][step * each + i]


def finish_kernel(quarters, top, place, own, router, *refs):
    count = len(quarters)
    nears, w_gates, w_ups, refs = (
        refs[:count],
        refs[count : 2 * count],
        refs[2 * count : 3 * count],
        refs[3 * count :],
    )
    total, logits_total, tags, hidden, rows, weights = refs
    step, each, units = pl.program_id(0), w_gates[0].shape[0], w_gates[0].shape[2]
    expert = lax.broadcasted_iota(jnp.int32, weights.shape, 1)

    @pl.when(step == 0)
    def _():
        logits = logits_total[...] + take_rows(quarters, place, own, nears, router, rows)
        named = tags[...].astype(F32).astype(jnp.int32)
        picked = named[:, 0:1] == expert
        for j in range(1, top):
            picked = jnp.logical_or(picked, named[:, j : j + 1] == expert)
        most = jnp.max(jnp.where(picked, logits, -1e30), axis=1, keepdims=True)
        spread = jnp.where(picked, jnp.exp(logits - most), 0.0)
        weights[...] = spread / jnp.sum(spread, axis=1, keepdims=True)

    for i in range(each):
        value = total[step * each + i] + both(rows, w_gates, w_ups, i)
        gate, up = value[:, :units], value[:, units:]
        mine = expert == (place[1] * pl.num_programs(0) + step) * each + i
        scale = jnp.sum(jnp.where(mine, weights[...], 0.0), axis=1, keepdims=True)
        hidden[:, i * units : (i + 1) * units] = (
            gate / (1.0 + jnp.exp(-gate)) * up * scale
        ).astype(BF16)


def expand(quarters, place, own, nears, router, w_gate, w_up, totals, tags, top):
    count = len(quarters)
    local, _ = own.shape
    tokens = local + nears[0].shape[0]
    experts, units = w_gate.shape[0], w_gate.shape[2]
    each = math.gcd(experts, 4 // count)
    width = nears[0].shape[1]
    last = tags is not None
    weight = [
        pl.BlockSpec((each, width, units), lambda e, place, k=k: (e, place[0] ^ k, 0))
        for k in quarters
    ]
    operands = [own, router] + [in_vmem(near) for near in nears]
    operands += [in_hbm(w_gate)] * count + [in_hbm(w_up)] * count
    operands += [in_vmem(t) for t in totals]
    scratch = [pltpu.VMEM((tokens, count * width), BF16)]
    if last:
        operands.append(tags)
        kernel = functools.partial(finish_kernel, quarters, top)
        scratch.append(pltpu.VMEM((tokens, router.shape[0]), F32))
        out_shape = pltpu.VMEM((tokens, experts * units), BF16)
        out_specs = pl.BlockSpec((tokens, each * units), lambda e, place: (0, e))
        aliases = {}
    else:
        kernel = functools.partial(gather_kernel, quarters, not totals)
        out_shape = [
            pltpu.VMEM((experts, tokens, 2 * units), F32),
            pltpu.VMEM((tokens, router.shape[0]), F32),
        ]
        out_specs = [WHOLE] * 2
        aliases = {3 + 3 * count + i: i for i in range(len(totals))}
    return pl.pallas_call(
        kernel,
        out_shape=out_shape,
        grid_spec=pltpu.PrefetchScalarGridSpec(
            num_scalar_prefetch=1,
            grid=(experts // each,),
            in_specs=[WHOLE] * (2 + count)
            + weight * 2
            + [WHOLE] * (len(operands) - 2 - 3 * count),
            out_specs=out_specs,
            scratch_shapes=scratch,
        ),
        input_output_aliases=aliases,
        compiler_params=params(1, 24 if tokens <= 1024 else 40),
        cost_estimate=pl.CostEstimate(
            flops=4 * tokens * width * experts * units * count,
            transcendentals=0,
            bytes_accessed=4 * experts * width * units * count,
        ),
        name="expand",
    )(place, *operands)


def reduce_kernel(place, hidden, w_down, out):
    weight = w_down[...].reshape(-1, w_down.shape[2])
    out[...] = jnp.dot(hidden[...], weight, preferred_element_type=F32).astype(BF16)


def reduce(k, place, hidden, w_down, width, block):
    experts, units, _ = w_down.shape
    steps = width // block
    tokens = hidden.shape[0]
    return pl.pallas_call(
        reduce_kernel,
        out_shape=jax.ShapeDtypeStruct((tokens, width), BF16),
        grid_spec=pltpu.PrefetchScalarGridSpec(
            num_scalar_prefetch=1,
            grid=(steps,),
            in_specs=[
                WHOLE,
                pl.BlockSpec(
                    (experts, units, block),
                    lambda i, place: (0, 0, (place[0] ^ k) * steps + i),
                ),
            ],
            out_specs=pl.BlockSpec((tokens, block), lambda i, place: (0, i)),
        ),
        compiler_params=params(1, 16),
        cost_estimate=pl.CostEstimate(
            flops=2 * tokens * width * experts * units,
            transcendentals=0,
            bytes_accessed=2 * experts * width * units,
        ),
        name="reduce",
    )(place, in_vmem(hidden), in_hbm(w_down))


def project_kernel(parts, origins, place, own, *refs):
    moe, refs = refs[:parts], refs[parts:]
    gain, mine, theirs, out, mixed, normed = refs
    half, ep, pool = place[0], place[1], place[2]
    width = moe[0].shape[1]
    square = jnp.zeros((own.shape[0], 1), F32)
    for k in range(parts):
        columns = columns_of(half ^ k, width)
        value = own[:, columns].astype(F32) + moe[k][...].astype(F32)
        mixed[:, columns] = value
        square += jnp.sum(value * value, axis=1, keepdims=True)
    factor = lax.rsqrt(square / mixed.shape[1] + 1e-06)
    normed[...] = (mixed[...] * factor * gain[...]).astype(BF16)
    depth, narrow = mine.shape[0] // len(origins), mine.shape[1]
    for side, pieces in ((pool, mine), (1 - pool, theirs)):
        total = 0.0
        for i, origin in enumerate(origins):
            total += jnp.dot(
                normed[:, columns_of(ep ^ origin, depth)],
                pieces[i * depth : (i + 1) * depth, :],
                preferred_element_type=F32,
            )
        out[:, columns_of(side, narrow)] = total.astype(BF16)


def project(place, own, moe, gain, mine, theirs, origins):
    return pl.pallas_call(
        functools.partial(project_kernel, len(moe), origins),
        out_shape=jax.ShapeDtypeStruct((own.shape[0], 2 * mine.shape[1]), BF16),
        grid_spec=pltpu.PrefetchScalarGridSpec(
            num_scalar_prefetch=1,
            grid=(),
            in_specs=[WHOLE] * (len(moe) + 4),
            out_specs=WHOLE,
            scratch_shapes=[pltpu.VMEM(own.shape, F32), pltpu.VMEM(own.shape, BF16)],
        ),
        compiler_params=params(0, 12),
        name="project",
    )(place, own, *moe, gain, mine, theirs)


def attend_kernel(k, prompts, place, block, query, fresh_key, fresh_value, w_out, out):
    rows = query.shape[0]
    group_tok = block.shape[0]
    kv_heads = fresh_key.shape[1] // HEAD
    per_head = query.shape[1] // HEAD // kv_heads
    heads = kv_heads * per_head
    position = lax.broadcasted_iota(jnp.int32, (rows, group_tok), 1)
    row = (place[0] ^ k) * rows + lax.broadcasted_iota(jnp.int32, (rows, group_tok), 0)
    segment = jnp.zeros((rows, group_tok), jnp.int32)
    end = jnp.int32(0)
    for p in range(prompts):
        end = end + place[3 + p]
        segment += (position >= end).astype(jnp.int32)
    allowed = jnp.where(segment == row // SAMPLES, 1.0, 0.0)
    allowed = jnp.concatenate([allowed] * heads, axis=0) > 0.5
    scale = 1.0 / math.sqrt(HEAD)
    scores, owns = [], []
    for kv in range(kv_heads):
        key = block[:, 2 * kv * HEAD : (2 * kv + 1) * HEAD]
        new_key = fresh_key[:, kv * HEAD : (kv + 1) * HEAD].astype(F32)
        first = kv * per_head * HEAD
        asked = [query[:, first + j * HEAD : first + (j + 1) * HEAD] for j in range(per_head)]
        scores.append(
            lax.dot_general(
                jnp.concatenate(asked, axis=0),
                key,
                (((1,), (1,)), ((), ())),
                preferred_element_type=F32,
            )
        )
        owns += [jnp.sum(q.astype(F32) * new_key, axis=1, keepdims=True) for q in asked]
    scores = jnp.where(allowed, jnp.concatenate(scores, axis=0) * scale, -1e30)
    own = jnp.concatenate(owns, axis=0) * scale
    top = jnp.maximum(jnp.max(scores, axis=1, keepdims=True), own)
    spread = jnp.where(allowed, jnp.exp(scores - top), 0.0)
    self_weight = jnp.exp(own - top)
    total = jnp.sum(spread, axis=1, keepdims=True) + self_weight
    probs = (spread / total).astype(BF16)
    self_prob = (self_weight / total).astype(BF16).astype(F32)
    mixed = []
    for kv in range(kv_heads):
        value = block[:, (2 * kv + 1) * HEAD : (2 * kv + 2) * HEAD]
        new_value = fresh_value[:, kv * HEAD : (kv + 1) * HEAD].astype(F32)
        lower = kv * per_head * rows
        summed = jnp.dot(
            probs[lower : lower + per_head * rows], value, preferred_element_type=F32
        )
        for j in range(per_head):
            at = slice(j * rows, (j + 1) * rows)
            own_part = self_prob[lower + j * rows : lower + (j + 1) * rows] * new_value
            mixed.append((summed[at] + own_part).astype(BF16))
    attention = jnp.concatenate(mixed, axis=1)
    out[...] = jnp.dot(attention, w_out[...], preferred_element_type=F32).astype(BF16)


def attend(k, prompts, place, block, query, fresh_key, fresh_value, w_out, rows):
    def cut(array):
        return pl.BlockSpec((rows, array.shape[1]), lambda i, place: (place[0] ^ k, 0))

    return pl.pallas_call(
        functools.partial(attend_kernel, k, prompts),
        out_shape=jax.ShapeDtypeStruct((rows, w_out.shape[1]), BF16),
        grid_spec=pltpu.PrefetchScalarGridSpec(
            num_scalar_prefetch=1,
            grid=(1,),
            in_specs=[WHOLE, cut(query), cut(fresh_key), cut(fresh_value), WHOLE],
            out_specs=pl.BlockSpec((rows, w_out.shape[1]), lambda i, place: (0, 0)),
        ),
        compiler_params=params(1, 8),
        cost_estimate=pl.CostEstimate(
            flops=4 * rows * w_out.shape[0] * w_out.shape[1],
            transcendentals=0,
            bytes_accessed=2 * w_out.size,
        ),
        name="attend",
    )(place, block, query, fresh_key, fresh_value, w_out)


def total_of(first, rest):
    value = first.astype(F32)
    for other in rest:
        value = value + other.astype(F32)
    return value


def on_device(
    tokens,
    routes,
    router,
    w_gate,
    w_up,
    w_down,
    norm_gain,
    w_kv,
    lengths,
    queries,
    new_keys,
    new_values,
    w_out,
):
    own = tokens[0]
    chosen = routes[0]
    local, model = own.shape
    top = chosen.shape[1]
    eps = lax.axis_size("ep")
    parts = lax.axis_size("half")
    half, ep, pool = lax.axis_index("half"), lax.axis_index("ep"), lax.axis_index("pool")
    width = model // parts

    prompt_lengths = lax.dynamic_index_in_dim(lengths, 1 - pool, 0, keepdims=False)[0]
    place = jnp.concatenate([jnp.stack([half, ep, pool]), prompt_lengths])

    narrow = w_kv.shape[1] // 2
    tags = jnp.pad(chosen.astype(BF16), ((0, 0), (0, LANES - top)))
    quarter = lax.dynamic_slice_in_dim(own, half * width, width, axis=1)
    parcel = jnp.concatenate([quarter, tags], axis=1)
    arrived = [shift(parcel, "ep", d) for d in range(1, eps)]
    near = jnp.concatenate([a[:, :width] for a in arrived], axis=0)
    all_tags = jnp.concatenate([tags] + [a[:, width:] for a in arrived], axis=0)
    order = sorted(range(1, parts), key=lambda k: bin(k).count("1"))
    far = order[::-1]
    others = {k: swap(near, "half", k) for k in order[:-1]}
    others[order[-1]] = swap(near, "half", order[-1])
    mine, near = lax.optimization_barrier(
        (lax.dynamic_slice_in_dim(w_kv, pool * narrow, narrow, axis=1), near)
    )
    others[0] = near
    origins = [0]
    for i in range(eps.bit_length() - 1):
        bit = eps >> i + 1
        mine = jnp.concatenate([mine, swap(mine, "ep", bit)], axis=0)
        origins += [origin ^ bit for origin in origins]

    totals = ()
    batches = [[0], order[:-1], order[-1:]]
    for quarters in batches:
        totals = expand(
            quarters,
            place,
            own,
            [others[k] for k in quarters],
            router.T,
            w_gate,
            w_up,
            totals,
            all_tags if quarters is batches[-1] else None,
            top,
        )
    hidden = totals
    partial = {}
    for k in far + [0]:
        partial[k] = reduce(k, place, hidden, w_down, width, width // 2)
    gathered = []
    for k in far:
        gathered.append(swap(partial[k], "half", k))
    mine, partial[0] = lax.optimization_barrier((mine, partial[0]))
    theirs = swap(mine, "pool", 1)
    summed = total_of(partial[0], gathered)
    returned = [
        shift(summed[d * local : (d + 1) * local].astype(BF16), "ep", -d) for d in range(1, eps)
    ]
    moe_quarter = total_of(summed[:local], returned).astype(BF16)
    moe = [moe_quarter] + [None] * (parts - 1)
    for k in order:
        moe[k] = swap(moe_quarter, "half", k)
    keyvals = project(place, own, moe, norm_gain[None], mine, theirs, origins)
    block = swap(keyvals, "pool", 1)

    rows = queries.shape[1] // parts
    decoded = {}
    for k in far + [0]:
        decoded[k] = attend(
            k,
            lengths.shape[2],
            place,
            block,
            queries[0],
            new_keys[0],
            new_values[0],
            w_out,
            rows,
        )
    sent = []
    for k in far:
        sent.append(swap(decoded[k], "half", k))
    return total_of(decoded[0], sent).astype(BF16)[None]


def solution(mesh):
    in_specs = (
        P("pool", "ep", None),
        P("pool", "ep", None),
        P(),
        P("ep", None, "half"),
        P("ep", None, "half"),
        P("ep", "half", None),
        P(),
        P("ep", "half"),
        P(None, "ep", None),
        P("pool", "ep", "half"),
        P("pool", "ep", "half"),
        P("pool", "ep", "half"),
        P("half", None),
    )
    out_specs = P("pool", ("ep", "half"), None)
    return jax.shard_map(
        on_device, mesh=mesh, in_specs=in_specs, out_specs=out_specs, check_vma=False
    )
```

```python
import functools
import math

import jax
import jax.numpy as jnp
from jax import lax
from jax.experimental import pallas as pl
from jax.experimental.pallas import tpu as pltpu
from jax.sharding import PartitionSpec as P


HEAD = 128
SAMPLES = 128
LANES = 128
F32 = jnp.float32
BF16 = jnp.bfloat16
WHOLE = pl.BlockSpec(memory_space=pltpu.VMEM)


def swap(shard, axis, bits):
    return lax.ppermute(shard, axis, [(i, i ^ bits) for i in range(lax.axis_size(axis))])


def shift(shard, axis, distance):
    count = lax.axis_size(axis)
    return lax.ppermute(shard, axis, [(i, (i + distance) % count) for i in range(count)])


def params(steps, mebibytes):
    return pltpu.CompilerParams(
        dimension_semantics=("arbitrary",) * steps, vmem_limit_bytes=mebibytes * 1024 * 1024
    )


def in_vmem(array):
    return pltpu.with_memory_space_constraint(array, pltpu.VMEM)


def in_hbm(array):
    return pltpu.with_memory_space_constraint(array, pltpu.HBM)


def columns_of(piece, width):
    return pl.ds(pl.multiple_of(piece * width, width), width)


def router_logits(rows, router, columns):
    return lax.dot_general(
        rows, router[:, columns], (((1,), (1,)), ((), ())), preferred_element_type=F32
    )


def take_rows(quarters, place, own, nears, router, rows):
    local = own.shape[0]
    width = nears[0].shape[1]
    logits = 0.0
    for i, (k, near) in enumerate(zip(quarters, nears)):
        columns = columns_of(place[0] ^ k, width)
        rows[:local, i * width : (i + 1) * width] = own[:, columns]
        rows[local:, i * width : (i + 1) * width] = near[...]
        logits += router_logits(rows[:, i * width : (i + 1) * width], router, columns)
    return logits


def both(rows, w_gates, w_ups, i):
    width = w_gates[0].shape[1]
    value = 0.0
    for j, (w_gate, w_up) in enumerate(zip(w_gates, w_ups)):
        weight = jnp.concatenate([w_gate[i], w_up[i]], axis=1)
        value += jnp.dot(
            rows[:, j * width : (j + 1) * width], weight, preferred_element_type=F32
        )
    return value


def with_weights(step, each, held, blocks, body):
    if not held[0]:
        body(*blocks, lambda i: i)
        return
    ready = held[0][0].shape[0] // each

    @pl.when(step < ready)
    def _():
        body(*held, lambda i: step * each + i)

    @pl.when(step >= ready)
    def _():
        body(*blocks, lambda i: i)


def split_refs(count, fetched, refs):
    groups = []
    for _ in range(3 + 2 * fetched):
        groups.append(refs[:count])
        refs = refs[count:]
    return groups[0], groups[1:3], groups[3:] if fetched else [(), ()], refs


def gather_kernel(quarters, fetched, first, place, own, router, *refs):
    nears, blocks, held, refs = split_refs(len(quarters), fetched, refs)
    totals, refs = ((None,) * 2, refs) if first else (refs[:2], refs[2:])
    out, logits_out, rows = refs
    step, each = pl.program_id(0), blocks[0][0].shape[0]

    @pl.when(step == 0)
    def _():
        logits = take_rows(quarters, place, own, nears, router, rows)
        logits_out[...] = logits if first else logits + totals[1][...]

    def body(w_gates, w_ups, at):
        for i in range(each):
            value = both(rows, w_gates, w_ups, at(i))
            out[step * each + i] = value if first else value + totals[0][step * each + i]

    with_weights(step, each, held, blocks, body)


def finish_kernel(quarters, fetched, top, place, own, router, *refs):
    nears, blocks, held, refs = split_refs(len(quarters), fetched, refs)
    total, logits_total, tags, hidden, rows, weights = refs
    step, (each, _, units) = pl.program_id(0), blocks[0][0].shape
    expert = lax.broadcasted_iota(jnp.int32, weights.shape, 1)

    @pl.when(step == 0)
    def _():
        logits = logits_total[...] + take_rows(quarters, place, own, nears, router, rows)
        named = tags[...].astype(F32).astype(jnp.int32)
        picked = named[:, 0:1] == expert
        for j in range(1, top):
            picked = jnp.logical_or(picked, named[:, j : j + 1] == expert)
        most = jnp.max(jnp.where(picked, logits, -1e30), axis=1, keepdims=True)
        spread = jnp.where(picked, jnp.exp(logits - most), 0.0)
        weights[...] = spread / jnp.sum(spread, axis=1, keepdims=True)

    def body(w_gates, w_ups, at):
        for i in range(each):
            value = total[step * each + i] + both(rows, w_gates, w_ups, at(i))
            gate, up = value[:, :units], value[:, units:]
            mine = expert == (place[1] * pl.num_programs(0) + step) * each + i
            scale = jnp.sum(jnp.where(mine, weights[...], 0.0), axis=1, keepdims=True)
            hidden[:, i * units : (i + 1) * units] = (
                gate / (1.0 + jnp.exp(-gate)) * up * scale
            ).astype(BF16)

    with_weights(step, each, held, blocks, body)


def fetch_kernel(quarters, place, w_gate, w_up, *refs):
    held, sems = refs[:-1], refs[-1]
    experts, width = held[0].shape[:2]
    copies = []
    for i, k in enumerate(quarters):
        rows = pl.ds(pl.multiple_of((place[0] ^ k) * width, width), width)
        for j, weight in enumerate((w_gate, w_up)):
            at = 2 * i + j
            source = weight.at[pl.ds(0, experts), rows, :]
            copies.append(pltpu.make_async_copy(source, held[at], sems.at[at]))
    for copy in copies:
        copy.start()
    for copy in copies:
        copy.wait()


def fetch(quarters, place, w_gate, w_up, width):
    experts, units = w_gate.shape[0] // 2, w_gate.shape[2]
    if experts == 0 or experts % 4:
        return {}
    count = 2 * len(quarters)
    held = pl.pallas_call(
        functools.partial(fetch_kernel, quarters),
        out_shape=[pltpu.VMEM((experts, width, units), BF16)] * count,
        grid_spec=pltpu.PrefetchScalarGridSpec(
            num_scalar_prefetch=1,
            grid=(),
            in_specs=[pl.BlockSpec(memory_space=pl.ANY)] * 2,
            out_specs=[WHOLE] * count,
            scratch_shapes=[pltpu.SemaphoreType.DMA((count,))],
        ),
        compiler_params=params(0, 2),
        name="fetch",
    )(place, in_hbm(w_gate), in_hbm(w_up))
    return {k: held[2 * i : 2 * i + 2] for i, k in enumerate(quarters)}


def expand(quarters, place, own, nears, router, w_gate, w_up, totals, tags, top, held):
    count = len(quarters)
    local, _ = own.shape
    tokens = local + nears[0].shape[0]
    experts, units = w_gate.shape[0], w_gate.shape[2]
    each = math.gcd(experts, 4 // count)
    width = nears[0].shape[1]
    last = tags is not None
    fetched = quarters[0] in held
    ready = held[quarters[0]][0].shape[0] // each if fetched else 0
    weight = [
        pl.BlockSpec(
            (each, width, units),
            lambda e, place, k=k: (jnp.maximum(e, ready) if fetched else e, place[0] ^ k, 0),
        )
        for k in quarters
    ]
    operands = [own, router] + [in_vmem(near) for near in nears]
    operands += [in_hbm(w_gate)] * count + [in_hbm(w_up)] * count
    if fetched:
        operands += [in_vmem(held[k][j]) for j in range(2) for k in quarters]
    operands += [in_vmem(t) for t in totals]
    scratch = [pltpu.VMEM((tokens, count * width), BF16)]
    if last:
        operands.append(tags)
        kernel = functools.partial(finish_kernel, quarters, fetched, top)
        scratch.append(pltpu.VMEM((tokens, router.shape[0]), F32))
        out_shape = pltpu.VMEM((tokens, experts * units), BF16)
        out_specs = pl.BlockSpec((tokens, each * units), lambda e, place: (0, e))
        aliases = {}
    else:
        kernel = functools.partial(gather_kernel, quarters, fetched, not totals)
        out_shape = [
            pltpu.VMEM((experts, tokens, 2 * units), F32),
            pltpu.VMEM((tokens, router.shape[0]), F32),
        ]
        out_specs = [WHOLE] * 2
        aliases = {3 + (3 + 2 * fetched) * count + i: i for i in range(len(totals))}
    return pl.pallas_call(
        kernel,
        out_shape=out_shape,
        grid_spec=pltpu.PrefetchScalarGridSpec(
            num_scalar_prefetch=1,
            grid=(experts // each,),
            in_specs=[WHOLE] * (2 + count)
            + weight * 2
            + [WHOLE] * (len(operands) - 2 - 3 * count),
            out_specs=out_specs,
            scratch_shapes=scratch,
        ),
        input_output_aliases=aliases,
        compiler_params=params(1, 24 if tokens <= 1024 else 40),
        cost_estimate=pl.CostEstimate(
            flops=4 * tokens * width * experts * units * count,
            transcendentals=0,
            bytes_accessed=4 * experts * width * units * count,
        ),
        name="expand",
    )(place, *operands)


def reduce_kernel(place, hidden, w_down, out):
    weight = w_down[...].reshape(-1, w_down.shape[2])
    out[...] = jnp.dot(hidden[...], weight, preferred_element_type=F32).astype(BF16)


def reduce(k, place, hidden, w_down, width, block):
    experts, units, _ = w_down.shape
    steps = width // block
    tokens = hidden.shape[0]
    return pl.pallas_call(
        reduce_kernel,
        out_shape=jax.ShapeDtypeStruct((tokens, width), BF16),
        grid_spec=pltpu.PrefetchScalarGridSpec(
            num_scalar_prefetch=1,
            grid=(steps,),
            in_specs=[
                WHOLE,
                pl.BlockSpec(
                    (experts, units, block),
                    lambda i, place: (0, 0, (place[0] ^ k) * steps + i),
                ),
            ],
            out_specs=pl.BlockSpec((tokens, block), lambda i, place: (0, i)),
        ),
        compiler_params=params(1, 16),
        cost_estimate=pl.CostEstimate(
            flops=2 * tokens * width * experts * units,
            transcendentals=0,
            bytes_accessed=2 * experts * width * units,
        ),
        name="reduce",
    )(place, in_vmem(hidden), in_hbm(w_down))


def project_kernel(parts, origins, place, own, *refs):
    moe, refs = refs[:parts], refs[parts:]
    gain, mine, theirs, out, mixed, normed = refs
    half, ep, pool = place[0], place[1], place[2]
    width = moe[0].shape[1]
    square = jnp.zeros((own.shape[0], 1), F32)
    for k in range(parts):
        columns = columns_of(half ^ k, width)
        value = own[:, columns].astype(F32) + moe[k][...].astype(F32)
        mixed[:, columns] = value
        square += jnp.sum(value * value, axis=1, keepdims=True)
    factor = lax.rsqrt(square / mixed.shape[1] + 1e-06)
    normed[...] = (mixed[...] * factor * gain[...]).astype(BF16)
    depth, narrow = mine.shape[0] // len(origins), mine.shape[1]
    for side, pieces in ((pool, mine), (1 - pool, theirs)):
        total = 0.0
        for i, origin in enumerate(origins):
            total += jnp.dot(
                normed[:, columns_of(ep ^ origin, depth)],
                pieces[i * depth : (i + 1) * depth, :],
                preferred_element_type=F32,
            )
        out[:, columns_of(side, narrow)] = total.astype(BF16)


def project(place, own, moe, gain, mine, theirs, origins):
    return pl.pallas_call(
        functools.partial(project_kernel, len(moe), origins),
        out_shape=jax.ShapeDtypeStruct((own.shape[0], 2 * mine.shape[1]), BF16),
        grid_spec=pltpu.PrefetchScalarGridSpec(
            num_scalar_prefetch=1,
            grid=(),
            in_specs=[WHOLE] * (len(moe) + 4),
            out_specs=WHOLE,
            scratch_shapes=[pltpu.VMEM(own.shape, F32), pltpu.VMEM(own.shape, BF16)],
        ),
        compiler_params=params(0, 12),
        name="project",
    )(place, own, *moe, gain, mine, theirs)


def attend_kernel(k, prompts, place, block, query, fresh_key, fresh_value, w_out, out):
    rows = query.shape[0]
    group_tok = block.shape[0]
    kv_heads = fresh_key.shape[1] // HEAD
    per_head = query.shape[1] // HEAD // kv_heads
    heads = kv_heads * per_head
    position = lax.broadcasted_iota(jnp.int32, (rows, group_tok), 1)
    row = (place[0] ^ k) * rows + lax.broadcasted_iota(jnp.int32, (rows, group_tok), 0)
    segment = jnp.zeros((rows, group_tok), jnp.int32)
    end = jnp.int32(0)
    for p in range(prompts):
        end = end + place[3 + p]
        segment += (position >= end).astype(jnp.int32)
    allowed = jnp.where(segment == row // SAMPLES, 1.0, 0.0)
    allowed = jnp.concatenate([allowed] * heads, axis=0) > 0.5
    scale = 1.0 / math.sqrt(HEAD)
    scores, owns = [], []
    for kv in range(kv_heads):
        key = block[:, 2 * kv * HEAD : (2 * kv + 1) * HEAD]
        new_key = fresh_key[:, kv * HEAD : (kv + 1) * HEAD].astype(F32)
        first = kv * per_head * HEAD
        asked = [query[:, first + j * HEAD : first + (j + 1) * HEAD] for j in range(per_head)]
        scores.append(
            lax.dot_general(
                jnp.concatenate(asked, axis=0),
                key,
                (((1,), (1,)), ((), ())),
                preferred_element_type=F32,
            )
        )
        owns += [jnp.sum(q.astype(F32) * new_key, axis=1, keepdims=True) for q in asked]
    scores = jnp.where(allowed, jnp.concatenate(scores, axis=0) * scale, -1e30)
    own = jnp.concatenate(owns, axis=0) * scale
    top = jnp.maximum(jnp.max(scores, axis=1, keepdims=True), own)
    spread = jnp.where(allowed, jnp.exp(scores - top), 0.0)
    self_weight = jnp.exp(own - top)
    total = jnp.sum(spread, axis=1, keepdims=True) + self_weight
    probs = (spread / total).astype(BF16)
    self_prob = (self_weight / total).astype(BF16).astype(F32)
    mixed = []
    for kv in range(kv_heads):
        value = block[:, (2 * kv + 1) * HEAD : (2 * kv + 2) * HEAD]
        new_value = fresh_value[:, kv * HEAD : (kv + 1) * HEAD].astype(F32)
        lower = kv * per_head * rows
        summed = jnp.dot(
            probs[lower : lower + per_head * rows], value, preferred_element_type=F32
        )
        for j in range(per_head):
            at = slice(j * rows, (j + 1) * rows)
            own_part = self_prob[lower + j * rows : lower + (j + 1) * rows] * new_value
            mixed.append((summed[at] + own_part).astype(BF16))
    attention = jnp.concatenate(mixed, axis=1)
    out[...] = jnp.dot(attention, w_out[...], preferred_element_type=F32).astype(BF16)


def attend(k, prompts, place, block, query, fresh_key, fresh_value, w_out, rows):
    def cut(array):
        return pl.BlockSpec((rows, array.shape[1]), lambda i, place: (place[0] ^ k, 0))

    return pl.pallas_call(
        functools.partial(attend_kernel, k, prompts),
        out_shape=jax.ShapeDtypeStruct((rows, w_out.shape[1]), BF16),
        grid_spec=pltpu.PrefetchScalarGridSpec(
            num_scalar_prefetch=1,
            grid=(1,),
            in_specs=[WHOLE, cut(query), cut(fresh_key), cut(fresh_value), WHOLE],
            out_specs=pl.BlockSpec((rows, w_out.shape[1]), lambda i, place: (0, 0)),
        ),
        compiler_params=params(1, 8),
        cost_estimate=pl.CostEstimate(
            flops=4 * rows * w_out.shape[0] * w_out.shape[1],
            transcendentals=0,
            bytes_accessed=2 * w_out.size,
        ),
        name="attend",
    )(place, block, query, fresh_key, fresh_value, w_out)


def total_of(first, rest):
    value = first.astype(F32)
    for other in rest:
        value = value + other.astype(F32)
    return value


def on_device(
    tokens,
    routes,
    router,
    w_gate,
    w_up,
    w_down,
    norm_gain,
    w_kv,
    lengths,
    queries,
    new_keys,
    new_values,
    w_out,
):
    own = tokens[0]
    chosen = routes[0]
    local, model = own.shape
    top = chosen.shape[1]
    eps = lax.axis_size("ep")
    parts = lax.axis_size("half")
    half, ep, pool = lax.axis_index("half"), lax.axis_index("ep"), lax.axis_index("pool")
    width = model // parts

    prompt_lengths = lax.dynamic_index_in_dim(lengths, 1 - pool, 0, keepdims=False)[0]
    place = jnp.concatenate([jnp.stack([half, ep, pool]), prompt_lengths])

    narrow = w_kv.shape[1] // 2
    tags = jnp.pad(chosen.astype(BF16), ((0, 0), (0, LANES - top)))
    quarter = lax.dynamic_slice_in_dim(own, half * width, width, axis=1)
    parcel = jnp.concatenate([quarter, tags], axis=1)
    order = sorted(range(1, parts), key=lambda k: bin(k).count("1"))
    arrived = [shift(parcel, "ep", d) for d in range(1, eps)]
    held = fetch([0] + order[:-1], place, w_gate, w_up, width)
    near = jnp.concatenate([a[:, :width] for a in arrived], axis=0)
    all_tags = jnp.concatenate([tags] + [a[:, width:] for a in arrived], axis=0)
    far = order[::-1]
    others = {k: swap(near, "half", k) for k in order[:-1]}
    others[order[-1]] = swap(near, "half", order[-1])
    mine, near = lax.optimization_barrier(
        (lax.dynamic_slice_in_dim(w_kv, pool * narrow, narrow, axis=1), near)
    )
    others[0] = near
    origins = [0]
    for i in range(eps.bit_length() - 1):
        bit = eps >> i + 1
        mine = jnp.concatenate([mine, swap(mine, "ep", bit)], axis=0)
        origins += [origin ^ bit for origin in origins]

    totals = ()
    batches = [[0], order[:-1], order[-1:]]
    for quarters in batches:
        totals = expand(
            quarters,
            place,
            own,
            [others[k] for k in quarters],
            router.T,
            w_gate,
            w_up,
            totals,
            all_tags if quarters is batches[-1] else None,
            top,
            held,
        )
    hidden = totals
    partial = {}
    for k in far + [0]:
        partial[k] = reduce(k, place, hidden, w_down, width, width // 2)
    gathered = []
    for k in far:
        gathered.append(swap(partial[k], "half", k))
    summed = total_of(partial[0], gathered)
    returned = [
        shift(summed[d * local : (d + 1) * local].astype(BF16), "ep", -d)
        for d in range(1, eps)
    ]
    mine, summed = lax.optimization_barrier((mine, summed))
    theirs = swap(mine, "pool", 1)
    moe_quarter = total_of(summed[:local], returned).astype(BF16)
    moe = [moe_quarter] + [None] * (parts - 1)
    for k in order:
        moe[k] = swap(moe_quarter, "half", k)
    keyvals = project(place, own, moe, norm_gain[None], mine, theirs, origins)
    block = swap(keyvals, "pool", 1)

    rows = queries.shape[1] // parts
    decoded = {}
    for k in far + [0]:
        decoded[k] = attend(
            k,
            lengths.shape[2],
            place,
            block,
            queries[0],
            new_keys[0],
            new_values[0],
            w_out,
            rows,
        )
    sent = []
    for k in far:
        sent.append(swap(decoded[k], "half", k))
    return total_of(decoded[0], sent).astype(BF16)[None]


def solution(mesh):
    in_specs = (
        P("pool", "ep", None),
        P("pool", "ep", None),
        P(),
        P("ep", None, "half"),
        P("ep", None, "half"),
        P("ep", "half", None),
        P(),
        P("ep", "half"),
        P(None, "ep", None),
        P("pool", "ep", "half"),
        P("pool", "ep", "half"),
        P("pool", "ep", "half"),
        P("half", None),
    )
    out_specs = P("pool", ("ep", "half"), None)
    return jax.shard_map(
        on_device, mesh=mesh, in_specs=in_specs, out_specs=out_specs, check_vma=False
    )
```

```python
import functools
import math

import jax
import jax.numpy as jnp
from jax import lax
from jax.experimental import pallas as pl
from jax.experimental.pallas import tpu as pltpu
from jax.sharding import PartitionSpec as P


HEAD = 128
SAMPLES = 128
LANES = 128
F32 = jnp.float32
BF16 = jnp.bfloat16
WHOLE = pl.BlockSpec(memory_space=pltpu.VMEM)


def swap(shard, axis, bits):
    return lax.ppermute(shard, axis, [(i, i ^ bits) for i in range(lax.axis_size(axis))])


def shift(shard, axis, distance):
    count = lax.axis_size(axis)
    return lax.ppermute(shard, axis, [(i, (i + distance) % count) for i in range(count)])


def params(steps, mebibytes):
    return pltpu.CompilerParams(
        dimension_semantics=("arbitrary",) * steps, vmem_limit_bytes=mebibytes * 1024 * 1024
    )


def in_vmem(array):
    return pltpu.with_memory_space_constraint(array, pltpu.VMEM)


def in_hbm(array):
    return pltpu.with_memory_space_constraint(array, pltpu.HBM)


def columns_of(piece, width):
    return pl.ds(pl.multiple_of(piece * width, width), width)


def router_logits(rows, router, columns):
    return lax.dot_general(
        rows, router[:, columns], (((1,), (1,)), ((), ())), preferred_element_type=F32
    )


def take_rows(quarters, place, own, nears, router, rows):
    local = own.shape[0]
    width = nears[0].shape[1]
    logits = 0.0
    for i, (k, near) in enumerate(zip(quarters, nears)):
        columns = columns_of(place[0] ^ k, width)
        rows[:local, i * width : (i + 1) * width] = own[:, columns]
        rows[local:, i * width : (i + 1) * width] = near[...]
        logits += router_logits(rows[:, i * width : (i + 1) * width], router, columns)
    return logits


def both(rows, w_gates, w_ups, i):
    weight = jnp.concatenate(
        [
            jnp.concatenate([w_gate[i], w_up[i]], axis=1)
            for w_gate, w_up in zip(w_gates, w_ups)
        ],
        axis=0,
    )
    return jnp.dot(rows[...], weight, preferred_element_type=F32)


def with_weights(step, each, held, blocks, body):
    if not held[0]:
        body(*blocks, lambda i: i)
        return
    ready = held[0][0].shape[0] // each

    @pl.when(step < ready)
    def _():
        body(*held, lambda i: step * each + i)

    @pl.when(step >= ready)
    def _():
        body(*blocks, lambda i: i)


def split_refs(count, fetched, refs):
    groups = []
    for _ in range(3 + 2 * fetched):
        groups.append(refs[:count])
        refs = refs[count:]
    return groups[0], groups[1:3], groups[3:] if fetched else [(), ()], refs


def gather_kernel(quarters, fetched, first, place, own, router, *refs):
    nears, blocks, held, refs = split_refs(len(quarters), fetched, refs)
    totals, refs = ((None,) * 2, refs) if first else (refs[:2], refs[2:])
    out, logits_out, rows = refs
    step, each = pl.program_id(0), blocks[0][0].shape[0]

    @pl.when(step == 0)
    def _():
        logits = take_rows(quarters, place, own, nears, router, rows)
        logits_out[...] = logits if first else logits + totals[1][...]

    def body(w_gates, w_ups, at):
        for i in range(each):
            value = both(rows, w_gates, w_ups, at(i))
            out[step * each + i] = value if first else value + totals[0][step * each + i]

    with_weights(step, each, held, blocks, body)


def finish_kernel(quarters, fetched, top, place, own, router, *refs):
    nears, blocks, held, refs = split_refs(len(quarters), fetched, refs)
    total, logits_total, tags, w_down, hidden, ahead, rows, weights, sem = refs
    step, (each, _, units) = pl.program_id(0), blocks[0][0].shape
    coming = pltpu.make_async_copy(
        w_down.at[:, :, columns_of(place[0] ^ quarters[-1], ahead.shape[2])], ahead, sem
    )
    expert = lax.broadcasted_iota(jnp.int32, weights.shape, 1)

    @pl.when(step == 0)
    def _():
        coming.start()
        logits = logits_total[...] + take_rows(quarters, place, own, nears, router, rows)
        named = tags[...].astype(F32).astype(jnp.int32)
        picked = named[:, 0:1] == expert
        for j in range(1, top):
            picked = jnp.logical_or(picked, named[:, j : j + 1] == expert)
        most = jnp.max(jnp.where(picked, logits, -1e30), axis=1, keepdims=True)
        spread = jnp.where(picked, jnp.exp(logits - most), 0.0)
        weights[...] = spread / jnp.sum(spread, axis=1, keepdims=True)

    def body(w_gates, w_ups, at):
        for i in range(each):
            value = total[step * each + i] + both(rows, w_gates, w_ups, at(i))
            gate, up = value[:, :units], value[:, units:]
            mine = expert == (place[1] * pl.num_programs(0) + step) * each + i
            scale = jnp.sum(jnp.where(mine, weights[...], 0.0), axis=1, keepdims=True)
            hidden[:, i * units : (i + 1) * units] = (
                gate / (1.0 + jnp.exp(-gate)) * up * scale
            ).astype(BF16)

    with_weights(step, each, held, blocks, body)

    @pl.when(step == pl.num_programs(0) - 1)
    def _():
        coming.wait()


def fetch_kernel(quarters, place, w_gate, w_up, *refs):
    held, sems = refs[:-1], refs[-1]
    experts, width = held[0].shape[:2]
    copies = []
    for i, k in enumerate(quarters):
        rows = pl.ds(pl.multiple_of((place[0] ^ k) * width, width), width)
        for j, weight in enumerate((w_gate, w_up)):
            at = 2 * i + j
            source = weight.at[pl.ds(0, experts), rows, :]
            copies.append(pltpu.make_async_copy(source, held[at], sems.at[at]))
    for copy in copies:
        copy.start()
    for copy in copies:
        copy.wait()


def fetch(quarters, place, w_gate, w_up, width):
    experts, units = w_gate.shape[0] // 2, w_gate.shape[2]
    if experts == 0 or experts % 4:
        return {}
    count = 2 * len(quarters)
    held = pl.pallas_call(
        functools.partial(fetch_kernel, quarters),
        out_shape=[pltpu.VMEM((experts, width, units), BF16)] * count,
        grid_spec=pltpu.PrefetchScalarGridSpec(
            num_scalar_prefetch=1,
            grid=(),
            in_specs=[pl.BlockSpec(memory_space=pl.ANY)] * 2,
            out_specs=[WHOLE] * count,
            scratch_shapes=[pltpu.SemaphoreType.DMA((count,))],
        ),
        compiler_params=params(0, 2),
        name="fetch",
    )(place, in_hbm(w_gate), in_hbm(w_up))
    return {k: held[2 * i : 2 * i + 2] for i, k in enumerate(quarters)}


def expand(quarters, place, own, nears, router, w_gate, w_up, totals, tags, top, held, w_down):
    count = len(quarters)
    local, _ = own.shape
    tokens = local + nears[0].shape[0]
    experts, units = w_gate.shape[0], w_gate.shape[2]
    each = math.gcd(experts, 4 // count)
    width = nears[0].shape[1]
    last = tags is not None
    fetched = quarters[0] in held
    ready = held[quarters[0]][0].shape[0] // each if fetched else 0
    weight = [
        pl.BlockSpec(
            (each, width, units),
            lambda e, place, k=k: (jnp.maximum(e, ready) if fetched else e, place[0] ^ k, 0),
        )
        for k in quarters
    ]
    operands = [own, router] + [in_vmem(near) for near in nears]
    operands += [in_hbm(w_gate)] * count + [in_hbm(w_up)] * count
    if fetched:
        operands += [in_vmem(held[k][j]) for j in range(2) for k in quarters]
    operands += [in_vmem(t) for t in totals]
    scratch = [pltpu.VMEM((tokens, count * width), BF16)]
    if last:
        operands += [tags, in_hbm(w_down)]
        kernel = functools.partial(finish_kernel, quarters, fetched, top)
        scratch += [pltpu.VMEM((tokens, router.shape[0]), F32), pltpu.SemaphoreType.DMA(())]
        out_shape = [
            pltpu.VMEM((tokens, experts * units), BF16),
            pltpu.VMEM((experts, units, width), BF16),
        ]
        out_specs = [pl.BlockSpec((tokens, each * units), lambda e, place: (0, e)), WHOLE]
        aliases = {}
    else:
        kernel = functools.partial(gather_kernel, quarters, fetched, not totals)
        out_shape = [
            pltpu.VMEM((experts, tokens, 2 * units), F32),
            pltpu.VMEM((tokens, router.shape[0]), F32),
        ]
        out_specs = [WHOLE] * 2
        aliases = {3 + (3 + 2 * fetched) * count + i: i for i in range(len(totals))}
    return pl.pallas_call(
        kernel,
        out_shape=out_shape,
        grid_spec=pltpu.PrefetchScalarGridSpec(
            num_scalar_prefetch=1,
            grid=(experts // each,),
            in_specs=[WHOLE] * (2 + count)
            + weight * 2
            + [WHOLE] * (len(operands) - 2 - 3 * count - last)
            + [pl.BlockSpec(memory_space=pl.ANY)] * last,
            out_specs=out_specs,
            scratch_shapes=scratch,
        ),
        input_output_aliases=aliases,
        compiler_params=params(1, 24 if tokens <= 1024 else 40),
        cost_estimate=pl.CostEstimate(
            flops=4 * tokens * width * experts * units * count,
            transcendentals=0,
            bytes_accessed=4 * experts * width * units * count,
        ),
        name="expand",
    )(place, *operands)


def reduce_kernel(place, hidden, w_down, out):
    weight = w_down[...].reshape(-1, w_down.shape[2])
    out[...] = jnp.dot(hidden[...], weight, preferred_element_type=F32).astype(BF16)


def reduce_ahead_kernel(hidden, weight, out):
    block = weight.shape[2] // 2
    for i in range(2):
        columns = slice(i * block, (i + 1) * block)
        piece = weight[:, :, columns].reshape(-1, block)
        out[:, columns] = jnp.dot(hidden[...], piece, preferred_element_type=F32).astype(BF16)


def reduce_ahead(hidden, weight):
    return pl.pallas_call(
        reduce_ahead_kernel,
        out_shape=jax.ShapeDtypeStruct((hidden.shape[0], weight.shape[2]), BF16),
        in_specs=[WHOLE] * 2,
        out_specs=WHOLE,
        compiler_params=params(0, 12),
        name="reduce",
    )(in_vmem(hidden), in_vmem(weight))


def reduce(k, place, hidden, w_down, width, block):
    experts, units, _ = w_down.shape
    steps = width // block
    tokens = hidden.shape[0]
    return pl.pallas_call(
        reduce_kernel,
        out_shape=jax.ShapeDtypeStruct((tokens, width), BF16),
        grid_spec=pltpu.PrefetchScalarGridSpec(
            num_scalar_prefetch=1,
            grid=(steps,),
            in_specs=[
                WHOLE,
                pl.BlockSpec(
                    (experts, units, block),
                    lambda i, place: (0, 0, (place[0] ^ k) * steps + i),
                ),
            ],
            out_specs=pl.BlockSpec((tokens, block), lambda i, place: (0, i)),
        ),
        compiler_params=params(1, 16),
        cost_estimate=pl.CostEstimate(
            flops=2 * tokens * width * experts * units,
            transcendentals=0,
            bytes_accessed=2 * experts * width * units,
        ),
        name="reduce",
    )(place, in_vmem(hidden), in_hbm(w_down))


def project_kernel(parts, origins, place, own, *refs):
    moe, refs = refs[:parts], refs[parts:]
    gain, mine, theirs, out, mixed, normed = refs
    half, ep, pool = place[0], place[1], place[2]
    width = moe[0].shape[1]
    square = jnp.zeros((own.shape[0], 1), F32)
    for k in range(parts):
        columns = columns_of(half ^ k, width)
        value = own[:, columns].astype(F32) + moe[k][...].astype(F32)
        mixed[:, columns] = value
        square += jnp.sum(value * value, axis=1, keepdims=True)
    factor = lax.rsqrt(square / mixed.shape[1] + 1e-06)
    normed[...] = (mixed[...] * factor * gain[...]).astype(BF16)
    depth, narrow = mine.shape[0] // len(origins), mine.shape[1]
    for side, pieces in ((pool, mine), (1 - pool, theirs)):
        total = 0.0
        for i, origin in enumerate(origins):
            total += jnp.dot(
                normed[:, columns_of(ep ^ origin, depth)],
                pieces[i * depth : (i + 1) * depth, :],
                preferred_element_type=F32,
            )
        out[:, columns_of(side, narrow)] = total.astype(BF16)


def project(place, own, moe, gain, mine, theirs, origins):
    return pl.pallas_call(
        functools.partial(project_kernel, len(moe), origins),
        out_shape=jax.ShapeDtypeStruct((own.shape[0], 2 * mine.shape[1]), BF16),
        grid_spec=pltpu.PrefetchScalarGridSpec(
            num_scalar_prefetch=1,
            grid=(),
            in_specs=[WHOLE] * (len(moe) + 4),
            out_specs=WHOLE,
            scratch_shapes=[pltpu.VMEM(own.shape, F32), pltpu.VMEM(own.shape, BF16)],
        ),
        compiler_params=params(0, 12),
        name="project",
    )(place, own, *moe, gain, mine, theirs)


def attend_kernel(k, prompts, place, block, query, fresh_key, fresh_value, w_out, out):
    rows = query.shape[0]
    group_tok = block.shape[0]
    kv_heads = fresh_key.shape[1] // HEAD
    per_head = query.shape[1] // HEAD // kv_heads
    heads = kv_heads * per_head
    position = lax.broadcasted_iota(jnp.int32, (rows, group_tok), 1)
    row = (place[0] ^ k) * rows + lax.broadcasted_iota(jnp.int32, (rows, group_tok), 0)
    segment = jnp.zeros((rows, group_tok), jnp.int32)
    end = jnp.int32(0)
    for p in range(prompts):
        end = end + place[3 + p]
        segment += (position >= end).astype(jnp.int32)
    allowed = jnp.where(segment == row // SAMPLES, 1.0, 0.0)
    allowed = jnp.concatenate([allowed] * heads, axis=0) > 0.5
    scale = 1.0 / math.sqrt(HEAD)
    scores, owns = [], []
    for kv in range(kv_heads):
        key = block[:, 2 * kv * HEAD : (2 * kv + 1) * HEAD]
        new_key = fresh_key[:, kv * HEAD : (kv + 1) * HEAD].astype(F32)
        first = kv * per_head * HEAD
        asked = [query[:, first + j * HEAD : first + (j + 1) * HEAD] for j in range(per_head)]
        scores.append(
            lax.dot_general(
                jnp.concatenate(asked, axis=0),
                key,
                (((1,), (1,)), ((), ())),
                preferred_element_type=F32,
            )
        )
        owns += [jnp.sum(q.astype(F32) * new_key, axis=1, keepdims=True) for q in asked]
    scores = jnp.where(allowed, jnp.concatenate(scores, axis=0) * scale, -1e30)
    own = jnp.concatenate(owns, axis=0) * scale
    top = jnp.maximum(jnp.max(scores, axis=1, keepdims=True), own)
    spread = jnp.where(allowed, jnp.exp(scores - top), 0.0)
    self_weight = jnp.exp(own - top)
    total = jnp.sum(spread, axis=1, keepdims=True) + self_weight
    probs = (spread / total).astype(BF16)
    self_prob = (self_weight / total).astype(BF16).astype(F32)
    mixed = []
    for kv in range(kv_heads):
        value = block[:, (2 * kv + 1) * HEAD : (2 * kv + 2) * HEAD]
        new_value = fresh_value[:, kv * HEAD : (kv + 1) * HEAD].astype(F32)
        lower = kv * per_head * rows
        summed = jnp.dot(
            probs[lower : lower + per_head * rows], value, preferred_element_type=F32
        )
        for j in range(per_head):
            at = slice(j * rows, (j + 1) * rows)
            own_part = self_prob[lower + j * rows : lower + (j + 1) * rows] * new_value
            mixed.append((summed[at] + own_part).astype(BF16))
    attention = jnp.concatenate(mixed, axis=1)
    out[...] = jnp.dot(attention, w_out[...], preferred_element_type=F32).astype(BF16)


def attend(k, prompts, place, block, query, fresh_key, fresh_value, w_out, rows):
    def cut(array):
        return pl.BlockSpec((rows, array.shape[1]), lambda i, place: (place[0] ^ k, 0))

    return pl.pallas_call(
        functools.partial(attend_kernel, k, prompts),
        out_shape=jax.ShapeDtypeStruct((rows, w_out.shape[1]), BF16),
        grid_spec=pltpu.PrefetchScalarGridSpec(
            num_scalar_prefetch=1,
            grid=(1,),
            in_specs=[WHOLE, cut(query), cut(fresh_key), cut(fresh_value), WHOLE],
            out_specs=pl.BlockSpec((rows, w_out.shape[1]), lambda i, place: (0, 0)),
        ),
        compiler_params=params(1, 8),
        cost_estimate=pl.CostEstimate(
            flops=4 * rows * w_out.shape[0] * w_out.shape[1],
            transcendentals=0,
            bytes_accessed=2 * w_out.size,
        ),
        name="attend",
    )(place, block, query, fresh_key, fresh_value, w_out)


def total_of(first, rest):
    value = first.astype(F32)
    for other in rest:
        value = value + other.astype(F32)
    return value


def on_device(
    tokens,
    routes,
    router,
    w_gate,
    w_up,
    w_down,
    norm_gain,
    w_kv,
    lengths,
    queries,
    new_keys,
    new_values,
    w_out,
):
    own = tokens[0]
    chosen = routes[0]
    local, model = own.shape
    top = chosen.shape[1]
    eps = lax.axis_size("ep")
    parts = lax.axis_size("half")
    half, ep, pool = lax.axis_index("half"), lax.axis_index("ep"), lax.axis_index("pool")
    width = model // parts

    prompt_lengths = lax.dynamic_index_in_dim(lengths, 1 - pool, 0, keepdims=False)[0]
    place = jnp.concatenate([jnp.stack([half, ep, pool]), prompt_lengths])

    narrow = w_kv.shape[1] // 2
    tags = jnp.pad(chosen.astype(BF16), ((0, 0), (0, LANES - top)))
    quarter = lax.dynamic_slice_in_dim(own, half * width, width, axis=1)
    parcel = jnp.concatenate([quarter, tags], axis=1)
    order = sorted(range(1, parts), key=lambda k: bin(k).count("1"))
    arrived = [shift(parcel, "ep", d) for d in range(1, eps)]
    held = fetch([0] + order[:-1], place, w_gate, w_up, width)
    near = jnp.concatenate([a[:, :width] for a in arrived], axis=0)
    all_tags = jnp.concatenate([tags] + [a[:, width:] for a in arrived], axis=0)
    far = order[::-1]
    others = {k: swap(near, "half", k) for k in order[:-1]}
    others[order[-1]] = swap(near, "half", order[-1])
    mine, near = lax.optimization_barrier(
        (lax.dynamic_slice_in_dim(w_kv, pool * narrow, narrow, axis=1), near)
    )
    others[0] = near
    origins = [0]
    for i in range(eps.bit_length() - 1):
        bit = eps >> i + 1
        mine = jnp.concatenate([mine, swap(mine, "ep", bit)], axis=0)
        origins += [origin ^ bit for origin in origins]

    totals = ()
    batches = [[0], order[:-1], order[-1:]]
    for quarters in batches:
        totals = expand(
            quarters,
            place,
            own,
            [others[k] for k in quarters],
            router.T,
            w_gate,
            w_up,
            totals,
            all_tags if quarters is batches[-1] else None,
            top,
            held,
            w_down,
        )
    hidden, ahead = totals
    partial = {}
    for k in far + [0]:
        if k == order[-1]:
            partial[k] = reduce_ahead(hidden, ahead)
        else:
            partial[k] = reduce(k, place, hidden, w_down, width, width // 2)
    gathered = []
    for k in far:
        gathered.append(swap(partial[k], "half", k))
    summed = total_of(partial[0], gathered)
    returned = [
        shift(summed[d * local : (d + 1) * local].astype(BF16), "ep", -d)
        for d in range(1, eps)
    ]
    mine, summed = lax.optimization_barrier((mine, summed))
    theirs = swap(mine, "pool", 1)
    moe_quarter = total_of(summed[:local], returned).astype(BF16)
    moe = [moe_quarter] + [None] * (parts - 1)
    for k in order:
        moe[k] = swap(moe_quarter, "half", k)
    keyvals = project(place, own, moe, norm_gain[None], mine, theirs, origins)
    block = swap(keyvals, "pool", 1)

    rows = queries.shape[1] // parts
    decoded = {}
    for k in far + [0]:
        decoded[k] = attend(
            k,
            lengths.shape[2],
            place,
            block,
            queries[0],
            new_keys[0],
            new_values[0],
            w_out,
            rows,
        )
    sent = []
    for k in far:
        sent.append(swap(decoded[k], "half", k))
    return total_of(decoded[0], sent).astype(BF16)[None]


def solution(mesh):
    in_specs = (
        P("pool", "ep", None),
        P("pool", "ep", None),
        P(),
        P("ep", None, "half"),
        P("ep", None, "half"),
        P("ep", "half", None),
        P(),
        P("ep", "half"),
        P(None, "ep", None),
        P("pool", "ep", "half"),
        P("pool", "ep", "half"),
        P("pool", "ep", "half"),
        P("half", None),
    )
    out_specs = P("pool", ("ep", "half"), None)
    return jax.shard_map(
        on_device, mesh=mesh, in_specs=in_specs, out_specs=out_specs, check_vma=False
    )
```

```python
import functools
import math

import jax
import jax.numpy as jnp
from jax import lax
from jax.experimental import pallas as pl
from jax.experimental.pallas import tpu as pltpu
from jax.sharding import PartitionSpec as P


HEAD = 128
SAMPLES = 128
LANES = 128
F32 = jnp.float32
BF16 = jnp.bfloat16
WHOLE = pl.BlockSpec(memory_space=pltpu.VMEM)


def swap(shard, axis, bits):
    return lax.ppermute(shard, axis, [(i, i ^ bits) for i in range(lax.axis_size(axis))])


def shift(shard, axis, distance):
    count = lax.axis_size(axis)
    return lax.ppermute(shard, axis, [(i, (i + distance) % count) for i in range(count)])


def params(steps, mebibytes):
    return pltpu.CompilerParams(
        dimension_semantics=("arbitrary",) * steps, vmem_limit_bytes=mebibytes * 1024 * 1024
    )


def in_vmem(array):
    return pltpu.with_memory_space_constraint(array, pltpu.VMEM)


def in_hbm(array):
    return pltpu.with_memory_space_constraint(array, pltpu.HBM)


def columns_of(piece, width):
    return pl.ds(pl.multiple_of(piece * width, width), width)


def router_logits(rows, router, columns):
    return lax.dot_general(
        rows, router[:, columns], (((1,), (1,)), ((), ())), preferred_element_type=F32
    )


def take_rows(quarters, place, own, nears, router, rows):
    local = own.shape[0]
    width = nears[0].shape[1]
    logits = 0.0
    for i, (k, near) in enumerate(zip(quarters, nears)):
        columns = columns_of(place[0] ^ k, width)
        rows[:local, i * width : (i + 1) * width] = own[:, columns]
        rows[local:, i * width : (i + 1) * width] = near[...]
        logits += router_logits(rows[:, i * width : (i + 1) * width], router, columns)
    return logits


PAIR, DOWN = 0, 2


def pair_copies(place, sources, k, low, high, out, sems):
    rows, count = columns_of(place[0] ^ k, out.shape[1]), high - low
    return [
        pltpu.make_async_copy(
            sources[j].at[pl.ds(low, count), rows, :], out.at[pl.ds(j * count, count)], sems.at[j]
        )
        for j in range(2)
    ]


def expert_copies(place, sources, k, low, e, out, sems):
    rows, count = columns_of(place[0] ^ k, out.shape[1]), out.shape[0] // 2
    return [
        pltpu.make_async_copy(
            sources[j].at[e, rows, :], out.at[j * count + e - low], sems.at[j, e - low]
        )
        for j in range(2)
    ]


def unpack_kernel(tags, *refs):
    *arrived, near, all_tags = refs
    local, width = tags.shape[0], near.shape[1]
    all_tags[:local, :] = tags[...]
    for d, parcel in enumerate(arrived):
        near[d * local : (d + 1) * local, :] = parcel[:, :width]
        all_tags[(d + 1) * local : (d + 2) * local, :] = parcel[:, width:]


def unpack(tags, arrived, width):
    local, extra = tags.shape
    count = len(arrived)
    return pl.pallas_call(
        unpack_kernel,
        out_shape=[
            jax.ShapeDtypeStruct((count * local, width), BF16),
            jax.ShapeDtypeStruct(((count + 1) * local, extra), BF16),
        ],
        in_specs=[WHOLE] * (1 + count),
        out_specs=[WHOLE] * 2,
        compiler_params=params(0, 4 if count < 8 else 32),
        name="unpack",
    )(tags, *arrived)


def stage_kernel(items, quarters, parts, first, top, place, *refs):
    refs = list(refs)

    def take(count):
        taken = refs[:count]
        del refs[:count]
        return taken

    sources, count = take(3), len(quarters)
    streams = [part for part in parts if part[3]]
    if count:
        (own, router), nears = take(2), take(count)
        held = take(len(parts) - len(streams))
        totals = [None, None] if first else take(2)
        tags = take(1)[0] if top else None
    ahead = take(len(items))
    out = take(1)[0] if count else None
    logits_out = take(1)[0] if count and not top else None
    ahead_sems = take(1)[0]
    rows = take(1)[0] if count else None
    weights = take(1)[0] if top else None
    buffers, buffer_sems = take(len(streams)), take(len(streams))

    for (k, low, high, _), buffer, sems in zip(streams, buffers, buffer_sems):
        for e in range(low, high):
            for copy in expert_copies(place, sources, k, low, e, buffer, sems):
                copy.start()
    copies = []
    for n, item in enumerate(items):
        if item[0] == PAIR:
            copies += pair_copies(place, sources, *item[1:], ahead[n], ahead_sems.at[n])
        else:
            columns = columns_of(place[0] ^ item[1], ahead[n].shape[2])
            copies.append(
                pltpu.make_async_copy(
                    sources[DOWN].at[:, :, columns], ahead[n], ahead_sems.at[n, 0]
                )
            )
    if not streams:
        for copy in copies:
            copy.start()
    if count:
        logits = take_rows(quarters, place, own, nears, router, rows)
        if not first:
            logits += totals[1][...]
        if top:
            expert = lax.broadcasted_iota(jnp.int32, logits.shape, 1)
            named = tags[...].astype(F32).astype(jnp.int32)
            picked = named[:, 0:1] == expert
            for j in range(1, top):
                picked = jnp.logical_or(picked, named[:, j : j + 1] == expert)
            most = jnp.max(jnp.where(picked, logits, -1e30), axis=1, keepdims=True)
            spread = jnp.where(picked, jnp.exp(logits - most), 0.0)
            weights[...] = spread / jnp.sum(spread, axis=1, keepdims=True)
        else:
            logits_out[...] = logits
        experts, (_, _, units) = sources[0].shape[0], sources[0].shape
        width = nears[0].shape[1]
        held, buffers, buffer_sems = list(held), list(buffers), list(buffer_sems)
        for n, (k, low, high, streamed) in enumerate(parts):
            weight = buffers.pop(0) if streamed else held.pop(0)
            sems = buffer_sems.pop(0) if streamed else None
            at = quarters.index(k) * width
            begun = any(k != part[0] for part in parts[:n])

            def body(e, carry, k=k, low=low, weight=weight, sems=sems, at=at, begun=begun):
                if sems is not None:
                    for copy in expert_copies(place, sources, k, low, e, weight, sems):
                        copy.wait()
                half = weight.shape[0] // 2
                both = jnp.concatenate([weight[e - low], weight[half + e - low]], axis=1)
                value = jnp.dot(rows[:, at : at + width], both, preferred_element_type=F32)
                if begun:
                    value += out[e]
                elif not first:
                    value += totals[0][e]
                if not top:
                    out[e] = value
                    return carry
                gate, up = value[:, :units], value[:, units:]
                mine = expert == place[1] * experts + e
                scale = jnp.sum(jnp.where(mine, weights[...], 0.0), axis=1, keepdims=True)
                out[:, columns_of(e, units)] = (
                    gate / (1.0 + jnp.exp(-gate)) * up * scale
                ).astype(BF16)
                return carry

            lax.fori_loop(low, high, body, 0)
            if streams and n == 0:
                for copy in copies:
                    copy.start()
    for copy in copies:
        copy.wait()


def stage(place, sources, items, own=None, router=None, nears=None, parts=(), held=(),
          totals=(), tags=None, top=0):
    experts, model, units = sources[0].shape
    nears = nears or {}
    quarters = list(nears)
    width = model // lax.axis_size("half")
    count = len(quarters)
    operands = [in_hbm(array) for array in sources]
    shapes = [
        pltpu.VMEM((2 * (item[3] - item[2]), width, units), BF16)
        if item[0] == PAIR
        else pltpu.VMEM((experts, units, width), BF16)
        for item in items
    ]
    scratch, aliases, tokens = [pltpu.SemaphoreType.DMA((max(1, len(items)), 2))], {}, 0
    streams = [part for part in parts if part[3]]
    mebibytes = 1
    if count:
        tokens = own.shape[0] + nears[quarters[0]].shape[0]
        mebibytes = 4 + -(-sum(4 * width * units * (p[2] - p[1]) for p in streams) >> 20)
        operands += [own, router] + [in_vmem(nears[k]) for k in quarters]
        operands += [in_vmem(array) for array in held]
        aliases = {1 + len(operands) + i: len(items) + i for i in range(len(totals))}
        operands += [in_vmem(total) for total in totals]
        scratch.append(pltpu.VMEM((tokens, count * width), BF16))
        if top:
            operands.append(tags)
            aliases = {}
            scratch.append(pltpu.VMEM((tokens, router.shape[0]), F32))
            shapes.append(pltpu.VMEM((tokens, experts * units), BF16))
        else:
            shapes.append(pltpu.VMEM((experts, tokens, 2 * units), F32))
            shapes.append(pltpu.VMEM((tokens, router.shape[0]), F32))
    scratch += [pltpu.VMEM((2 * (p[2] - p[1]), width, units), BF16) for p in streams]
    scratch += [pltpu.SemaphoreType.DMA((2, p[2] - p[1])) for p in streams]
    outs = pl.pallas_call(
        functools.partial(stage_kernel, items, quarters, parts, not totals, top),
        out_shape=shapes,
        grid_spec=pltpu.PrefetchScalarGridSpec(
            num_scalar_prefetch=1,
            grid=(),
            in_specs=[pl.BlockSpec(memory_space=pl.ANY)] * 3 + [WHOLE] * (len(operands) - 3),
            out_specs=[WHOLE] * len(shapes),
            scratch_shapes=scratch,
        ),
        input_output_aliases=aliases,
        compiler_params=params(0, mebibytes if tokens <= 1024 else 32),
    )(place, *operands)
    return outs[: len(items)], outs[len(items) :]


def reduce_kernel(place, hidden, w_down, out):
    weight = w_down[...].reshape(-1, w_down.shape[2])
    out[...] = jnp.dot(hidden[...], weight, preferred_element_type=F32).astype(BF16)


def reduce_ahead_kernel(hidden, weight, out):
    block = weight.shape[2] // 2
    for i in range(2):
        columns = slice(i * block, (i + 1) * block)
        piece = weight[:, :, columns].reshape(-1, block)
        out[:, columns] = jnp.dot(hidden[...], piece, preferred_element_type=F32).astype(BF16)


def reduce_ahead(hidden, weight):
    return pl.pallas_call(
        reduce_ahead_kernel,
        out_shape=jax.ShapeDtypeStruct((hidden.shape[0], weight.shape[2]), BF16),
        in_specs=[WHOLE] * 2,
        out_specs=WHOLE,
        compiler_params=params(0, 12),
        name="reduce",
    )(in_vmem(hidden), in_vmem(weight))


def reduce(k, place, hidden, w_down, width, block):
    experts, units, _ = w_down.shape
    steps = width // block
    tokens = hidden.shape[0]
    return pl.pallas_call(
        reduce_kernel,
        out_shape=jax.ShapeDtypeStruct((tokens, width), BF16),
        grid_spec=pltpu.PrefetchScalarGridSpec(
            num_scalar_prefetch=1,
            grid=(steps,),
            in_specs=[
                WHOLE,
                pl.BlockSpec(
                    (experts, units, block),
                    lambda i, place: (0, 0, (place[0] ^ k) * steps + i),
                ),
            ],
            out_specs=pl.BlockSpec((tokens, block), lambda i, place: (0, i)),
        ),
        compiler_params=params(1, 16),
        cost_estimate=pl.CostEstimate(
            flops=2 * tokens * width * experts * units,
            transcendentals=0,
            bytes_accessed=2 * experts * width * units,
        ),
        name="reduce",
    )(place, in_vmem(hidden), in_hbm(w_down))


def project_kernel(parts, origins, place, own, *refs):
    moe, refs = refs[:parts], refs[parts:]
    gain, mine, theirs, out, mixed, normed = refs
    half, ep, pool = place[0], place[1], place[2]
    width = moe[0].shape[1]
    square = jnp.zeros((own.shape[0], 1), F32)
    for k in range(parts):
        columns = columns_of(half ^ k, width)
        value = own[:, columns].astype(F32) + moe[k][...].astype(F32)
        mixed[:, columns] = value
        square += jnp.sum(value * value, axis=1, keepdims=True)
    factor = lax.rsqrt(square / mixed.shape[1] + 1e-06)
    normed[...] = (mixed[...] * factor * gain[...]).astype(BF16)
    depth, narrow = mine.shape[0] // len(origins), mine.shape[1]
    for side, pieces in ((pool, mine), (1 - pool, theirs)):
        total = 0.0
        for i, origin in enumerate(origins):
            total += jnp.dot(
                normed[:, columns_of(ep ^ origin, depth)],
                pieces[i * depth : (i + 1) * depth, :],
                preferred_element_type=F32,
            )
        out[:, columns_of(side, narrow)] = total.astype(BF16)


def project(place, own, moe, gain, mine, theirs, origins):
    return pl.pallas_call(
        functools.partial(project_kernel, len(moe), origins),
        out_shape=jax.ShapeDtypeStruct((own.shape[0], 2 * mine.shape[1]), BF16),
        grid_spec=pltpu.PrefetchScalarGridSpec(
            num_scalar_prefetch=1,
            grid=(),
            in_specs=[WHOLE] * (len(moe) + 4),
            out_specs=WHOLE,
            scratch_shapes=[pltpu.VMEM(own.shape, F32), pltpu.VMEM(own.shape, BF16)],
        ),
        compiler_params=params(0, 12),
        name="project",
    )(place, own, *moe, gain, mine, theirs)


def attend_kernel(k, prompts, place, block, query, fresh_key, fresh_value, w_out, out):
    rows = query.shape[0]
    group_tok = block.shape[0]
    kv_heads = fresh_key.shape[1] // HEAD
    per_head = query.shape[1] // HEAD // kv_heads
    heads = kv_heads * per_head
    position = lax.broadcasted_iota(jnp.int32, (rows, group_tok), 1)
    row = (place[0] ^ k) * rows + lax.broadcasted_iota(jnp.int32, (rows, group_tok), 0)
    segment = jnp.zeros((rows, group_tok), jnp.int32)
    end = jnp.int32(0)
    for p in range(prompts):
        end = end + place[3 + p]
        segment += (position >= end).astype(jnp.int32)
    allowed = jnp.where(segment == row // SAMPLES, 1.0, 0.0)
    allowed = jnp.concatenate([allowed] * heads, axis=0) > 0.5
    scale = 1.0 / math.sqrt(HEAD)
    scores, owns = [], []
    for kv in range(kv_heads):
        key = block[:, 2 * kv * HEAD : (2 * kv + 1) * HEAD]
        new_key = fresh_key[:, kv * HEAD : (kv + 1) * HEAD].astype(F32)
        first = kv * per_head * HEAD
        asked = [query[:, first + j * HEAD : first + (j + 1) * HEAD] for j in range(per_head)]
        scores.append(
            lax.dot_general(
                jnp.concatenate(asked, axis=0),
                key,
                (((1,), (1,)), ((), ())),
                preferred_element_type=F32,
            )
        )
        owns += [jnp.sum(q.astype(F32) * new_key, axis=1, keepdims=True) for q in asked]
    scores = jnp.where(allowed, jnp.concatenate(scores, axis=0) * scale, -1e30)
    own = jnp.concatenate(owns, axis=0) * scale
    top = jnp.maximum(jnp.max(scores, axis=1, keepdims=True), own)
    spread = jnp.where(allowed, jnp.exp(scores - top), 0.0)
    self_weight = jnp.exp(own - top)
    total = jnp.sum(spread, axis=1, keepdims=True) + self_weight
    probs = (spread / total).astype(BF16)
    self_prob = (self_weight / total).astype(BF16).astype(F32)
    mixed = []
    for kv in range(kv_heads):
        value = block[:, (2 * kv + 1) * HEAD : (2 * kv + 2) * HEAD]
        new_value = fresh_value[:, kv * HEAD : (kv + 1) * HEAD].astype(F32)
        lower = kv * per_head * rows
        summed = jnp.dot(
            probs[lower : lower + per_head * rows], value, preferred_element_type=F32
        )
        for j in range(per_head):
            at = slice(j * rows, (j + 1) * rows)
            own_part = self_prob[lower + j * rows : lower + (j + 1) * rows] * new_value
            mixed.append((summed[at] + own_part).astype(BF16))
    attention = jnp.concatenate(mixed, axis=1)
    out[...] = jnp.dot(attention, w_out[...], preferred_element_type=F32).astype(BF16)


def attend(k, prompts, place, block, query, fresh_key, fresh_value, w_out, rows):
    def cut(array):
        return pl.BlockSpec((rows, array.shape[1]), lambda i, place: (place[0] ^ k, 0))

    return pl.pallas_call(
        functools.partial(attend_kernel, k, prompts),
        out_shape=jax.ShapeDtypeStruct((rows, w_out.shape[1]), BF16),
        grid_spec=pltpu.PrefetchScalarGridSpec(
            num_scalar_prefetch=1,
            grid=(1,),
            in_specs=[WHOLE, cut(query), cut(fresh_key), cut(fresh_value), WHOLE],
            out_specs=pl.BlockSpec((rows, w_out.shape[1]), lambda i, place: (0, 0)),
        ),
        compiler_params=params(1, 8),
        cost_estimate=pl.CostEstimate(
            flops=4 * rows * w_out.shape[0] * w_out.shape[1],
            transcendentals=0,
            bytes_accessed=2 * w_out.size,
        ),
        name="attend",
    )(place, block, query, fresh_key, fresh_value, w_out)


def total_of(first, rest):
    value = first.astype(F32)
    for other in rest:
        value = value + other.astype(F32)
    return value


def on_device(
    tokens,
    routes,
    router,
    w_gate,
    w_up,
    w_down,
    norm_gain,
    w_kv,
    lengths,
    queries,
    new_keys,
    new_values,
    w_out,
):
    own = tokens[0]
    chosen = routes[0]
    local, model = own.shape
    top = chosen.shape[1]
    eps = lax.axis_size("ep")
    parts = lax.axis_size("half")
    half, ep, pool = lax.axis_index("half"), lax.axis_index("ep"), lax.axis_index("pool")
    width = model // parts

    prompt_lengths = lax.dynamic_index_in_dim(lengths, 1 - pool, 0, keepdims=False)[0]
    place = jnp.concatenate([jnp.stack([half, ep, pool]), prompt_lengths])

    narrow = w_kv.shape[1] // 2
    tags = jnp.pad(chosen.astype(BF16), ((0, 0), (0, LANES - top)))
    quarter = lax.dynamic_slice_in_dim(own, half * width, width, axis=1)
    parcel = jnp.concatenate([quarter, tags], axis=1)
    order = sorted(range(1, parts), key=lambda k: bin(k).count("1"))
    arrived = [shift(parcel, "ep", d) for d in range(1, eps)]
    sources = (w_gate, w_up, w_down)
    experts = w_gate.shape[0]
    beside, last = order[:-1], order[-1]
    got, _ = stage(place, sources, [(PAIR, 0, 0, experts)])
    near, all_tags = unpack(tags, arrived, width)
    far = order[::-1]
    others = {k: swap(near, "half", k) for k in order[:-1]}
    others[order[-1]] = swap(near, "half", order[-1])
    mine, near = lax.optimization_barrier(
        (lax.dynamic_slice_in_dim(w_kv, pool * narrow, narrow, axis=1), near)
    )
    others[0] = near
    origins = [0]
    for i in range(eps.bit_length() - 1):
        bit = eps >> i + 1
        mine = jnp.concatenate([mine, swap(mine, "ep", bit)], axis=0)
        origins += [origin ^ bit for origin in origins]

    got, totals = stage(
        place, sources, [(PAIR, beside[0], 0, experts)], own, router.T, {0: others[0]},
        [(0, 0, experts, False)], got,
    )
    early = experts // 2
    got, totals = stage(
        place, sources, [(PAIR, last, 0, early)] if early else [], own, router.T,
        {k: others[k] for k in beside},
        [(k, 0, experts, k != beside[0]) for k in beside], got, totals,
    )
    pieces = [(last, 0, early, False)] if early else []
    got, (hidden,) = stage(
        place, sources, [(DOWN, far[0])], own, router.T, {last: others[last]},
        pieces + [(last, early, experts, True)], got, totals, all_tags, top,
    )
    ahead = {far[0]: got[0]}
    partial = {}
    for k in far + [0]:
        if k in ahead:
            partial[k] = reduce_ahead(hidden, ahead[k])
        else:
            partial[k] = reduce(k, place, hidden, w_down, width, width // 2)
    gathered = []
    for k in far:
        gathered.append(swap(partial[k], "half", k))
    summed = total_of(partial[0], gathered)
    returned = [
        shift(summed[d * local : (d + 1) * local].astype(BF16), "ep", -d)
        for d in range(1, eps)
    ]
    mine, summed = lax.optimization_barrier((mine, summed))
    theirs = swap(mine, "pool", 1)
    moe_quarter = total_of(summed[:local], returned).astype(BF16)
    moe = [moe_quarter] + [None] * (parts - 1)
    for k in order:
        moe[k] = swap(moe_quarter, "half", k)
    keyvals = project(place, own, moe, norm_gain[None], mine, theirs, origins)
    block = swap(keyvals, "pool", 1)

    rows = queries.shape[1] // parts
    decoded = {}
    for k in far + [0]:
        decoded[k] = attend(
            k,
            lengths.shape[2],
            place,
            block,
            queries[0],
            new_keys[0],
            new_values[0],
            w_out,
            rows,
        )
    sent = []
    for k in far:
        sent.append(swap(decoded[k], "half", k))
    return total_of(decoded[0], sent).astype(BF16)[None]


def solution(mesh):
    in_specs = (
        P("pool", "ep", None),
        P("pool", "ep", None),
        P(),
        P("ep", None, "half"),
        P("ep", None, "half"),
        P("ep", "half", None),
        P(),
        P("ep", "half"),
        P(None, "ep", None),
        P("pool", "ep", "half"),
        P("pool", "ep", "half"),
        P("pool", "ep", "half"),
        P("half", None),
    )
    out_specs = P("pool", ("ep", "half"), None)
    return jax.shard_map(
        on_device, mesh=mesh, in_specs=in_specs, out_specs=out_specs, check_vma=False
    )
```

```python
import functools
import math

import jax
import jax.numpy as jnp
from jax import lax
from jax.experimental import pallas as pl
from jax.experimental.pallas import tpu as pltpu
from jax.sharding import PartitionSpec as P


HEAD = 128
SAMPLES = 128
LANES = 128
F32 = jnp.float32
BF16 = jnp.bfloat16
WHOLE = pl.BlockSpec(memory_space=pltpu.VMEM)


def swap(shard, axis, bits):
    return lax.ppermute(shard, axis, [(i, i ^ bits) for i in range(lax.axis_size(axis))])


def shift(shard, axis, distance):
    count = lax.axis_size(axis)
    return lax.ppermute(shard, axis, [(i, (i + distance) % count) for i in range(count)])


def params(steps, mebibytes):
    return pltpu.CompilerParams(
        dimension_semantics=("arbitrary",) * steps, vmem_limit_bytes=mebibytes * 1024 * 1024
    )


def in_vmem(array):
    return pltpu.with_memory_space_constraint(array, pltpu.VMEM)


def in_hbm(array):
    return pltpu.with_memory_space_constraint(array, pltpu.HBM)


def columns_of(piece, width):
    return pl.ds(pl.multiple_of(piece * width, width), width)


def router_logits(rows, router, columns):
    return lax.dot_general(
        rows, router[:, columns], (((1,), (1,)), ((), ())), preferred_element_type=F32
    )


def take_rows(quarters, place, own, nears, router, rows):
    local = own.shape[0]
    width = nears[0].shape[1]
    logits = 0.0
    for i, (k, near) in enumerate(zip(quarters, nears)):
        columns = columns_of(place[0] ^ k, width)
        rows[:local, i * width : (i + 1) * width] = own[:, columns]
        rows[local:, i * width : (i + 1) * width] = near[...]
        logits += router_logits(rows[:, i * width : (i + 1) * width], router, columns)
    return logits


PAIR, DOWN = 0, 2


def pair_copies(place, sources, k, low, high, out, sems):
    rows, count = columns_of(place[0] ^ k, out.shape[1]), high - low
    return [
        pltpu.make_async_copy(
            sources[j].at[pl.ds(low, count), rows, :], out.at[pl.ds(j * count, count)], sems.at[j]
        )
        for j in range(2)
    ]


def expert_copies(place, sources, k, low, e, out, sems):
    rows, count = columns_of(place[0] ^ k, out.shape[1]), out.shape[0] // 2
    return [
        pltpu.make_async_copy(
            sources[j].at[e, rows, :], out.at[j * count + e - low], sems.at[j, e - low]
        )
        for j in range(2)
    ]


def unpack_kernel(tags, *refs):
    *arrived, near, all_tags = refs
    local, width = tags.shape[0], near.shape[1]
    all_tags[:local, :] = tags[...]
    for d, parcel in enumerate(arrived):
        near[d * local : (d + 1) * local, :] = parcel[:, :width]
        all_tags[(d + 1) * local : (d + 2) * local, :] = parcel[:, width:]


def unpack(tags, arrived, width):
    local, extra = tags.shape
    count = len(arrived)
    return pl.pallas_call(
        unpack_kernel,
        out_shape=[
            jax.ShapeDtypeStruct((count * local, width), BF16),
            jax.ShapeDtypeStruct(((count + 1) * local, extra), BF16),
        ],
        in_specs=[WHOLE] * (1 + count),
        out_specs=[WHOLE] * 2,
        compiler_params=params(0, 4 if count < 8 else 32),
        name="unpack",
    )(tags, *arrived)


def streams_of(parts):
    return [(k, low, high) for low, high, ks in parts for k, streamed in ks if streamed]


def stage_kernel(items, quarters, parts, first, top, place, *refs):
    refs = list(refs)

    def take(count):
        taken = refs[:count]
        del refs[:count]
        return taken

    sources, count = take(3), len(quarters)
    streams = streams_of(parts)
    if count:
        (own, router), nears = take(2), take(count)
        held = take(sum(len(part[2]) for part in parts) - len(streams))
        totals = [None, None] if first else take(2)
        tags = take(1)[0] if top else None
    ahead = take(len(items))
    out = take(1)[0] if count else None
    logits_out = take(1)[0] if count and not top else None
    ahead_sems = take(1)[0]
    rows = take(1)[0] if count else None
    weights = take(1)[0] if top else None
    buffers, buffer_sems = take(len(streams)), take(len(streams))

    for (k, low, high), buffer, sems in zip(streams, buffers, buffer_sems):
        for e in range(low, high):
            for copy in expert_copies(place, sources, k, low, e, buffer, sems):
                copy.start()
    copies = []
    for n, item in enumerate(items):
        if item[0] == PAIR:
            copies += pair_copies(place, sources, *item[1:], ahead[n], ahead_sems.at[n])
        else:
            columns = columns_of(place[0] ^ item[1], ahead[n].shape[2])
            copies.append(
                pltpu.make_async_copy(
                    sources[DOWN].at[:, :, columns], ahead[n], ahead_sems.at[n, 0]
                )
            )
    if not streams:
        for copy in copies:
            copy.start()
    if count:
        logits = take_rows(quarters, place, own, nears, router, rows)
        if not first:
            logits += totals[1][...]
        if top:
            expert = lax.broadcasted_iota(jnp.int32, logits.shape, 1)
            named = tags[...].astype(F32).astype(jnp.int32)
            picked = named[:, 0:1] == expert
            for j in range(1, top):
                picked = jnp.logical_or(picked, named[:, j : j + 1] == expert)
            most = jnp.max(jnp.where(picked, logits, -1e30), axis=1, keepdims=True)
            spread = jnp.where(picked, jnp.exp(logits - most), 0.0)
            weights[...] = spread / jnp.sum(spread, axis=1, keepdims=True)
        else:
            logits_out[...] = logits
        experts, (_, _, units) = sources[0].shape[0], sources[0].shape
        held, buffers, buffer_sems = list(held), list(buffers), list(buffer_sems)
        for n, (low, high, ks) in enumerate(parts):
            sources_of = [
                (k, buffers.pop(0), buffer_sems.pop(0)) if streamed else (k, held.pop(0), None)
                for k, streamed in ks
            ]

            def body(e, carry, n=n, low=low, high=high, sources_of=sources_of):
                both = []
                for k, weight, sems in sources_of:
                    if sems is not None:
                        for copy in expert_copies(place, sources, k, low, e, weight, sems):
                            copy.wait()
                    half = weight.shape[0] // 2
                    both.append(
                        jnp.concatenate([weight[e - low], weight[half + e - low]], axis=1)
                    )
                if streams and n == 0:

                    @pl.when(e == (low + high) // 2)
                    def _():
                        for copy in copies:
                            copy.start()

                both = jnp.concatenate(both, axis=0)
                value = jnp.dot(rows[...], both, preferred_element_type=F32)
                if not first:
                    value += totals[0][e]
                if not top:
                    out[e] = value
                    return carry
                gate, up = value[:, :units], value[:, units:]
                mine = expert == place[1] * experts + e
                scale = jnp.sum(jnp.where(mine, weights[...], 0.0), axis=1, keepdims=True)
                out[:, columns_of(e, units)] = (
                    gate / (1.0 + jnp.exp(-gate)) * up * scale
                ).astype(BF16)
                return carry

            lax.fori_loop(low, high, body, 0, unroll=math.gcd(2, high - low))
    for copy in copies:
        copy.wait()


def stage(place, sources, items, own=None, router=None, nears=None, parts=(), held=(),
          totals=(), tags=None, top=0):
    experts, model, units = sources[0].shape
    nears = nears or {}
    quarters = list(nears)
    width = model // lax.axis_size("half")
    count = len(quarters)
    operands = [in_hbm(array) for array in sources]
    shapes = [
        pltpu.VMEM((2 * (item[3] - item[2]), width, units), BF16)
        if item[0] == PAIR
        else pltpu.VMEM((experts, units, width), BF16)
        for item in items
    ]
    scratch, aliases, tokens = [pltpu.SemaphoreType.DMA((max(1, len(items)), 2))], {}, 0
    streams = streams_of(parts)
    mebibytes = 1
    if count:
        tokens = own.shape[0] + nears[quarters[0]].shape[0]
        mebibytes = 8 + -(-sum(4 * width * units * (p[2] - p[1]) for p in streams) >> 20)
        operands += [own, router] + [in_vmem(nears[k]) for k in quarters]
        operands += [in_vmem(array) for array in held]
        aliases = {1 + len(operands) + i: len(items) + i for i in range(len(totals))}
        operands += [in_vmem(total) for total in totals]
        scratch.append(pltpu.VMEM((tokens, count * width), BF16))
        if top:
            operands.append(tags)
            aliases = {}
            scratch.append(pltpu.VMEM((tokens, router.shape[0]), F32))
            shapes.append(pltpu.VMEM((tokens, experts * units), BF16))
        else:
            shapes.append(pltpu.VMEM((experts, tokens, 2 * units), F32))
            shapes.append(pltpu.VMEM((tokens, router.shape[0]), F32))
    scratch += [pltpu.VMEM((2 * (p[2] - p[1]), width, units), BF16) for p in streams]
    scratch += [pltpu.SemaphoreType.DMA((2, p[2] - p[1])) for p in streams]
    outs = pl.pallas_call(
        functools.partial(stage_kernel, items, quarters, parts, not totals, top),
        out_shape=shapes,
        grid_spec=pltpu.PrefetchScalarGridSpec(
            num_scalar_prefetch=1,
            grid=(),
            in_specs=[pl.BlockSpec(memory_space=pl.ANY)] * 3 + [WHOLE] * (len(operands) - 3),
            out_specs=[WHOLE] * len(shapes),
            scratch_shapes=scratch,
        ),
        input_output_aliases=aliases,
        compiler_params=params(0, mebibytes if tokens <= 1024 else 32),
    )(place, *operands)
    return outs[: len(items)], outs[len(items) :]


def reduce_kernel(place, hidden, w_down, out):
    weight = w_down[...].reshape(-1, w_down.shape[2])
    out[...] = jnp.dot(hidden[...], weight, preferred_element_type=F32).astype(BF16)


def reduce_ahead_kernel(hidden, weight, out):
    block = weight.shape[2] // 2
    for i in range(2):
        columns = slice(i * block, (i + 1) * block)
        piece = weight[:, :, columns].reshape(-1, block)
        out[:, columns] = jnp.dot(hidden[...], piece, preferred_element_type=F32).astype(BF16)


def reduce_ahead(hidden, weight):
    return pl.pallas_call(
        reduce_ahead_kernel,
        out_shape=jax.ShapeDtypeStruct((hidden.shape[0], weight.shape[2]), BF16),
        in_specs=[WHOLE] * 2,
        out_specs=WHOLE,
        compiler_params=params(0, 12),
        name="reduce",
    )(in_vmem(hidden), in_vmem(weight))


def reduce(k, place, hidden, w_down, width, block):
    experts, units, _ = w_down.shape
    steps = width // block
    tokens = hidden.shape[0]
    return pl.pallas_call(
        reduce_kernel,
        out_shape=jax.ShapeDtypeStruct((tokens, width), BF16),
        grid_spec=pltpu.PrefetchScalarGridSpec(
            num_scalar_prefetch=1,
            grid=(steps,),
            in_specs=[
                WHOLE,
                pl.BlockSpec(
                    (experts, units, block),
                    lambda i, place: (0, 0, (place[0] ^ k) * steps + i),
                ),
            ],
            out_specs=pl.BlockSpec((tokens, block), lambda i, place: (0, i)),
        ),
        compiler_params=params(1, 16),
        cost_estimate=pl.CostEstimate(
            flops=2 * tokens * width * experts * units,
            transcendentals=0,
            bytes_accessed=2 * experts * width * units,
        ),
        name="reduce",
    )(place, in_vmem(hidden), in_hbm(w_down))


def project_kernel(parts, origins, place, own, *refs):
    moe, refs = refs[:parts], refs[parts:]
    gain, mine, theirs, out, mixed, normed = refs
    half, ep, pool = place[0], place[1], place[2]
    width = moe[0].shape[1]
    square = jnp.zeros((own.shape[0], 1), F32)
    for k in range(parts):
        columns = columns_of(half ^ k, width)
        value = own[:, columns].astype(F32) + moe[k][...].astype(F32)
        mixed[:, columns] = value
        square += jnp.sum(value * value, axis=1, keepdims=True)
    factor = lax.rsqrt(square / mixed.shape[1] + 1e-06)
    normed[...] = (mixed[...] * factor * gain[...]).astype(BF16)
    depth, narrow = mine.shape[0] // len(origins), mine.shape[1]
    for side, pieces in ((pool, mine), (1 - pool, theirs)):
        total = 0.0
        for i, origin in enumerate(origins):
            total += jnp.dot(
                normed[:, columns_of(ep ^ origin, depth)],
                pieces[i * depth : (i + 1) * depth, :],
                preferred_element_type=F32,
            )
        out[:, columns_of(side, narrow)] = total.astype(BF16)


def project(place, own, moe, gain, mine, theirs, origins):
    return pl.pallas_call(
        functools.partial(project_kernel, len(moe), origins),
        out_shape=jax.ShapeDtypeStruct((own.shape[0], 2 * mine.shape[1]), BF16),
        grid_spec=pltpu.PrefetchScalarGridSpec(
            num_scalar_prefetch=1,
            grid=(),
            in_specs=[WHOLE] * (len(moe) + 4),
            out_specs=WHOLE,
            scratch_shapes=[pltpu.VMEM(own.shape, F32), pltpu.VMEM(own.shape, BF16)],
        ),
        compiler_params=params(0, 12),
        name="project",
    )(place, own, *moe, gain, mine, theirs)


def attend_kernel(k, prompts, place, block, query, fresh_key, fresh_value, w_out, out):
    rows = query.shape[0]
    group_tok = block.shape[0]
    kv_heads = fresh_key.shape[1] // HEAD
    per_head = query.shape[1] // HEAD // kv_heads
    heads = kv_heads * per_head
    position = lax.broadcasted_iota(jnp.int32, (rows, group_tok), 1)
    row = (place[0] ^ k) * rows + lax.broadcasted_iota(jnp.int32, (rows, group_tok), 0)
    segment = jnp.zeros((rows, group_tok), jnp.int32)
    end = jnp.int32(0)
    for p in range(prompts):
        end = end + place[3 + p]
        segment += (position >= end).astype(jnp.int32)
    allowed = jnp.where(segment == row // SAMPLES, 1.0, 0.0)
    allowed = jnp.concatenate([allowed] * heads, axis=0) > 0.5
    scale = 1.0 / math.sqrt(HEAD)
    scores, owns = [], []
    for kv in range(kv_heads):
        key = block[:, 2 * kv * HEAD : (2 * kv + 1) * HEAD]
        new_key = fresh_key[:, kv * HEAD : (kv + 1) * HEAD].astype(F32)
        first = kv * per_head * HEAD
        asked = [query[:, first + j * HEAD : first + (j + 1) * HEAD] for j in range(per_head)]
        scores.append(
            lax.dot_general(
                jnp.concatenate(asked, axis=0),
                key,
                (((1,), (1,)), ((), ())),
                preferred_element_type=F32,
            )
        )
        owns += [jnp.sum(q.astype(F32) * new_key, axis=1, keepdims=True) for q in asked]
    scores = jnp.where(allowed, jnp.concatenate(scores, axis=0) * scale, -1e30)
    own = jnp.concatenate(owns, axis=0) * scale
    top = jnp.maximum(jnp.max(scores, axis=1, keepdims=True), own)
    spread = jnp.where(allowed, jnp.exp(scores - top), 0.0)
    self_weight = jnp.exp(own - top)
    total = jnp.sum(spread, axis=1, keepdims=True) + self_weight
    probs = (spread / total).astype(BF16)
    self_prob = (self_weight / total).astype(BF16).astype(F32)
    mixed = []
    for kv in range(kv_heads):
        value = block[:, (2 * kv + 1) * HEAD : (2 * kv + 2) * HEAD]
        new_value = fresh_value[:, kv * HEAD : (kv + 1) * HEAD].astype(F32)
        lower = kv * per_head * rows
        summed = jnp.dot(
            probs[lower : lower + per_head * rows], value, preferred_element_type=F32
        )
        for j in range(per_head):
            at = slice(j * rows, (j + 1) * rows)
            own_part = self_prob[lower + j * rows : lower + (j + 1) * rows] * new_value
            mixed.append((summed[at] + own_part).astype(BF16))
    attention = jnp.concatenate(mixed, axis=1)
    out[...] = jnp.dot(attention, w_out[...], preferred_element_type=F32).astype(BF16)


def attend(k, prompts, place, block, query, fresh_key, fresh_value, w_out, rows):
    def cut(array):
        return pl.BlockSpec((rows, array.shape[1]), lambda i, place: (place[0] ^ k, 0))

    return pl.pallas_call(
        functools.partial(attend_kernel, k, prompts),
        out_shape=jax.ShapeDtypeStruct((rows, w_out.shape[1]), BF16),
        grid_spec=pltpu.PrefetchScalarGridSpec(
            num_scalar_prefetch=1,
            grid=(1,),
            in_specs=[WHOLE, cut(query), cut(fresh_key), cut(fresh_value), WHOLE],
            out_specs=pl.BlockSpec((rows, w_out.shape[1]), lambda i, place: (0, 0)),
        ),
        compiler_params=params(1, 8),
        cost_estimate=pl.CostEstimate(
            flops=4 * rows * w_out.shape[0] * w_out.shape[1],
            transcendentals=0,
            bytes_accessed=2 * w_out.size,
        ),
        name="attend",
    )(place, block, query, fresh_key, fresh_value, w_out)


def total_of(first, rest):
    value = first.astype(F32)
    for other in rest:
        value = value + other.astype(F32)
    return value


def on_device(
    tokens,
    routes,
    router,
    w_gate,
    w_up,
    w_down,
    norm_gain,
    w_kv,
    lengths,
    queries,
    new_keys,
    new_values,
    w_out,
):
    own = tokens[0]
    chosen = routes[0]
    local, model = own.shape
    top = chosen.shape[1]
    eps = lax.axis_size("ep")
    parts = lax.axis_size("half")
    half, ep, pool = lax.axis_index("half"), lax.axis_index("ep"), lax.axis_index("pool")
    width = model // parts

    prompt_lengths = lax.dynamic_index_in_dim(lengths, 1 - pool, 0, keepdims=False)[0]
    place = jnp.concatenate([jnp.stack([half, ep, pool]), prompt_lengths])

    narrow = w_kv.shape[1] // 2
    tags = jnp.pad(chosen.astype(BF16), ((0, 0), (0, LANES - top)))
    quarter = lax.dynamic_slice_in_dim(own, half * width, width, axis=1)
    parcel = jnp.concatenate([quarter, tags], axis=1)
    order = sorted(range(1, parts), key=lambda k: bin(k).count("1"))
    arrived = [shift(parcel, "ep", d) for d in range(1, eps)]
    sources = (w_gate, w_up, w_down)
    experts = w_gate.shape[0]
    beside, last = order[:-1], order[-1]
    got, _ = stage(place, sources, [(PAIR, 0, 0, experts)])
    near, all_tags = unpack(tags, arrived, width)
    far = order[::-1]
    others = {k: swap(near, "half", k) for k in order[:-1]}
    again, others = lax.optimization_barrier((near, others))
    others[order[-1]] = swap(again, "half", order[-1])
    mine = lax.dynamic_slice_in_dim(w_kv, pool * narrow, narrow, axis=1)
    others[0] = near
    bits = [eps >> i + 1 for i in range(eps.bit_length() - 1)]
    received = swap(mine, "ep", bits[0])
    origins = [0, bits[0]]
    got, totals = stage(
        place, sources, [(PAIR, beside[0], 0, experts)], own, router.T, {0: others[0]},
        [(0, experts, [(0, False)])], got,
    )
    early = experts // 2
    got, totals = stage(
        place, sources, [(PAIR, last, 0, early)] if early else [], own, router.T,
        {k: others[k] for k in beside},
        [(0, experts, [(k, k != beside[0]) for k in beside])], got, totals,
    )
    pieces = [(0, early, [(last, False)])] if early else []
    got, (hidden,) = stage(
        place, sources, [(DOWN, far[0])], own, router.T, {last: others[last]},
        pieces + [(early, experts, [(last, True)])], got, totals, all_tags, top,
    )
    ahead = {far[0]: got[0]}
    partial = {}
    for k in far + [0]:
        if k in ahead:
            partial[k] = reduce_ahead(hidden, ahead[k])
        else:
            partial[k] = reduce(k, place, hidden, w_down, width, width // 2)
    received, partial[far[1]] = lax.optimization_barrier((received, partial[far[1]]))
    mine = jnp.concatenate([mine, received], axis=0)
    for bit in bits[1:]:
        mine = jnp.concatenate([mine, swap(mine, "ep", bit)], axis=0)
        origins += [origin ^ bit for origin in origins]
    gathered = []
    for k in far:
        gathered.append(swap(partial[k], "half", k))
    summed = total_of(partial[0], gathered)
    returned = [
        shift(summed[d * local : (d + 1) * local].astype(BF16), "ep", -d)
        for d in range(1, eps)
    ]
    mine, summed = lax.optimization_barrier((mine, summed))
    theirs = swap(mine, "pool", 1)
    moe_quarter = total_of(summed[:local], returned).astype(BF16)
    moe = [moe_quarter] + [None] * (parts - 1)
    for k in order:
        moe[k] = swap(moe_quarter, "half", k)
    keyvals = project(place, own, moe, norm_gain[None], mine, theirs, origins)
    block = swap(keyvals, "pool", 1)

    rows = queries.shape[1] // parts
    decoded = {}
    for k in far + [0]:
        decoded[k] = attend(
            k,
            lengths.shape[2],
            place,
            block,
            queries[0],
            new_keys[0],
            new_values[0],
            w_out,
            rows,
        )
    sent = []
    for k in far:
        sent.append(swap(decoded[k], "half", k))
    return total_of(decoded[0], sent).astype(BF16)[None]


def solution(mesh):
    in_specs = (
        P("pool", "ep", None),
        P("pool", "ep", None),
        P(),
        P("ep", None, "half"),
        P("ep", None, "half"),
        P("ep", "half", None),
        P(),
        P("ep", "half"),
        P(None, "ep", None),
        P("pool", "ep", "half"),
        P("pool", "ep", "half"),
        P("pool", "ep", "half"),
        P("half", None),
    )
    out_specs = P("pool", ("ep", "half"), None)
    return jax.shard_map(
        on_device, mesh=mesh, in_specs=in_specs, out_specs=out_specs, check_vma=False
    )
```

```python
import functools
import math

import jax
import jax.numpy as jnp
from jax import lax
from jax.experimental import pallas as pl
from jax.experimental.pallas import tpu as pltpu
from jax.sharding import PartitionSpec as P


HEAD = 128
SAMPLES = 128
LANES = 128
F32 = jnp.float32
BF16 = jnp.bfloat16
WHOLE = pl.BlockSpec(memory_space=pltpu.VMEM)


def swap(shard, axis, bits):
    return lax.ppermute(shard, axis, [(i, i ^ bits) for i in range(lax.axis_size(axis))])


def shift(shard, axis, distance):
    count = lax.axis_size(axis)
    return lax.ppermute(shard, axis, [(i, (i + distance) % count) for i in range(count)])


def params(steps, mebibytes):
    return pltpu.CompilerParams(
        dimension_semantics=("arbitrary",) * steps, vmem_limit_bytes=mebibytes * 1024 * 1024
    )


def in_vmem(array):
    return pltpu.with_memory_space_constraint(array, pltpu.VMEM)


def in_hbm(array):
    return pltpu.with_memory_space_constraint(array, pltpu.HBM)


def columns_of(piece, width):
    return pl.ds(pl.multiple_of(piece * width, width), width)


def router_logits(rows, router, columns):
    return lax.dot_general(
        rows, router[:, columns], (((1,), (1,)), ((), ())), preferred_element_type=F32
    )


def take_rows(quarters, place, own, nears, router, rows):
    local = own.shape[0]
    width = nears[0].shape[1]
    logits = 0.0
    for i, (k, near) in enumerate(zip(quarters, nears)):
        columns = columns_of(place[0] ^ k, width)
        rows[:local, i * width : (i + 1) * width] = own[:, columns]
        rows[local:, i * width : (i + 1) * width] = near[...]
        logits += router_logits(rows[:, i * width : (i + 1) * width], router, columns)
    return logits


PAIR, DOWN = 0, 2


def pair_copies(place, sources, k, low, high, out, sems):
    rows, count = columns_of(place[0] ^ k, out.shape[1]), high - low
    return [
        pltpu.make_async_copy(
            sources[j].at[pl.ds(low, count), rows, :], out.at[pl.ds(j * count, count)], sems.at[j]
        )
        for j in range(2)
    ]


def expert_copies(place, sources, k, low, e, out, sems):
    rows, count = columns_of(place[0] ^ k, out.shape[1]), out.shape[0] // 2
    return [
        pltpu.make_async_copy(
            sources[j].at[e, rows, :], out.at[j * count + e - low], sems.at[j, e - low]
        )
        for j in range(2)
    ]


def unpack_kernel(tags, *refs):
    *arrived, near, all_tags = refs
    local, width = tags.shape[0], near.shape[1]
    all_tags[:local, :] = tags[...]
    for d, parcel in enumerate(arrived):
        near[d * local : (d + 1) * local, :] = parcel[:, :width]
        all_tags[(d + 1) * local : (d + 2) * local, :] = parcel[:, width:]


def unpack(tags, arrived, width):
    local, extra = tags.shape
    count = len(arrived)
    return pl.pallas_call(
        unpack_kernel,
        out_shape=[
            jax.ShapeDtypeStruct((count * local, width), BF16),
            jax.ShapeDtypeStruct(((count + 1) * local, extra), BF16),
        ],
        in_specs=[WHOLE] * (1 + count),
        out_specs=[WHOLE] * 2,
        compiler_params=params(0, 4 if count < 8 else 32),
        name="unpack",
    )(tags, *arrived)


def streams_of(parts):
    return [(k, low, high) for low, high, ks in parts for k, streamed in ks if streamed]


def stage_kernel(items, quarters, parts, first, top, place, *refs):
    refs = list(refs)

    def take(count):
        taken = refs[:count]
        del refs[:count]
        return taken

    sources, count = take(3), len(quarters)
    streams = streams_of(parts)
    if count:
        (own, router), nears = take(2), take(count)
        held = take(sum(len(part[2]) for part in parts) - len(streams))
        totals = [None, None] if first else take(2)
        tags = take(1)[0] if top else None
    ahead = take(len(items))
    out = take(1)[0] if count else None
    logits_out = take(1)[0] if count and not top else None
    ahead_sems = take(1)[0]
    rows = take(1)[0] if count else None
    weights = take(1)[0] if top else None
    buffers, buffer_sems = take(len(streams)), take(len(streams))

    for (k, low, high), buffer, sems in zip(streams, buffers, buffer_sems):
        for e in range(low, high):
            for copy in expert_copies(place, sources, k, low, e, buffer, sems):
                copy.start()
    copies = []
    for n, item in enumerate(items):
        if item[0] == PAIR:
            copies += pair_copies(place, sources, *item[1:], ahead[n], ahead_sems.at[n])
        else:
            columns = columns_of(place[0] ^ item[1], ahead[n].shape[2])
            copies.append(
                pltpu.make_async_copy(
                    sources[DOWN].at[:, :, columns], ahead[n], ahead_sems.at[n, 0]
                )
            )
    if not streams:
        for copy in copies:
            copy.start()
    if count:
        logits = take_rows(quarters, place, own, nears, router, rows)
        if not first:
            logits += totals[1][...]
        if top:
            expert = lax.broadcasted_iota(jnp.int32, logits.shape, 1)
            named = tags[...].astype(F32).astype(jnp.int32)
            picked = named[:, 0:1] == expert
            for j in range(1, top):
                picked = jnp.logical_or(picked, named[:, j : j + 1] == expert)
            most = jnp.max(jnp.where(picked, logits, -1e30), axis=1, keepdims=True)
            spread = jnp.where(picked, jnp.exp(logits - most), 0.0)
            weights[...] = spread / jnp.sum(spread, axis=1, keepdims=True)
        else:
            logits_out[...] = logits
        experts, (_, _, units) = sources[0].shape[0], sources[0].shape
        near_width = nears[0].shape[1]
        held, buffers, buffer_sems = list(held), list(buffers), list(buffer_sems)
        for n, (low, high, ks) in enumerate(parts):
            sources_of = [
                (k, buffers.pop(0), buffer_sems.pop(0)) if streamed else (k, held.pop(0), None)
                for k, streamed in ks
            ]

            begun = any(part[0] <= low < part[1] for part in parts[:n])

            def body(e, carry, n=n, low=low, high=high, sources_of=sources_of, begun=begun):
                both = []
                at = quarters.index(sources_of[0][0]) * near_width
                for k, weight, sems in sources_of:
                    if sems is not None:
                        for copy in expert_copies(place, sources, k, low, e, weight, sems):
                            copy.wait()
                    half = weight.shape[0] // 2
                    both.append(
                        jnp.concatenate([weight[e - low], weight[half + e - low]], axis=1)
                    )
                if streams and n == 0:

                    @pl.when(e == (low + high) // 2)
                    def _():
                        for copy in copies:
                            copy.start()

                both = jnp.concatenate(both, axis=0)
                used = rows[:, at : at + both.shape[0]]
                value = jnp.dot(used, both, preferred_element_type=F32)
                if begun:
                    value += out[e]
                elif not first:
                    value += totals[0][e]
                if not top:
                    out[e] = value
                    return carry
                gate, up = value[:, :units], value[:, units:]
                mine = expert == place[1] * experts + e
                scale = jnp.sum(jnp.where(mine, weights[...], 0.0), axis=1, keepdims=True)
                out[:, columns_of(e, units)] = (
                    gate / (1.0 + jnp.exp(-gate)) * up * scale
                ).astype(BF16)
                return carry

            lax.fori_loop(low, high, body, 0, unroll=math.gcd(2, high - low))
    for copy in copies:
        copy.wait()


def stage(place, sources, items, own=None, router=None, nears=None, parts=(), held=(),
          totals=(), tags=None, top=0):
    experts, model, units = sources[0].shape
    nears = nears or {}
    quarters = list(nears)
    width = model // lax.axis_size("half")
    count = len(quarters)
    operands = [in_hbm(array) for array in sources]
    shapes = [
        pltpu.VMEM((2 * (item[3] - item[2]), width, units), BF16)
        if item[0] == PAIR
        else pltpu.VMEM((experts, units, width), BF16)
        for item in items
    ]
    scratch, aliases, tokens = [pltpu.SemaphoreType.DMA((max(1, len(items)), 2))], {}, 0
    streams = streams_of(parts)
    mebibytes = 1
    if count:
        tokens = own.shape[0] + nears[quarters[0]].shape[0]
        mebibytes = 8 + -(-sum(4 * width * units * (p[2] - p[1]) for p in streams) >> 20)
        operands += [own, router] + [in_vmem(nears[k]) for k in quarters]
        operands += [in_vmem(array) for array in held]
        aliases = {1 + len(operands) + i: len(items) + i for i in range(len(totals))}
        operands += [in_vmem(total) for total in totals]
        scratch.append(pltpu.VMEM((tokens, count * width), BF16))
        if top:
            operands.append(tags)
            aliases = {}
            scratch.append(pltpu.VMEM((tokens, router.shape[0]), F32))
            shapes.append(pltpu.VMEM((tokens, experts * units), BF16))
        else:
            shapes.append(pltpu.VMEM((experts, tokens, 2 * units), F32))
            shapes.append(pltpu.VMEM((tokens, router.shape[0]), F32))
    scratch += [pltpu.VMEM((2 * (p[2] - p[1]), width, units), BF16) for p in streams]
    scratch += [pltpu.SemaphoreType.DMA((2, p[2] - p[1])) for p in streams]
    outs = pl.pallas_call(
        functools.partial(stage_kernel, items, quarters, parts, not totals, top),
        out_shape=shapes,
        grid_spec=pltpu.PrefetchScalarGridSpec(
            num_scalar_prefetch=1,
            grid=(),
            in_specs=[pl.BlockSpec(memory_space=pl.ANY)] * 3 + [WHOLE] * (len(operands) - 3),
            out_specs=[WHOLE] * len(shapes),
            scratch_shapes=scratch,
        ),
        input_output_aliases=aliases,
        compiler_params=params(0, mebibytes if tokens <= 1024 else 32),
    )(place, *operands)
    return outs[: len(items)], outs[len(items) :]


def reduce_kernel(place, hidden, w_down, out):
    weight = w_down[...].reshape(-1, w_down.shape[2])
    out[...] = jnp.dot(hidden[...], weight, preferred_element_type=F32).astype(BF16)


def reduce_ahead_kernel(hidden, weight, out):
    block = weight.shape[2] // 2
    for i in range(2):
        columns = slice(i * block, (i + 1) * block)
        piece = weight[:, :, columns].reshape(-1, block)
        out[:, columns] = jnp.dot(hidden[...], piece, preferred_element_type=F32).astype(BF16)


def reduce_ahead(hidden, weight):
    return pl.pallas_call(
        reduce_ahead_kernel,
        out_shape=jax.ShapeDtypeStruct((hidden.shape[0], weight.shape[2]), BF16),
        in_specs=[WHOLE] * 2,
        out_specs=WHOLE,
        compiler_params=params(0, 12),
        name="reduce",
    )(in_vmem(hidden), in_vmem(weight))


def reduce(k, place, hidden, w_down, width, block):
    experts, units, _ = w_down.shape
    steps = width // block
    tokens = hidden.shape[0]
    return pl.pallas_call(
        reduce_kernel,
        out_shape=jax.ShapeDtypeStruct((tokens, width), BF16),
        grid_spec=pltpu.PrefetchScalarGridSpec(
            num_scalar_prefetch=1,
            grid=(steps,),
            in_specs=[
                WHOLE,
                pl.BlockSpec(
                    (experts, units, block),
                    lambda i, place: (0, 0, (place[0] ^ k) * steps + i),
                ),
            ],
            out_specs=pl.BlockSpec((tokens, block), lambda i, place: (0, i)),
        ),
        compiler_params=params(1, 16),
        cost_estimate=pl.CostEstimate(
            flops=2 * tokens * width * experts * units,
            transcendentals=0,
            bytes_accessed=2 * experts * width * units,
        ),
        name="reduce",
    )(place, in_vmem(hidden), in_hbm(w_down))


def project_kernel(parts, eps, place, own, *refs):
    moe, refs = refs[:parts], refs[parts:]
    gain, mine, theirs, out, mixed, normed = refs
    half, ep, pool = place[0], place[1], place[2]
    width = moe[0].shape[1]
    square = jnp.zeros((own.shape[0], 1), F32)
    for k in range(parts):
        columns = columns_of(half ^ k, width)
        value = own[:, columns].astype(F32) + moe[k][...].astype(F32)
        mixed[:, columns] = value
        square += jnp.sum(value * value, axis=1, keepdims=True)
    factor = lax.rsqrt(square / mixed.shape[1] + 1e-06)
    normed[...] = (mixed[...] * factor * gain[...]).astype(BF16)
    depth, narrow = mine.shape[0] // eps, mine.shape[1]
    for side, pieces in ((pool, mine), (1 - pool, theirs)):
        total = 0.0
        for d in range(eps):
            total += jnp.dot(
                normed[:, columns_of(lax.rem(ep + eps - d, eps), depth)],
                pieces[d * depth : (d + 1) * depth, :],
                preferred_element_type=F32,
            )
        out[:, columns_of(side, narrow)] = total.astype(BF16)


def project(place, own, moe, gain, mine, theirs, eps):
    return pl.pallas_call(
        functools.partial(project_kernel, len(moe), eps),
        out_shape=jax.ShapeDtypeStruct((own.shape[0], 2 * mine.shape[1]), BF16),
        grid_spec=pltpu.PrefetchScalarGridSpec(
            num_scalar_prefetch=1,
            grid=(),
            in_specs=[WHOLE] * (len(moe) + 4),
            out_specs=WHOLE,
            scratch_shapes=[pltpu.VMEM(own.shape, F32), pltpu.VMEM(own.shape, BF16)],
        ),
        compiler_params=params(0, 12),
        name="project",
    )(place, own, *moe, gain, mine, theirs)


def attend_kernel(k, prompts, place, block, query, fresh_key, fresh_value, w_out, out):
    rows = query.shape[0]
    group_tok = block.shape[0]
    kv_heads = fresh_key.shape[1] // HEAD
    per_head = query.shape[1] // HEAD // kv_heads
    heads = kv_heads * per_head
    position = lax.broadcasted_iota(jnp.int32, (rows, group_tok), 1)
    row = (place[0] ^ k) * rows + lax.broadcasted_iota(jnp.int32, (rows, group_tok), 0)
    segment = jnp.zeros((rows, group_tok), jnp.int32)
    end = jnp.int32(0)
    for p in range(prompts):
        end = end + place[3 + p]
        segment += (position >= end).astype(jnp.int32)
    allowed = jnp.where(segment == row // SAMPLES, 1.0, 0.0)
    allowed = jnp.concatenate([allowed] * heads, axis=0) > 0.5
    scale = 1.0 / math.sqrt(HEAD)
    scores, owns = [], []
    for kv in range(kv_heads):
        key = block[:, 2 * kv * HEAD : (2 * kv + 1) * HEAD]
        new_key = fresh_key[:, kv * HEAD : (kv + 1) * HEAD].astype(F32)
        first = kv * per_head * HEAD
        asked = [query[:, first + j * HEAD : first + (j + 1) * HEAD] for j in range(per_head)]
        scores.append(
            lax.dot_general(
                jnp.concatenate(asked, axis=0),
                key,
                (((1,), (1,)), ((), ())),
                preferred_element_type=F32,
            )
        )
        owns += [jnp.sum(q.astype(F32) * new_key, axis=1, keepdims=True) for q in asked]
    scores = jnp.where(allowed, jnp.concatenate(scores, axis=0) * scale, -1e30)
    own = jnp.concatenate(owns, axis=0) * scale
    top = jnp.maximum(jnp.max(scores, axis=1, keepdims=True), own)
    spread = jnp.where(allowed, jnp.exp(scores - top), 0.0)
    self_weight = jnp.exp(own - top)
    total = jnp.sum(spread, axis=1, keepdims=True) + self_weight
    probs = (spread / total).astype(BF16)
    self_prob = (self_weight / total).astype(BF16).astype(F32)
    mixed = []
    for kv in range(kv_heads):
        value = block[:, (2 * kv + 1) * HEAD : (2 * kv + 2) * HEAD]
        new_value = fresh_value[:, kv * HEAD : (kv + 1) * HEAD].astype(F32)
        lower = kv * per_head * rows
        summed = jnp.dot(
            probs[lower : lower + per_head * rows], value, preferred_element_type=F32
        )
        for j in range(per_head):
            at = slice(j * rows, (j + 1) * rows)
            own_part = self_prob[lower + j * rows : lower + (j + 1) * rows] * new_value
            mixed.append((summed[at] + own_part).astype(BF16))
    attention = jnp.concatenate(mixed, axis=1)
    out[...] = jnp.dot(attention, w_out[...], preferred_element_type=F32).astype(BF16)


def attend(k, prompts, place, block, query, fresh_key, fresh_value, w_out, rows):
    def cut(array):
        return pl.BlockSpec((rows, array.shape[1]), lambda i, place: (place[0] ^ k, 0))

    return pl.pallas_call(
        functools.partial(attend_kernel, k, prompts),
        out_shape=jax.ShapeDtypeStruct((rows, w_out.shape[1]), BF16),
        grid_spec=pltpu.PrefetchScalarGridSpec(
            num_scalar_prefetch=1,
            grid=(1,),
            in_specs=[WHOLE, cut(query), cut(fresh_key), cut(fresh_value), WHOLE],
            out_specs=pl.BlockSpec((rows, w_out.shape[1]), lambda i, place: (0, 0)),
        ),
        compiler_params=params(1, 8),
        cost_estimate=pl.CostEstimate(
            flops=4 * rows * w_out.shape[0] * w_out.shape[1],
            transcendentals=0,
            bytes_accessed=2 * w_out.size,
        ),
        name="attend",
    )(place, block, query, fresh_key, fresh_value, w_out)


def total_of(first, rest):
    value = first.astype(F32)
    for other in rest:
        value = value + other.astype(F32)
    return value


def on_device(
    tokens,
    routes,
    router,
    w_gate,
    w_up,
    w_down,
    norm_gain,
    w_kv,
    lengths,
    queries,
    new_keys,
    new_values,
    w_out,
):
    own = tokens[0]
    chosen = routes[0]
    local, model = own.shape
    top = chosen.shape[1]
    eps = lax.axis_size("ep")
    parts = lax.axis_size("half")
    half, ep, pool = lax.axis_index("half"), lax.axis_index("ep"), lax.axis_index("pool")
    width = model // parts

    prompt_lengths = lax.dynamic_index_in_dim(lengths, 1 - pool, 0, keepdims=False)[0]
    place = jnp.concatenate([jnp.stack([half, ep, pool]), prompt_lengths])

    narrow = w_kv.shape[1] // 2
    tags = jnp.pad(chosen.astype(BF16), ((0, 0), (0, LANES - top)))
    quarter = lax.dynamic_slice_in_dim(own, half * width, width, axis=1)
    parcel = jnp.concatenate([quarter, tags], axis=1)
    order = sorted(range(1, parts), key=lambda k: bin(k).count("1"))
    arrived = [shift(parcel, "ep", d) for d in range(1, eps)]
    sources = (w_gate, w_up, w_down)
    experts = w_gate.shape[0]
    beside, last = order[:-1], order[-1]
    got, _ = stage(place, sources, [(PAIR, 0, 0, experts)])
    near, all_tags = unpack(tags, arrived, width)
    far = order[::-1]
    others = {k: swap(near, "half", k) for k in order[:-1]}
    again, others = lax.optimization_barrier((near, others))
    others[order[-1]] = swap(again, "half", order[-1])
    mine = lax.dynamic_slice_in_dim(w_kv, pool * narrow, narrow, axis=1)
    others[0] = near
    received = [shift(mine, "ep", d) for d in range(1, eps)]
    got, totals = stage(
        place, sources, [(PAIR, beside[0], 0, experts)], own, router.T, {0: others[0]},
        [(0, experts, [(0, False)])], got,
    )
    early = experts // 2
    got, totals = stage(
        place, sources, [(PAIR, last, 0, early)] if early else [], own, router.T,
        {k: others[k] for k in beside},
        [(0, experts, [(k, k != beside[0])]) for k in beside], got, totals,
    )
    pieces = [(0, early, [(last, False)])] if early else []
    got, (hidden,) = stage(
        place, sources, [(DOWN, far[0])], own, router.T, {last: others[last]},
        pieces + [(early, experts, [(last, True)])], got, totals, all_tags, top,
    )
    ahead = {far[0]: got[0]}
    partial = {}
    for k in far + [0]:
        if k in ahead:
            partial[k] = reduce_ahead(hidden, ahead[k])
        else:
            partial[k] = reduce(k, place, hidden, w_down, width, width // 2)
    received, partial[0] = lax.optimization_barrier((received, partial[0]))
    mine = jnp.concatenate([mine] + received, axis=0)
    gathered = []
    for k in far:
        gathered.append(swap(partial[k], "half", k))
    summed = total_of(partial[0], gathered)
    returned = [
        shift(summed[d * local : (d + 1) * local].astype(BF16), "ep", -d)
        for d in range(1, eps)
    ]
    mine, summed = lax.optimization_barrier((mine, summed))
    theirs = swap(mine, "pool", 1)
    moe_quarter = total_of(summed[:local], returned).astype(BF16)
    moe = [moe_quarter] + [None] * (parts - 1)
    for k in order:
        moe[k] = swap(moe_quarter, "half", k)
    keyvals = project(place, own, moe, norm_gain[None], mine, theirs, eps)
    block = swap(keyvals, "pool", 1)

    rows = queries.shape[1] // parts
    decoded = {}
    for k in far + [0]:
        decoded[k] = attend(
            k,
            lengths.shape[2],
            place,
            block,
            queries[0],
            new_keys[0],
            new_values[0],
            w_out,
            rows,
        )
    sent = []
    for k in far:
        sent.append(swap(decoded[k], "half", k))
    return total_of(decoded[0], sent).astype(BF16)[None]


def solution(mesh):
    in_specs = (
        P("pool", "ep", None),
        P("pool", "ep", None),
        P(),
        P("ep", None, "half"),
        P("ep", None, "half"),
        P("ep", "half", None),
        P(),
        P("ep", "half"),
        P(None, "ep", None),
        P("pool", "ep", "half"),
        P("pool", "ep", "half"),
        P("pool", "ep", "half"),
        P("half", None),
    )
    out_specs = P("pool", ("ep", "half"), None)
    return jax.shard_map(
        on_device, mesh=mesh, in_specs=in_specs, out_specs=out_specs, check_vma=False
    )
```

```python
import functools
import math

import jax
import jax.numpy as jnp
from jax import lax
from jax.experimental import pallas as pl
from jax.experimental.pallas import tpu as pltpu
from jax.sharding import PartitionSpec as P


HEAD = 128
SAMPLES = 128
LANES = 128
F32 = jnp.float32
BF16 = jnp.bfloat16
WHOLE = pl.BlockSpec(memory_space=pltpu.VMEM)


def swap(shard, axis, bits):
    return lax.ppermute(shard, axis, [(i, i ^ bits) for i in range(lax.axis_size(axis))])


def shift(shard, axis, distance):
    count = lax.axis_size(axis)
    return lax.ppermute(shard, axis, [(i, (i + distance) % count) for i in range(count)])


def params(steps, mebibytes):
    return pltpu.CompilerParams(
        dimension_semantics=("arbitrary",) * steps, vmem_limit_bytes=mebibytes * 1024 * 1024
    )


def in_vmem(array):
    return pltpu.with_memory_space_constraint(array, pltpu.VMEM)


def in_hbm(array):
    return pltpu.with_memory_space_constraint(array, pltpu.HBM)


def columns_of(piece, width):
    return pl.ds(pl.multiple_of(piece * width, width), width)


def router_logits(rows, router, columns):
    return lax.dot_general(
        rows, router[:, columns], (((1,), (1,)), ((), ())), preferred_element_type=F32
    )


def take_rows(quarters, place, own, nears, router, rows):
    local = own.shape[0]
    width = nears[0].shape[1]
    logits = 0.0
    for i, (k, near) in enumerate(zip(quarters, nears)):
        columns = columns_of(place[0] ^ k, width)
        rows[:local, i * width : (i + 1) * width] = own[:, columns]
        rows[local:, i * width : (i + 1) * width] = near[...]
        logits += router_logits(rows[:, i * width : (i + 1) * width], router, columns)
    return logits


PAIR, DOWN = 0, 2


def pair_copies(place, sources, k, low, high, out, sems):
    rows, count = columns_of(place[0] ^ k, out.shape[1]), high - low
    return [
        pltpu.make_async_copy(
            sources[j].at[pl.ds(low, count), rows, :], out.at[pl.ds(j * count, count)], sems.at[j]
        )
        for j in range(2)
    ]


def expert_copies(place, sources, k, low, e, out, sems):
    rows, count = columns_of(place[0] ^ k, out.shape[1]), out.shape[0] // 2
    return [
        pltpu.make_async_copy(
            sources[j].at[e, rows, :], out.at[j * count + e - low], sems.at[j, e - low]
        )
        for j in range(2)
    ]


def unpack_kernel(tags, *refs):
    *arrived, near, all_tags = refs
    local, width = tags.shape[0], near.shape[1]
    all_tags[:local, :] = tags[...]
    for d, parcel in enumerate(arrived):
        near[d * local : (d + 1) * local, :] = parcel[:, :width]
        all_tags[(d + 1) * local : (d + 2) * local, :] = parcel[:, width:]


def unpack(tags, arrived, width):
    local, extra = tags.shape
    count = len(arrived)
    return pl.pallas_call(
        unpack_kernel,
        out_shape=[
            jax.ShapeDtypeStruct((count * local, width), BF16),
            jax.ShapeDtypeStruct(((count + 1) * local, extra), BF16),
        ],
        in_specs=[WHOLE] * (1 + count),
        out_specs=[WHOLE] * 2,
        compiler_params=params(0, 4 if count < 8 else 32),
        name="unpack",
    )(tags, *arrived)


def streams_of(parts):
    return [(k, low, high) for low, high, ks in parts for k, streamed in ks if streamed]


def stage_kernel(items, quarters, parts, first, top, place, *refs):
    refs = list(refs)

    def take(count):
        taken = refs[:count]
        del refs[:count]
        return taken

    sources, count = take(3), len(quarters)
    streams = streams_of(parts)
    if count:
        (own, router), nears = take(2), take(count)
        held = take(sum(len(part[2]) for part in parts) - len(streams))
        totals = [None, None] if first else take(2)
        tags = take(1)[0] if top else None
    ahead = take(len(items))
    out = take(1)[0] if count else None
    logits_out = take(1)[0] if count and not top else None
    ahead_sems = take(1)[0]
    rows = take(1)[0] if count else None
    weights = take(1)[0] if top else None
    buffers, buffer_sems = take(len(streams)), take(len(streams))

    for (k, low, high), buffer, sems in zip(streams, buffers, buffer_sems):
        for e in range(low, high):
            for copy in expert_copies(place, sources, k, low, e, buffer, sems):
                copy.start()
    copies = []
    for n, item in enumerate(items):
        if item[0] == PAIR:
            copies += pair_copies(place, sources, *item[1:], ahead[n], ahead_sems.at[n])
        else:
            columns = columns_of(place[0] ^ item[1], ahead[n].shape[2])
            copies.append(
                pltpu.make_async_copy(
                    sources[DOWN].at[:, :, columns], ahead[n], ahead_sems.at[n, 0]
                )
            )
    if not streams:
        for copy in copies:
            copy.start()
    if count:
        logits = take_rows(quarters, place, own, nears, router, rows)
        if not first:
            logits += totals[1][...]
        if top:
            expert = lax.broadcasted_iota(jnp.int32, logits.shape, 1)
            named = tags[...].astype(F32).astype(jnp.int32)
            picked = named[:, 0:1] == expert
            for j in range(1, top):
                picked = jnp.logical_or(picked, named[:, j : j + 1] == expert)
            most = jnp.max(jnp.where(picked, logits, -1e30), axis=1, keepdims=True)
            spread = jnp.where(picked, jnp.exp(logits - most), 0.0)
            weights[...] = spread / jnp.sum(spread, axis=1, keepdims=True)
        else:
            logits_out[...] = logits
        experts, (_, _, units) = sources[0].shape[0], sources[0].shape
        near_width = nears[0].shape[1]
        held, buffers, buffer_sems = list(held), list(buffers), list(buffer_sems)
        for n, (low, high, ks) in enumerate(parts):
            sources_of = [
                (k, buffers.pop(0), buffer_sems.pop(0)) if streamed else (k, held.pop(0), None)
                for k, streamed in ks
            ]

            begun = any(part[0] <= low < part[1] for part in parts[:n])

            def body(e, carry, n=n, low=low, high=high, sources_of=sources_of, begun=begun):
                both = []
                at = quarters.index(sources_of[0][0]) * near_width
                for k, weight, sems in sources_of:
                    if sems is not None:
                        for copy in expert_copies(place, sources, k, low, e, weight, sems):
                            copy.wait()
                    half = weight.shape[0] // 2
                    both.append(
                        jnp.concatenate([weight[e - low], weight[half + e - low]], axis=1)
                    )
                if streams and n == 0:

                    @pl.when(e == (low if top else (low + high) // 2))
                    def _():
                        for copy in copies:
                            copy.start()

                both = jnp.concatenate(both, axis=0)
                used = rows[:, at : at + both.shape[0]]
                value = jnp.dot(used, both, preferred_element_type=F32)
                if begun:
                    value += out[e]
                elif not first:
                    value += totals[0][e]
                if not top:
                    out[e] = value
                    return carry
                gate, up = value[:, :units], value[:, units:]
                mine = expert == place[1] * experts + e
                scale = jnp.sum(jnp.where(mine, weights[...], 0.0), axis=1, keepdims=True)
                out[:, columns_of(e, units)] = (
                    gate / (1.0 + jnp.exp(-gate)) * up * scale
                ).astype(BF16)
                return carry

            lax.fori_loop(low, high, body, 0, unroll=math.gcd(2, high - low))
    for copy in copies:
        copy.wait()


def stage(place, sources, items, own=None, router=None, nears=None, parts=(), held=(),
          totals=(), tags=None, top=0):
    experts, model, units = sources[0].shape
    nears = nears or {}
    quarters = list(nears)
    width = model // lax.axis_size("half")
    count = len(quarters)
    operands = [in_hbm(array) for array in sources]
    shapes = [
        pltpu.VMEM((2 * (item[3] - item[2]), width, units), BF16)
        if item[0] == PAIR
        else pltpu.VMEM((experts, units, width), BF16)
        for item in items
    ]
    scratch, aliases, tokens = [pltpu.SemaphoreType.DMA((max(1, len(items)), 2))], {}, 0
    streams = streams_of(parts)
    mebibytes = 1
    if count:
        tokens = own.shape[0] + nears[quarters[0]].shape[0]
        mebibytes = 8 + -(-sum(4 * width * units * (p[2] - p[1]) for p in streams) >> 20)
        operands += [own, router] + [in_vmem(nears[k]) for k in quarters]
        operands += [in_vmem(array) for array in held]
        aliases = {1 + len(operands) + i: len(items) + i for i in range(len(totals))}
        operands += [in_vmem(total) for total in totals]
        scratch.append(pltpu.VMEM((tokens, count * width), BF16))
        if top:
            operands.append(tags)
            aliases = {}
            scratch.append(pltpu.VMEM((tokens, router.shape[0]), F32))
            shapes.append(pltpu.VMEM((tokens, experts * units), BF16))
        else:
            shapes.append(pltpu.VMEM((experts, tokens, 2 * units), F32))
            shapes.append(pltpu.VMEM((tokens, router.shape[0]), F32))
    scratch += [pltpu.VMEM((2 * (p[2] - p[1]), width, units), BF16) for p in streams]
    scratch += [pltpu.SemaphoreType.DMA((2, p[2] - p[1])) for p in streams]
    outs = pl.pallas_call(
        functools.partial(stage_kernel, items, quarters, parts, not totals, top),
        out_shape=shapes,
        grid_spec=pltpu.PrefetchScalarGridSpec(
            num_scalar_prefetch=1,
            grid=(),
            in_specs=[pl.BlockSpec(memory_space=pl.ANY)] * 3 + [WHOLE] * (len(operands) - 3),
            out_specs=[WHOLE] * len(shapes),
            scratch_shapes=scratch,
        ),
        input_output_aliases=aliases,
        compiler_params=params(0, mebibytes if tokens <= 1024 else 32),
    )(place, *operands)
    return list(outs[: len(items)]), outs[len(items) :]


def reduce_kernel(place, hidden, w_down, out):
    weight = w_down[...].reshape(-1, w_down.shape[2])
    out[...] = jnp.dot(hidden[...], weight, preferred_element_type=F32).astype(BF16)


def reduce_ahead_kernel(hidden, weight, out):
    block = weight.shape[2] // 2
    for i in range(2):
        columns = slice(i * block, (i + 1) * block)
        piece = weight[:, :, columns].reshape(-1, block)
        out[:, columns] = jnp.dot(hidden[...], piece, preferred_element_type=F32).astype(BF16)


def reduce_ahead(hidden, weight):
    return pl.pallas_call(
        reduce_ahead_kernel,
        out_shape=jax.ShapeDtypeStruct((hidden.shape[0], weight.shape[2]), BF16),
        in_specs=[WHOLE] * 2,
        out_specs=WHOLE,
        compiler_params=params(0, 12),
        name="reduce",
    )(in_vmem(hidden), in_vmem(weight))


def reduce(k, place, hidden, w_down, width, block):
    experts, units, _ = w_down.shape
    steps = width // block
    tokens = hidden.shape[0]
    return pl.pallas_call(
        reduce_kernel,
        out_shape=jax.ShapeDtypeStruct((tokens, width), BF16),
        grid_spec=pltpu.PrefetchScalarGridSpec(
            num_scalar_prefetch=1,
            grid=(steps,),
            in_specs=[
                WHOLE,
                pl.BlockSpec(
                    (experts, units, block),
                    lambda i, place: (0, 0, (place[0] ^ k) * steps + i),
                ),
            ],
            out_specs=pl.BlockSpec((tokens, block), lambda i, place: (0, i)),
        ),
        compiler_params=params(1, 16),
        cost_estimate=pl.CostEstimate(
            flops=2 * tokens * width * experts * units,
            transcendentals=0,
            bytes_accessed=2 * experts * width * units,
        ),
        name="reduce",
    )(place, in_vmem(hidden), in_hbm(w_down))


def project_kernel(parts, eps, place, own, *refs):
    moe, refs = refs[:parts], refs[parts:]
    gain, mine, theirs, out, mixed, normed = refs
    half, ep, pool = place[0], place[1], place[2]
    width = moe[0].shape[1]
    square = jnp.zeros((own.shape[0], 1), F32)
    for k in range(parts):
        columns = columns_of(half ^ k, width)
        value = own[:, columns].astype(F32) + moe[k][...].astype(F32)
        mixed[:, columns] = value
        square += jnp.sum(value * value, axis=1, keepdims=True)
    factor = lax.rsqrt(square / mixed.shape[1] + 1e-06)
    normed[...] = (mixed[...] * factor * gain[...]).astype(BF16)
    depth, narrow = mine.shape[0] // eps, mine.shape[1]
    for side, pieces in ((pool, mine), (1 - pool, theirs)):
        total = 0.0
        for d in range(eps):
            total += jnp.dot(
                normed[:, columns_of(lax.rem(ep + eps - d, eps), depth)],
                pieces[d * depth : (d + 1) * depth, :],
                preferred_element_type=F32,
            )
        out[:, columns_of(side, narrow)] = total.astype(BF16)


def project(place, own, moe, gain, mine, theirs, eps):
    return pl.pallas_call(
        functools.partial(project_kernel, len(moe), eps),
        out_shape=jax.ShapeDtypeStruct((own.shape[0], 2 * mine.shape[1]), BF16),
        grid_spec=pltpu.PrefetchScalarGridSpec(
            num_scalar_prefetch=1,
            grid=(),
            in_specs=[WHOLE] * (len(moe) + 4),
            out_specs=WHOLE,
            scratch_shapes=[pltpu.VMEM(own.shape, F32), pltpu.VMEM(own.shape, BF16)],
        ),
        compiler_params=params(0, 12),
        name="project",
    )(place, own, *moe, gain, mine, theirs)


def attend_kernel(k, prompts, place, block, query, fresh_key, fresh_value, w_out, out):
    rows = query.shape[0]
    group_tok = block.shape[0]
    kv_heads = fresh_key.shape[1] // HEAD
    per_head = query.shape[1] // HEAD // kv_heads
    heads = kv_heads * per_head
    position = lax.broadcasted_iota(jnp.int32, (rows, group_tok), 1)
    row = (place[0] ^ k) * rows + lax.broadcasted_iota(jnp.int32, (rows, group_tok), 0)
    segment = jnp.zeros((rows, group_tok), jnp.int32)
    end = jnp.int32(0)
    for p in range(prompts):
        end = end + place[3 + p]
        segment += (position >= end).astype(jnp.int32)
    allowed = jnp.where(segment == row // SAMPLES, 1.0, 0.0)
    allowed = jnp.concatenate([allowed] * heads, axis=0) > 0.5
    scale = 1.0 / math.sqrt(HEAD)
    scores, owns = [], []
    for kv in range(kv_heads):
        key = block[:, 2 * kv * HEAD : (2 * kv + 1) * HEAD]
        new_key = fresh_key[:, kv * HEAD : (kv + 1) * HEAD].astype(F32)
        first = kv * per_head * HEAD
        asked = [query[:, first + j * HEAD : first + (j + 1) * HEAD] for j in range(per_head)]
        scores.append(
            lax.dot_general(
                jnp.concatenate(asked, axis=0),
                key,
                (((1,), (1,)), ((), ())),
                preferred_element_type=F32,
            )
        )
        owns += [jnp.sum(q.astype(F32) * new_key, axis=1, keepdims=True) for q in asked]
    scores = jnp.where(allowed, jnp.concatenate(scores, axis=0) * scale, -1e30)
    own = jnp.concatenate(owns, axis=0) * scale
    top = jnp.maximum(jnp.max(scores, axis=1, keepdims=True), own)
    spread = jnp.where(allowed, jnp.exp(scores - top), 0.0)
    self_weight = jnp.exp(own - top)
    total = jnp.sum(spread, axis=1, keepdims=True) + self_weight
    probs = (spread / total).astype(BF16)
    self_prob = (self_weight / total).astype(BF16).astype(F32)
    mixed = []
    for kv in range(kv_heads):
        value = block[:, (2 * kv + 1) * HEAD : (2 * kv + 2) * HEAD]
        new_value = fresh_value[:, kv * HEAD : (kv + 1) * HEAD].astype(F32)
        lower = kv * per_head * rows
        summed = jnp.dot(
            probs[lower : lower + per_head * rows], value, preferred_element_type=F32
        )
        for j in range(per_head):
            at = slice(j * rows, (j + 1) * rows)
            own_part = self_prob[lower + j * rows : lower + (j + 1) * rows] * new_value
            mixed.append((summed[at] + own_part).astype(BF16))
    attention = jnp.concatenate(mixed, axis=1)
    out[...] = jnp.dot(attention, w_out[...], preferred_element_type=F32).astype(BF16)


def attend(k, prompts, place, block, query, fresh_key, fresh_value, w_out, rows):
    def cut(array):
        return pl.BlockSpec((rows, array.shape[1]), lambda i, place: (place[0] ^ k, 0))

    return pl.pallas_call(
        functools.partial(attend_kernel, k, prompts),
        out_shape=jax.ShapeDtypeStruct((rows, w_out.shape[1]), BF16),
        grid_spec=pltpu.PrefetchScalarGridSpec(
            num_scalar_prefetch=1,
            grid=(1,),
            in_specs=[WHOLE, cut(query), cut(fresh_key), cut(fresh_value), WHOLE],
            out_specs=pl.BlockSpec((rows, w_out.shape[1]), lambda i, place: (0, 0)),
        ),
        compiler_params=params(1, 8),
        cost_estimate=pl.CostEstimate(
            flops=4 * rows * w_out.shape[0] * w_out.shape[1],
            transcendentals=0,
            bytes_accessed=2 * w_out.size,
        ),
        name="attend",
    )(place, block, query, fresh_key, fresh_value, w_out)


def total_of(first, rest):
    value = first.astype(F32)
    for other in rest:
        value = value + other.astype(F32)
    return value


def on_device(
    tokens,
    routes,
    router,
    w_gate,
    w_up,
    w_down,
    norm_gain,
    w_kv,
    lengths,
    queries,
    new_keys,
    new_values,
    w_out,
):
    own = tokens[0]
    chosen = routes[0]
    local, model = own.shape
    top = chosen.shape[1]
    eps = lax.axis_size("ep")
    parts = lax.axis_size("half")
    half, ep, pool = lax.axis_index("half"), lax.axis_index("ep"), lax.axis_index("pool")
    width = model // parts

    prompt_lengths = lax.dynamic_index_in_dim(lengths, 1 - pool, 0, keepdims=False)[0]
    place = jnp.concatenate([jnp.stack([half, ep, pool]), prompt_lengths])

    narrow = w_kv.shape[1] // 2
    tags = jnp.pad(chosen.astype(BF16), ((0, 0), (0, LANES - top)))
    quarter = lax.dynamic_slice_in_dim(own, half * width, width, axis=1)
    parcel = jnp.concatenate([quarter, tags], axis=1)
    order = sorted(range(1, parts), key=lambda k: bin(k).count("1"))
    arrived = [shift(parcel, "ep", d) for d in range(1, eps)]
    sources = (w_gate, w_up, w_down)
    experts = w_gate.shape[0]
    beside, last = order[:-1], order[-1]
    got, _ = stage(place, sources, [(PAIR, 0, 0, experts)])
    near, all_tags = unpack(tags, arrived, width)
    far = order[::-1]
    others = {k: swap(near, "half", k) for k in order[:-1]}
    again, others = lax.optimization_barrier((near, others))
    others[order[-1]] = swap(again, "half", order[-1])
    mine = lax.dynamic_slice_in_dim(w_kv, pool * narrow, narrow, axis=1)
    others[0] = near
    received = [shift(mine, "ep", d) for d in range(1, eps)]
    got, totals = stage(
        place, sources, [(PAIR, beside[0], 0, experts)], own, router.T, {0: others[0]},
        [(0, experts, [(0, False)])], got,
    )
    early = experts // 2
    got, totals = stage(
        place, sources, [(PAIR, last, 0, early)] * (early > 0) + [(DOWN, far[0])], own, router.T,
        {k: others[k] for k in beside},
        [(0, experts, [(k, k != beside[0])]) for k in beside], got, totals,
    )
    pieces = [(0, early, [(last, False)])] if early else []
    ahead = {far[0]: got.pop()}
    got, (hidden,) = stage(
        place, sources, [(DOWN, far[1])], own, router.T, {last: others[last]},
        pieces + [(early, experts, [(last, True)])], got, totals, all_tags, top,
    )
    ahead[far[1]] = got[0]
    partial = {}
    for k in far + [0]:
        if k in ahead:
            partial[k] = reduce_ahead(hidden, ahead[k])
        else:
            partial[k] = reduce(k, place, hidden, w_down, width, width // 2)
    received, partial[0] = lax.optimization_barrier((received, partial[0]))
    mine = jnp.concatenate([mine] + received, axis=0)
    gathered = []
    for k in far:
        gathered.append(swap(partial[k], "half", k))
    summed = total_of(partial[0], gathered)
    returned = [
        shift(summed[d * local : (d + 1) * local].astype(BF16), "ep", -d)
        for d in range(1, eps)
    ]
    mine, summed = lax.optimization_barrier((mine, summed))
    theirs = swap(mine, "pool", 1)
    moe_quarter = total_of(summed[:local], returned).astype(BF16)
    moe = [moe_quarter] + [None] * (parts - 1)
    for k in far:
        moe[k] = swap(moe_quarter, "half", k)
    keyvals = project(place, own, moe, norm_gain[None], mine, theirs, eps)
    block = swap(keyvals, "pool", 1)

    rows = queries.shape[1] // parts
    decoded = {}
    for k in far + [0]:
        decoded[k] = attend(
            k,
            lengths.shape[2],
            place,
            block,
            queries[0],
            new_keys[0],
            new_values[0],
            w_out,
            rows,
        )
    sent = []
    for k in far:
        sent.append(swap(decoded[k], "half", k))
    return total_of(decoded[0], sent).astype(BF16)[None]


def solution(mesh):
    in_specs = (
        P("pool", "ep", None),
        P("pool", "ep", None),
        P(),
        P("ep", None, "half"),
        P("ep", None, "half"),
        P("ep", "half", None),
        P(),
        P("ep", "half"),
        P(None, "ep", None),
        P("pool", "ep", "half"),
        P("pool", "ep", "half"),
        P("pool", "ep", "half"),
        P("half", None),
    )
    out_specs = P("pool", ("ep", "half"), None)
    return jax.shard_map(
        on_device, mesh=mesh, in_specs=in_specs, out_specs=out_specs, check_vma=False
    )
```

```python
import functools
import math

import jax
import jax.numpy as jnp
from jax import lax
from jax.experimental import pallas as pl
from jax.experimental.pallas import tpu as pltpu
from jax.sharding import PartitionSpec as P


HEAD = 128
SAMPLES = 128
LANES = 128
F32 = jnp.float32
BF16 = jnp.bfloat16
WHOLE = pl.BlockSpec(memory_space=pltpu.VMEM)


def swap(shard, axis, bits):
    return lax.ppermute(shard, axis, [(i, i ^ bits) for i in range(lax.axis_size(axis))])


def shift(shard, axis, distance):
    count = lax.axis_size(axis)
    return lax.ppermute(shard, axis, [(i, (i + distance) % count) for i in range(count)])


def params(steps, mebibytes):
    return pltpu.CompilerParams(
        dimension_semantics=("arbitrary",) * steps, vmem_limit_bytes=mebibytes * 1024 * 1024
    )


def in_vmem(array):
    return pltpu.with_memory_space_constraint(array, pltpu.VMEM)


def in_hbm(array):
    return pltpu.with_memory_space_constraint(array, pltpu.HBM)


def columns_of(piece, width):
    return pl.ds(pl.multiple_of(piece * width, width), width)


def router_logits(rows, router, columns):
    return lax.dot_general(
        rows, router[:, columns], (((1,), (1,)), ((), ())), preferred_element_type=F32
    )


def take_rows(quarters, place, own, nears, router, rows):
    local = own.shape[0]
    width = nears[0].shape[1]
    logits = 0.0
    for i, (k, near) in enumerate(zip(quarters, nears)):
        columns = columns_of(place[0] ^ k, width)
        rows[:local, i * width : (i + 1) * width] = own[:, columns]
        rows[local:, i * width : (i + 1) * width] = near[...]
        logits += router_logits(rows[:, i * width : (i + 1) * width], router, columns)
    return logits


PAIR, DOWN = 0, 2


def pair_copies(place, sources, k, low, high, out, sems):
    rows, count = columns_of(place[0] ^ k, out.shape[1]), high - low
    return [
        pltpu.make_async_copy(
            sources[j].at[pl.ds(low, count), rows, :], out.at[pl.ds(j * count, count)], sems.at[j]
        )
        for j in range(2)
    ]


def expert_copies(place, sources, k, low, e, out, sems):
    rows, count = columns_of(place[0] ^ k, out.shape[1]), out.shape[0] // 2
    return [
        pltpu.make_async_copy(
            sources[j].at[e, rows, :], out.at[j * count + e - low], sems.at[j, e - low]
        )
        for j in range(2)
    ]


def unpack_kernel(tags, *refs):
    *arrived, near, all_tags = refs
    local, width = tags.shape[0], near.shape[1]
    all_tags[:local, :] = tags[...]
    for d, parcel in enumerate(arrived):
        near[d * local : (d + 1) * local, :] = parcel[:, :width]
        all_tags[(d + 1) * local : (d + 2) * local, :] = parcel[:, width:]


def unpack(tags, arrived, width):
    local, extra = tags.shape
    count = len(arrived)
    return pl.pallas_call(
        unpack_kernel,
        out_shape=[
            jax.ShapeDtypeStruct((count * local, width), BF16),
            jax.ShapeDtypeStruct(((count + 1) * local, extra), BF16),
        ],
        in_specs=[WHOLE] * (1 + count),
        out_specs=[WHOLE] * 2,
        compiler_params=params(0, 4 if count < 8 else 32),
        name="unpack",
    )(tags, *arrived)


def streams_of(parts):
    return [(k, low, high) for low, high, ks in parts for k, streamed in ks if streamed]


def stage_kernel(items, quarters, parts, first, top, place, *refs):
    refs = list(refs)

    def take(count):
        taken = refs[:count]
        del refs[:count]
        return taken

    sources, count = take(3), len(quarters)
    streams = streams_of(parts)
    if count:
        (own, router), nears = take(2), take(count)
        held = take(sum(len(part[2]) for part in parts) - len(streams))
        totals = [None, None] if first else take(2)
        tags = take(1)[0] if top else None
    ahead = take(len(items))
    out = take(1)[0] if count else None
    logits_out = take(1)[0] if count and not top else None
    ahead_sems = take(1)[0]
    rows = take(1)[0] if count else None
    weights = take(1)[0] if top else None
    buffers, buffer_sems = take(len(streams)), take(len(streams))

    for (k, low, high), buffer, sems in zip(streams, buffers, buffer_sems):
        for e in range(low, high):
            for copy in expert_copies(place, sources, k, low, e, buffer, sems):
                copy.start()
    copies = []
    for n, item in enumerate(items):
        if item[0] == PAIR:
            copies += pair_copies(place, sources, *item[1:], ahead[n], ahead_sems.at[n])
        else:
            columns = columns_of(place[0] ^ item[1], ahead[n].shape[2])
            copies.append(
                pltpu.make_async_copy(
                    sources[DOWN].at[:, :, columns], ahead[n], ahead_sems.at[n, 0]
                )
            )
    if not streams:
        for copy in copies:
            copy.start()
    if count:
        logits = take_rows(quarters, place, own, nears, router, rows)
        if not first:
            logits += totals[1][...]
        if top:
            expert = lax.broadcasted_iota(jnp.int32, logits.shape, 1)
            named = tags[...].astype(F32).astype(jnp.int32)
            picked = named[:, 0:1] == expert
            for j in range(1, top):
                picked = jnp.logical_or(picked, named[:, j : j + 1] == expert)
            most = jnp.max(jnp.where(picked, logits, -1e30), axis=1, keepdims=True)
            spread = jnp.where(picked, jnp.exp(logits - most), 0.0)
            weights[...] = spread / jnp.sum(spread, axis=1, keepdims=True)
        else:
            logits_out[...] = logits
        experts, (_, _, units) = sources[0].shape[0], sources[0].shape
        near_width = nears[0].shape[1]
        held, buffers, buffer_sems = list(held), list(buffers), list(buffer_sems)
        for n, (low, high, ks) in enumerate(parts):
            sources_of = [
                (k, buffers.pop(0), buffer_sems.pop(0)) if streamed else (k, held.pop(0), None)
                for k, streamed in ks
            ]

            begun = any(part[0] <= low < part[1] for part in parts[:n])

            def body(e, carry, n=n, low=low, high=high, sources_of=sources_of, begun=begun):
                both = []
                at = quarters.index(sources_of[0][0]) * near_width
                for k, weight, sems in sources_of:
                    if sems is not None:
                        for copy in expert_copies(place, sources, k, low, e, weight, sems):
                            copy.wait()
                    half = weight.shape[0] // 2
                    both.append(
                        jnp.concatenate([weight[e - low], weight[half + e - low]], axis=1)
                    )
                if streams and n == 0:

                    @pl.when(e == (low + high) // 2)
                    def _():
                        for copy in copies:
                            copy.start()

                both = jnp.concatenate(both, axis=0)
                used = rows[:, at : at + both.shape[0]]
                value = jnp.dot(used, both, preferred_element_type=F32)
                if begun:
                    value += out[e]
                elif not first:
                    value += totals[0][e]
                if not top:
                    out[e] = value
                    return carry
                gate, up = value[:, :units], value[:, units:]
                mine = expert == place[1] * experts + e
                scale = jnp.sum(jnp.where(mine, weights[...], 0.0), axis=1, keepdims=True)
                out[:, columns_of(e, units)] = (
                    gate / (1.0 + jnp.exp(-gate)) * up * scale
                ).astype(BF16)
                return carry

            lax.fori_loop(low, high, body, 0, unroll=math.gcd(2, high - low))
    for copy in copies:
        copy.wait()


def stage(place, sources, items, own=None, router=None, nears=None, parts=(), held=(),
          totals=(), tags=None, top=0):
    experts, model, units = sources[0].shape
    nears = nears or {}
    quarters = list(nears)
    width = model // lax.axis_size("half")
    count = len(quarters)
    operands = [in_hbm(array) for array in sources]
    shapes = [
        pltpu.VMEM((2 * (item[3] - item[2]), width, units), BF16)
        if item[0] == PAIR
        else pltpu.VMEM((experts, units, width), BF16)
        for item in items
    ]
    scratch, aliases, tokens = [pltpu.SemaphoreType.DMA((max(1, len(items)), 2))], {}, 0
    streams = streams_of(parts)
    mebibytes = 1
    if count:
        tokens = own.shape[0] + nears[quarters[0]].shape[0]
        mebibytes = 8 + -(-sum(4 * width * units * (p[2] - p[1]) for p in streams) >> 20)
        operands += [own, router] + [in_vmem(nears[k]) for k in quarters]
        operands += [in_vmem(array) for array in held]
        aliases = {1 + len(operands) + i: len(items) + i for i in range(len(totals))}
        operands += [in_vmem(total) for total in totals]
        scratch.append(pltpu.VMEM((tokens, count * width), BF16))
        if top:
            operands.append(tags)
            aliases = {}
            scratch.append(pltpu.VMEM((tokens, router.shape[0]), F32))
            shapes.append(pltpu.VMEM((tokens, experts * units), BF16))
        else:
            shapes.append(pltpu.VMEM((experts, tokens, 2 * units), F32))
            shapes.append(pltpu.VMEM((tokens, router.shape[0]), F32))
    scratch += [pltpu.VMEM((2 * (p[2] - p[1]), width, units), BF16) for p in streams]
    scratch += [pltpu.SemaphoreType.DMA((2, p[2] - p[1])) for p in streams]
    outs = pl.pallas_call(
        functools.partial(stage_kernel, items, quarters, parts, not totals, top),
        out_shape=shapes,
        grid_spec=pltpu.PrefetchScalarGridSpec(
            num_scalar_prefetch=1,
            grid=(),
            in_specs=[pl.BlockSpec(memory_space=pl.ANY)] * 3 + [WHOLE] * (len(operands) - 3),
            out_specs=[WHOLE] * len(shapes),
            scratch_shapes=scratch,
        ),
        input_output_aliases=aliases,
        compiler_params=params(0, mebibytes if tokens <= 1024 else 32),
    )(place, *operands)
    return list(outs[: len(items)]), outs[len(items) :]


def reduce_kernel(place, hidden, w_down, out):
    weight = w_down[...].reshape(-1, w_down.shape[2])
    out[...] = jnp.dot(hidden[...], weight, preferred_element_type=F32).astype(BF16)


def reduce_ahead_kernel(hidden, weight, out):
    block = weight.shape[2] // 2
    for i in range(2):
        columns = slice(i * block, (i + 1) * block)
        piece = weight[:, :, columns].reshape(-1, block)
        out[:, columns] = jnp.dot(hidden[...], piece, preferred_element_type=F32).astype(BF16)


def reduce_ahead(hidden, weight):
    return pl.pallas_call(
        reduce_ahead_kernel,
        out_shape=jax.ShapeDtypeStruct((hidden.shape[0], weight.shape[2]), BF16),
        in_specs=[WHOLE] * 2,
        out_specs=WHOLE,
        compiler_params=params(0, 12),
        name="reduce",
    )(in_vmem(hidden), in_vmem(weight))


def reduce(k, place, hidden, w_down, width, block):
    experts, units, _ = w_down.shape
    steps = width // block
    tokens = hidden.shape[0]
    return pl.pallas_call(
        reduce_kernel,
        out_shape=jax.ShapeDtypeStruct((tokens, width), BF16),
        grid_spec=pltpu.PrefetchScalarGridSpec(
            num_scalar_prefetch=1,
            grid=(steps,),
            in_specs=[
                WHOLE,
                pl.BlockSpec(
                    (experts, units, block),
                    lambda i, place: (0, 0, (place[0] ^ k) * steps + i),
                ),
            ],
            out_specs=pl.BlockSpec((tokens, block), lambda i, place: (0, i)),
        ),
        compiler_params=params(1, 16),
        cost_estimate=pl.CostEstimate(
            flops=2 * tokens * width * experts * units,
            transcendentals=0,
            bytes_accessed=2 * experts * width * units,
        ),
        name="reduce",
    )(place, in_vmem(hidden), in_hbm(w_down))


def project_kernel(parts, eps, place, own, *refs):
    moe, refs = refs[:parts], refs[parts:]
    gain, mine, theirs, out, mixed, normed = refs
    half, ep, pool = place[0], place[1], place[2]
    width = moe[0].shape[1]
    square = jnp.zeros((own.shape[0], 1), F32)
    for k in range(parts):
        columns = columns_of(half ^ k, width)
        value = own[:, columns].astype(F32) + moe[k][...].astype(F32)
        mixed[:, columns] = value
        square += jnp.sum(value * value, axis=1, keepdims=True)
    factor = lax.rsqrt(square / mixed.shape[1] + 1e-06)
    normed[...] = (mixed[...] * factor * gain[...]).astype(BF16)
    depth, narrow = mine.shape[0] // eps, mine.shape[1]
    for side, pieces in ((pool, mine), (1 - pool, theirs)):
        total = 0.0
        for d in range(eps):
            total += jnp.dot(
                normed[:, columns_of(lax.rem(ep + eps - d, eps), depth)],
                pieces[d * depth : (d + 1) * depth, :],
                preferred_element_type=F32,
            )
        out[:, columns_of(side, narrow)] = total.astype(BF16)


def project(place, own, moe, gain, mine, theirs, eps):
    return pl.pallas_call(
        functools.partial(project_kernel, len(moe), eps),
        out_shape=jax.ShapeDtypeStruct((own.shape[0], 2 * mine.shape[1]), BF16),
        grid_spec=pltpu.PrefetchScalarGridSpec(
            num_scalar_prefetch=1,
            grid=(),
            in_specs=[WHOLE] * (len(moe) + 4),
            out_specs=WHOLE,
            scratch_shapes=[pltpu.VMEM(own.shape, F32), pltpu.VMEM(own.shape, BF16)],
        ),
        compiler_params=params(0, 12),
        name="project",
    )(place, own, *moe, gain, mine, theirs)


def attend_kernel(k, prompts, place, block, query, fresh_key, fresh_value, w_out, out):
    rows = query.shape[0]
    group_tok = block.shape[0]
    kv_heads = fresh_key.shape[1] // HEAD
    per_head = query.shape[1] // HEAD // kv_heads
    heads = kv_heads * per_head
    position = lax.broadcasted_iota(jnp.int32, (rows, group_tok), 1)
    row = (place[0] ^ k) * rows + lax.broadcasted_iota(jnp.int32, (rows, group_tok), 0)
    segment = jnp.zeros((rows, group_tok), jnp.int32)
    end = jnp.int32(0)
    for p in range(prompts):
        end = end + place[3 + p]
        segment += (position >= end).astype(jnp.int32)
    allowed = jnp.where(segment == row // SAMPLES, 1.0, 0.0)
    allowed = jnp.concatenate([allowed] * heads, axis=0) > 0.5
    scale = 1.0 / math.sqrt(HEAD)
    scores, owns = [], []
    for kv in range(kv_heads):
        key = block[:, 2 * kv * HEAD : (2 * kv + 1) * HEAD]
        new_key = fresh_key[:, kv * HEAD : (kv + 1) * HEAD].astype(F32)
        first = kv * per_head * HEAD
        asked = [query[:, first + j * HEAD : first + (j + 1) * HEAD] for j in range(per_head)]
        scores.append(
            lax.dot_general(
                jnp.concatenate(asked, axis=0),
                key,
                (((1,), (1,)), ((), ())),
                preferred_element_type=F32,
            )
        )
        owns += [jnp.sum(q.astype(F32) * new_key, axis=1, keepdims=True) for q in asked]
    scores = jnp.where(allowed, jnp.concatenate(scores, axis=0) * scale, -1e30)
    own = jnp.concatenate(owns, axis=0) * scale
    top = jnp.maximum(jnp.max(scores, axis=1, keepdims=True), own)
    spread = jnp.where(allowed, jnp.exp(scores - top), 0.0)
    self_weight = jnp.exp(own - top)
    total = jnp.sum(spread, axis=1, keepdims=True) + self_weight
    probs = (spread / total).astype(BF16)
    self_prob = (self_weight / total).astype(BF16).astype(F32)
    mixed = []
    for kv in range(kv_heads):
        value = block[:, (2 * kv + 1) * HEAD : (2 * kv + 2) * HEAD]
        new_value = fresh_value[:, kv * HEAD : (kv + 1) * HEAD].astype(F32)
        lower = kv * per_head * rows
        summed = jnp.dot(
            probs[lower : lower + per_head * rows], value, preferred_element_type=F32
        )
        for j in range(per_head):
            at = slice(j * rows, (j + 1) * rows)
            own_part = self_prob[lower + j * rows : lower + (j + 1) * rows] * new_value
            mixed.append((summed[at] + own_part).astype(BF16))
    attention = jnp.concatenate(mixed, axis=1)
    out[...] = jnp.dot(attention, w_out[...], preferred_element_type=F32).astype(BF16)


def attend(k, prompts, place, block, query, fresh_key, fresh_value, w_out, rows):
    def cut(array):
        return pl.BlockSpec((rows, array.shape[1]), lambda i, place: (place[0] ^ k, 0))

    return pl.pallas_call(
        functools.partial(attend_kernel, k, prompts),
        out_shape=jax.ShapeDtypeStruct((rows, w_out.shape[1]), BF16),
        grid_spec=pltpu.PrefetchScalarGridSpec(
            num_scalar_prefetch=1,
            grid=(1,),
            in_specs=[WHOLE, cut(query), cut(fresh_key), cut(fresh_value), WHOLE],
            out_specs=pl.BlockSpec((rows, w_out.shape[1]), lambda i, place: (0, 0)),
        ),
        compiler_params=params(1, 8),
        cost_estimate=pl.CostEstimate(
            flops=4 * rows * w_out.shape[0] * w_out.shape[1],
            transcendentals=0,
            bytes_accessed=2 * w_out.size,
        ),
        name="attend",
    )(place, block, query, fresh_key, fresh_value, w_out)


def total_of(first, rest):
    value = first.astype(F32)
    for other in rest:
        value = value + other.astype(F32)
    return value


def on_device(
    tokens,
    routes,
    router,
    w_gate,
    w_up,
    w_down,
    norm_gain,
    w_kv,
    lengths,
    queries,
    new_keys,
    new_values,
    w_out,
):
    own = tokens[0]
    chosen = routes[0]
    local, model = own.shape
    top = chosen.shape[1]
    eps = lax.axis_size("ep")
    parts = lax.axis_size("half")
    half, ep, pool = lax.axis_index("half"), lax.axis_index("ep"), lax.axis_index("pool")
    width = model // parts

    prompt_lengths = lax.dynamic_index_in_dim(lengths, 1 - pool, 0, keepdims=False)[0]
    place = jnp.concatenate([jnp.stack([half, ep, pool]), prompt_lengths])

    narrow = w_kv.shape[1] // 2
    tags = jnp.pad(chosen.astype(BF16), ((0, 0), (0, LANES - top)))
    quarter = lax.dynamic_slice_in_dim(own, half * width, width, axis=1)
    parcel = jnp.concatenate([quarter, tags], axis=1)
    order = sorted(range(1, parts), key=lambda k: bin(k).count("1"))
    arrived = []
    for d in range(1, eps):
        arrived.append(shift(parcel, "ep", d))
    sources = (w_gate, w_up, w_down)
    experts = w_gate.shape[0]
    beside, last = order[:-1], order[-1]
    got, _ = stage(place, sources, [(PAIR, 0, 0, experts)])
    near, all_tags = unpack(tags, arrived, width)
    far = order[::-1]
    others = {k: swap(near, "half", k) for k in order[:-1]}
    again, others = lax.optimization_barrier((near, others))
    others[order[-1]] = swap(again, "half", order[-1])
    mine = lax.dynamic_slice_in_dim(w_kv, pool * narrow, narrow, axis=1)
    others[0] = near
    received = [shift(mine, "ep", d) for d in range(1, eps)]
    got, totals = stage(
        place, sources, [(PAIR, beside[0], 0, experts)], own, router.T, {0: others[0]},
        [(0, experts, [(0, False)])], got,
    )
    early = experts // 2
    got, totals = stage(
        place, sources, [(PAIR, last, 0, early)] * (early > 0) + [(DOWN, far[0])], own, router.T,
        {k: others[k] for k in beside},
        [(0, experts, [(k, k != beside[0])]) for k in beside], got, totals,
    )
    pieces = [(0, early, [(last, False)])] if early else []
    ahead = {far[0]: got.pop()}
    got, (hidden,) = stage(
        place, sources, [(DOWN, far[1])], own, router.T, {last: others[last]},
        pieces + [(early, experts, [(last, True)])], got, totals, all_tags, top,
    )
    ahead[far[1]] = got[0]
    partial = {}
    for k in far + [0]:
        if k in ahead:
            partial[k] = reduce_ahead(hidden, ahead[k])
        else:
            partial[k] = reduce(k, place, hidden, w_down, width, width // 2)
    received, partial[0] = lax.optimization_barrier((received, partial[0]))
    mine = jnp.concatenate([mine] + received, axis=0)
    gathered = []
    for k in far:
        gathered.append(swap(partial[k], "half", k))
    summed = total_of(partial[0], gathered)
    returned = []
    for d in range(1, eps):
        block = summed[d * local : (d + 1) * local].astype(BF16)
        returned.append(shift(block, "ep", -d))
    mine, summed = lax.optimization_barrier((mine, summed))
    theirs = swap(mine, "pool", 1)
    moe_quarter = total_of(summed[:local], returned).astype(BF16)
    moe = [moe_quarter] + [None] * (parts - 1)
    for k in order:
        moe[k] = swap(moe_quarter, "half", k)
    keyvals = project(place, own, moe, norm_gain[None], mine, theirs, eps)
    block = swap(keyvals, "pool", 1)

    rows = queries.shape[1] // parts
    decoded = {}
    for k in far + [0]:
        decoded[k] = attend(
            k,
            lengths.shape[2],
            place,
            block,
            queries[0],
            new_keys[0],
            new_values[0],
            w_out,
            rows,
        )
    sent = []
    for k in far:
        sent.append(swap(decoded[k], "half", k))
    return total_of(decoded[0], sent).astype(BF16)[None]


def solution(mesh):
    in_specs = (
        P("pool", "ep", None),
        P("pool", "ep", None),
        P(),
        P("ep", None, "half"),
        P("ep", None, "half"),
        P("ep", "half", None),
        P(),
        P("ep", "half"),
        P(None, "ep", None),
        P("pool", "ep", "half"),
        P("pool", "ep", "half"),
        P("pool", "ep", "half"),
        P("half", None),
    )
    out_specs = P("pool", ("ep", "half"), None)
    return jax.shard_map(
        on_device, mesh=mesh, in_specs=in_specs, out_specs=out_specs, check_vma=False
    )
```
